512 devices in a mesh: ctx: 64 (over x, z_lo, y), dp: 8 (over z_hi, core).
Axes of the slice: x: 4, y: 4, z: 16 (z_hi: 4, z_lo: 4; z = z_hi * 4 + z_lo), core: 2. Of those that a mesh axis runs over, the one named last changes fastest.
Arguments:
- layer_input: bfloat16 [16, 4096, 4096], P('dp', 'ctx'), may hold values from -1 to 1
- queries: bfloat16 [16, 4096, 1024], P('dp', 'ctx'), may hold values from -8 to 8
- key_states: bfloat16 [16, 4096, 128], P('dp', 'ctx'), may hold values from -8 to 8
- value_states: bfloat16 [16, 4096, 128], P('dp', 'ctx'), may hold values from -6 to 6
- attn_output: bfloat16 [16, 4096, 1024], P('dp', 'ctx'), may hold values from -6 to 6
- out_grad: bfloat16 [16, 4096, 1024], P('dp', 'ctx'), may hold values from -6 to 6
- doc_ids: int32 [16, 4096], P('dp'), may hold values from 0 to 15, never falling along the last dimension, each value on 1 to 1024 neighbouring positions
- positions: int32 [16, 4096], P('dp'), may hold values from 0 to 4095, as said below
Outputs:
- query_grad: bfloat16 [16, 4096, 1024], P('dp', 'ctx')
- kv_weight_grad: float32 [4096, 256], P('ctx')
The draws below stay inside these ranges and needn't reach their ends.
Inputs may be any that keep to these rules, and one draw needn't show every extreme that they name: `positions`: stored row c * 64 + r of a sequence (c below 64, r below 64) holds a position from r * (64) to (r + 1) * 64 - 1; every position of a sequence is held by exactly one row.
All inputs are finite; a program needn't handle non-finite values.
Results may differ from the reference program's by a relative error of at most 0.005.
Values may be sent and summed in bfloat16 or wider, within the bound.
No kernel may reach another device: no remote copies, remote signals or barrier semaphores. Data moves between devices by JAX's collectives and lax.ppermute only.
A program may use at most 64 MiB of HBM per device.

```python
import math
import jax
import jax.numpy as jnp
import numpy as np
from jax import lax

D = 4096
HEADS = 8
HD = 128
SROWS = 64
SEQ_LEN = 4096
BATCH = 16
DOCS = 16
DOC_MOST = 1024


def draw_queries(key, part):
    first_key = jax.random.fold_in(key, 0)
    whole_shape = (BATCH, SEQ_LEN, HEADS * HD)
    return jax.random.truncated_normal(first_key, -4.0, 4.0, whole_shape, jnp.float32).astype(jnp.bfloat16)


def draw_key_states(key, part):
    first_key = jax.random.fold_in(jax.random.fold_in(key, 7), 0)
    whole_shape = (BATCH, SEQ_LEN, HD)
    return jax.random.truncated_normal(first_key, -4.0, 4.0, whole_shape, jnp.float32).astype(jnp.bfloat16)


def draw_positions(key, part):
    device_count = SEQ_LEN // SROWS
    round_keys = jax.random.split(jax.random.fold_in(key, 11), BATCH * SROWS)
    orders = jax.vmap(lambda round_key: jax.random.permutation(round_key, device_count))(round_keys)
    orders = orders.reshape(BATCH, SROWS, device_count).astype(jnp.int32)
    round_base = (jnp.arange(SROWS, dtype=jnp.int32) * device_count)[None, :, None]
    placed = round_base + orders
    return placed.transpose(0, 2, 1).reshape(BATCH, SEQ_LEN)


def spiked(drawn, stream_key, source, target, blocks, factor):
    owner, partner = [(jnp.arange(drawn.shape[axis_at]) // (drawn.shape[axis_at] // blocks)).reshape([-1 if axis == axis_at else 1 for axis in range(drawn.ndim)]) for axis_at in (source, target)]
    chosen = jax.random.permutation(stream_key, blocks)[partner]
    strong = (owner == chosen) | (owner == (partner + blocks // 2) % blocks)
    return jnp.where(strong, factor * drawn, drawn)


def level_of(key, extent, pieces, low, high):
    level, own = 1.0, jax.random.fold_in(key, 6)
    for axis_at, shards_of in pieces:
        draws = jnp.exp(jax.random.uniform(jax.random.fold_in(own, axis_at), (shards_of,), jnp.float32, low / len(pieces), high / len(pieces)))
        level = level * jnp.repeat(draws, extent[axis_at] // shards_of).reshape([-1 if axis == axis_at else 1 for axis in range(len(extent))])
    return level


def profile(count, total, reach, lean):
    weights = [(1 << 20) // math.isqrt(rank ** lean) + 1 for rank in range(2, count + 1)]
    surplus, counts = total - reach - (count - 1), [1] * (count - 1)
    while surplus > 0:
        free = [i for i in range(count - 1) if counts[i] < reach]
        mass, left = sum([weights[i] for i in free]), surplus
        for i in free:
            extra = min(reach - counts[i], max(1, left * weights[i] // mass), surplus)
            counts[i] = counts[i] + extra
            surplus = surplus - extra
    return np.array([reach] + counts)


def ragged_sizes(stream_key, number_of, total, limit, slope):
    if number_of == 2:
        one = jax.random.randint(stream_key, (), max(1, total - limit), min(limit, total - 1) + 1)
        return jnp.stack([one, total - one])
    sizes = jnp.asarray(profile(number_of, total, limit, slope), jnp.int32)
    twos = (number_of - 1) // 2
    donor, taker = sizes[1:1 + 2 * twos:2], sizes[2:2 + 2 * twos:2]
    room = jnp.minimum(donor - 1, limit - taker)
    shifted = jax.random.randint(jax.random.fold_in(stream_key, 1), (twos,), 0, 1 << 20) % (room + 1)
    sizes = sizes.at[1:1 + 2 * twos:2].set(donor - shifted).at[2:2 + 2 * twos:2].set(taker + shifted)
    return sizes[jax.random.permutation(jax.random.fold_in(stream_key, 2), number_of)]


def centred(key, shape, spread, bound, pieces=(), kind=jnp.bfloat16):
    level = level_of(key, shape, pieces, -0.22, 0.18) if pieces else 1.0
    drawn = jax.random.normal(key, shape, jnp.float32) * spread * level
    return jnp.minimum(jnp.maximum(drawn, -bound), bound).astype(kind)


def heavy_noise(rng, extent, deviation, most, cuts, heavy, held_as=jnp.bfloat16):
    values = deviation * jax.random.normal(rng, extent, jnp.float32)
    if cuts:
        values = values * level_of(rng, extent, cuts, -0.22, 0.18)
    return jnp.clip(spiked(values, jax.random.fold_in(rng, 3), *heavy), -most, most).astype(held_as)


def setup_inputs(seed: int = 0) -> dict:
    key_list = jax.random.split(jax.random.key(seed), 9)
    layer_input = heavy_noise(key_list[0], (BATCH, SEQ_LEN, D), 0.0625, 1.0, ((0, 8), (1, 64)), (1, 2, 64, 4.0))
    queries = draw_queries(jax.random.fold_in(key_list[8], 71), 0)
    key_states = draw_key_states(jax.random.fold_in(key_list[8], 71), 0)
    value_states = centred(key_list[3], (BATCH, SEQ_LEN, HD), 1.0, 6.0, ((0, 8), (1, 64)))
    attn_output = centred(key_list[4], (BATCH, SEQ_LEN, HEADS * HD), 1.0, 6.0, ((0, 8), (1, 64)))
    out_grad = centred(key_list[5], (BATCH, SEQ_LEN, HEADS * HD), 1.0, 6.0, ((0, 8), (1, 64)))
    doc_ids = jax.vmap(lambda own: jnp.searchsorted(jnp.cumsum(ragged_sizes(own, DOCS, SEQ_LEN, DOC_MOST, 2)), jnp.arange(SEQ_LEN), side="right"))(jax.random.split(key_list[6], BATCH)).reshape((BATCH, SEQ_LEN)).astype(jnp.int32)
    positions = draw_positions(jax.random.fold_in(key_list[8], 71), 0)
    return dict(layer_input=layer_input, queries=queries, key_states=key_states, value_states=value_states, attn_output=attn_output, out_grad=out_grad, doc_ids=doc_ids, positions=positions)


NEG_FILL = -1e+30

def one_sequence(operands):
    query_seq, key_seq, value_seq, output_seq, grad_seq, doc_seq, pos_seq = operands
    seq_length = key_seq.shape[0]
    head_size = key_seq.shape[1]
    head_count = query_seq.shape[1] // head_size
    score_scale = 1.0 / math.sqrt(head_size)
    doc_rows = jnp.take(doc_seq, pos_seq)
    live_pairs = (doc_rows[:, None] == doc_rows[None, :]) & (pos_seq[None, :] <= pos_seq[:, None])
    query_heads = query_seq.reshape(seq_length, head_count, head_size).transpose(1, 0, 2)
    output_heads = output_seq.reshape(seq_length, head_count, head_size).transpose(1, 0, 2)
    grad_heads = grad_seq.reshape(seq_length, head_count, head_size).transpose(1, 0, 2)

    def one_head(key_accum, head_operands):
        query_head, output_head, grad_head = head_operands
        scores = jnp.dot(query_head, key_seq.T, preferred_element_type=jnp.float32) * score_scale
        masked = jnp.where(live_pairs, scores, NEG_FILL)
        row_max = lax.optimization_barrier(jnp.max(masked, axis=1))
        row_sum = lax.optimization_barrier(jnp.sum(jnp.where(live_pairs, jnp.exp(scores - row_max[:, None]), 0.0), axis=1))
        log_total = row_max + jnp.log(row_sum)
        probs = jnp.where(live_pairs, jnp.exp(scores - log_total[:, None]), 0.0)
        probs_half = probs.astype(jnp.bfloat16)
        row_delta = lax.optimization_barrier(jnp.sum(grad_head.astype(jnp.float32) * output_head.astype(jnp.float32), axis=1))
        prob_grad = jnp.dot(grad_head, value_seq.T, preferred_element_type=jnp.float32)
        score_grad = (probs * (prob_grad - row_delta[:, None])).astype(jnp.bfloat16)
        query_grad = (jnp.dot(score_grad, key_seq, preferred_element_type=jnp.float32) * score_scale).astype(jnp.bfloat16)
        key_grad = jnp.dot(score_grad.T, query_head, preferred_element_type=jnp.float32) * score_scale
        value_grad = jnp.dot(probs_half.T, grad_head, preferred_element_type=jnp.float32)
        return (key_accum + jnp.concatenate([key_grad, value_grad], axis=1), query_grad)
    start_accum = jnp.zeros((seq_length, 2 * head_size), jnp.float32)
    key_total, query_parts = lax.scan(one_head, start_accum, (query_heads, output_heads, grad_heads))
    query_rows = query_parts.transpose(1, 0, 2).reshape(seq_length, head_count * head_size)
    return (query_rows, key_total)

def reference(layer_input, queries, key_states, value_states, attn_output, out_grad, doc_ids, positions):
    query_grad, key_totals = lax.map(one_sequence, (queries, key_states, value_states, attn_output, out_grad, doc_ids, positions))
    kv_grad = key_totals.astype(jnp.bfloat16)
    model_width = layer_input.shape[2]
    flat_input = layer_input.reshape(-1, model_width)
    flat_grad = kv_grad.reshape(-1, kv_grad.shape[2])
    kv_weight_grad = lax.dot_general(flat_input, flat_grad, (((0,), (0,)), ((), ())), preferred_element_type=jnp.float32)
    return (query_grad, kv_weight_grad)
```

```python
import math

import jax
import jax.numpy as jnp
from jax import lax
from jax.experimental import pallas as pl
from jax.experimental.pallas import tpu as pltpu
from jax.sharding import Mesh
from jax.sharding import PartitionSpec as P

BF = jnp.bfloat16
F32 = jnp.float32
HEADS = 8
HD = 128
ROWS = 64
CTX = 64
PAIRS = 32
HALO = 16
SEND = 72
BACK = 56
QN = CTX * 2 * HEADS
KH = CTX * HALO
KN = KH + CTX * 2
NEG = -1e30
FAR = 1 << 20
SCALE = 1.0 / math.sqrt(HD)
LOG2E = math.log2(math.e)


def iota(shape, dim):
    return lax.broadcasted_iota(jnp.int32, shape, dim)


def one_hot(condition):
    return jnp.where(condition, 1.0, 0.0).astype(BF)


def dot(a, b):
    return lax.dot_general(a, b, (((1,), (0,)), ((), ())), preferred_element_type=F32)


def dot_t(a, b):
    return lax.dot_general(a, b, (((1,), (1,)), ((), ())), preferred_element_type=F32)


def pack_kernel(q_ref, g_ref, o_ref, k_ref, v_ref, out_ref, split):
    def heads_to_rows(ref, at):
        wide = ref[0].astype(F32)
        for h in range(HEADS):
            split[pl.ds(h, ROWS, stride=HEADS), :] = wide[:, h * HD : (h + 1) * HD]
        out_ref[:, at : at + 16, :] = split[...].reshape(PAIRS, 16, HD).astype(BF)

    heads_to_rows(q_ref, 0)
    heads_to_rows(g_ref, 16)
    product = g_ref[0].astype(F32) * o_ref[0].astype(F32)
    lane = iota((ROWS, HD), 1)
    delta = jnp.zeros((ROWS, HD), F32)
    for h in range(HEADS):
        total = jnp.sum(product[:, h * HD : (h + 1) * HD], axis=1, keepdims=True)
        delta = jnp.where(lane % HEADS == h, total, delta)
    high = delta.astype(BF).astype(F32)
    rest = delta - high
    middle = rest.astype(BF).astype(F32)
    low = rest - middle
    pieces = jnp.where(lane < 8, high, jnp.where(lane < 16, middle, low))
    pieces = jnp.where(lane < 24, -pieces, 0.0).astype(BF)
    keys, values = k_ref[0], v_ref[0]
    target, row = iota((PAIRS * HALO, ROWS), 0), iota((PAIRS * HALO, ROWS), 1)
    window = one_hot(row == 2 * (target // HALO) + target % HALO - HALO)
    out_ref[:, 32:48, :] = dot(window, keys).reshape(PAIRS, HALO, HD).astype(BF)
    out_ref[:, 48:64, :] = dot(window, values).reshape(PAIRS, HALO, HD).astype(BF)
    target, row = iota((PAIRS * 8, ROWS), 0), iota((PAIRS * 8, ROWS), 1)
    slot = target % 8
    here = row == 2 * (target // 8) + slot % 2
    own = dot(one_hot(here & (slot // 2 == 0)), keys)
    own = own + dot(one_hot(here & (slot // 2 == 1)), values)
    own = own + dot(one_hot(here & (slot // 2 == 2)), pieces)
    out_ref[:, 64:72, :] = own.reshape(PAIRS, 8, HD).astype(BF)


def attend_kernel(in_ref, kpos_ref, qpos_ref, qlow_ref, out_ref, keys, values, dkey, dvalue):
    extra = in_ref[:, 64:72, :].astype(F32).reshape(CTX * 8, HD).astype(BF)
    token, source = iota((CTX * 2, CTX * 8), 0), iota((CTX * 2, CTX * 8), 1)
    base = source == (token // 2) * 8 + token % 2

    def picked(offset):
        chosen = source == (token // 2) * 8 + token % 2 + offset
        return dot(one_hot(chosen), extra).astype(BF)

    keys[0:KH, :] = in_ref[:, 32:48, :].reshape(KH, HD)
    keys[KH:KN, :] = picked(0)
    values[0:KH, 0:HD] = in_ref[:, 48:64, :].reshape(KH, HD)
    values[KH:KN, 0:HD] = picked(2)
    values[:, HD : 2 * HD] = one_hot(iota((KN, HD), 1) < 24)
    delta = picked(4)
    kpos = jnp.broadcast_to(kpos_ref[...], (HD, KN)).T
    key_columns = keys[...].astype(F32).T.astype(BF)
    count = 256
    for c in range(QN // count):
        first = c * (count // 16)
        qc = in_ref[first : first + count // 16, 0:16, :].reshape(count, HD)
        gc = in_ref[first : first + count // 16, 16:32, :].reshape(count, HD)
        row, col = iota((count, HD), 0), iota((count, HD), 1)
        spread = dot(one_hot(col == c * (count // HEADS) + row // HEADS), delta)
        spread = jnp.where(col % HEADS == row % HEADS, spread, 0.0).astype(BF)
        scores = dot_t(keys[...], qc)
        at = slice(c * count, (c + 1) * count)
        qpos, qlow = qpos_ref[:, at], qlow_ref[:, at]
        kp = jnp.concatenate([kpos, kpos], axis=1)
        scores = jnp.where((kp <= qpos) & (kp >= qlow), scores, NEG)
        top = jnp.max(scores, axis=0, keepdims=True)
        probs = jnp.exp2((scores - top) * (SCALE * LOG2E))
        probs = probs * (1.0 / jnp.sum(probs, axis=0, keepdims=True))
        change = dot_t(values[...], jnp.concatenate([gc, spread], axis=1))
        sgrad = (probs * change).astype(BF)
        value_part = dot(probs.astype(BF), gc)
        key_part = dot(sgrad, qc)
        if c == 0:
            dvalue[...] = value_part
            dkey[...] = key_part
        else:
            dvalue[...] += value_part
            dkey[...] += key_part
        qgrad = (dot(key_columns, sgrad) * SCALE).T
        out_ref[first : first + count // 16, 0:16, :] = qgrad.reshape(count // 16, 16, HD).astype(BF)
    out_ref[:, 16:32, :] = (dkey[0:KH, :] * SCALE).reshape(CTX, HALO, HD).astype(BF)
    out_ref[:, 32:48, :] = dvalue[0:KH, :].reshape(CTX, HALO, HD).astype(BF)
    source, token = iota((CTX * 8, CTX * 2), 0), iota((CTX * 8, CTX * 2), 1)
    home = (token // 2) * 8 + token % 2
    own = dot(one_hot(source == home), (dkey[KH:KN, :] * SCALE).astype(BF))
    own = own + dot(one_hot(source == home + 2), dvalue[KH:KN, :].astype(BF))
    out_ref[:, 48:56, :] = own.reshape(CTX, 8, HD).astype(BF)


def collect_kernel(in_ref, q_ref, kv_ref, split):
    split[...] = in_ref[:, 0:16, :].astype(F32).reshape(PAIRS * 16, HD)
    for h in range(HEADS):
        q_ref[0, :, h * HD : (h + 1) * HD] = split[pl.ds(h, ROWS, stride=HEADS), :].astype(BF)
    row, source = iota((ROWS, PAIRS * HALO), 0), iota((ROWS, PAIRS * HALO), 1)
    window = one_hot(row == 2 * (source // HALO) + source % HALO - HALO)
    row, source = iota((ROWS, PAIRS * 8), 0), iota((ROWS, PAIRS * 8), 1)
    slot = source % 8
    here = row == 2 * (source // 8) + slot % 2
    extra = in_ref[:, 48:56, :].astype(F32).reshape(PAIRS * 8, HD).astype(BF)
    for part in range(2):
        halo = in_ref[:, 16 + 16 * part : 32 + 16 * part, :].reshape(PAIRS * HALO, HD)
        total = dot(window, halo) + dot(one_hot(here & (slot // 2 == part)), extra)
        kv_ref[0, :, part * HD : (part + 1) * HD] = total.astype(BF)


def whole(shape):
    return pl.BlockSpec(shape, lambda *_: (0,) * len(shape))


def local(
    layer_input, queries, key_states, value_states, attn_output, out_grad, doc_ids, positions
):
    ctx = ("x", "zl", "y")
    index = lax.axis_index(ctx)
    sequence, pair = index // PAIRS, index % PAIRS

    x_at = lax.axis_index("x")
    model = layer_input.shape[2]
    quarter = model // 4
    flat_input = layer_input.reshape(2 * ROWS, model)
    pieces = []
    for step in range(4):
        piece = lax.dynamic_slice_in_dim(flat_input, (x_at + step) % 4 * quarter, quarter, 1)
        if step:
            piece = lax.ppermute(piece, "x", [(i, (i + step) % 4) for i in range(4)])
        pieces.append(piece)

    row_spec = lambda width: pl.BlockSpec((1, ROWS, width), lambda s: (s, 0, 0))
    sent = pl.pallas_call(
        pack_kernel,
        out_shape=jax.ShapeDtypeStruct((CTX, SEND, HD), BF),
        grid=(2,),
        in_specs=[row_spec(1024), row_spec(1024), row_spec(1024), row_spec(HD), row_spec(HD)],
        out_specs=pl.BlockSpec((PAIRS, SEND, HD), lambda s: (s, 0, 0)),
        scratch_shapes=[pltpu.VMEM((ROWS * HEADS, HD), F32)],
        name="pack",
    )(queries, out_grad, attn_output, key_states, value_states)
    arrived = lax.all_to_all(sent, ctx, 0, 0, tiled=True)

    docs = lax.dynamic_index_in_dim(doc_ids, sequence, 0, keepdims=False)
    places = lax.dynamic_index_in_dim(positions, sequence, 0, keepdims=False).reshape(CTX, ROWS)
    places = jnp.pad(places, ((0, 0), (HALO, 0)), constant_values=FAR)
    places = lax.dynamic_slice_in_dim(places, 2 * pair, HALO + 2, 1)
    own = places[:, HALO:].reshape(CTX * 2)
    kpos = jnp.concatenate([places[:, :HALO].reshape(KH), own])[None, :]
    starts = jnp.sum(docs[None, :] < jnp.arange(16)[:, None], axis=1)
    low = jnp.max(jnp.where(starts[:, None] <= own[None, :], starts[:, None], 0), axis=0)
    qpos = jnp.repeat(own, HEADS)[None, :]
    qlow = jnp.repeat(low, HEADS)[None, :]

    back = pl.pallas_call(
        attend_kernel,
        out_shape=jax.ShapeDtypeStruct((CTX, BACK, HD), BF),
        grid=(1,),
        in_specs=[whole((CTX, SEND, HD)), whole((1, KN)), whole((1, QN)), whole((1, QN))],
        out_specs=whole((CTX, BACK, HD)),
        scratch_shapes=[
            pltpu.VMEM((KN, HD), BF),
            pltpu.VMEM((KN, 2 * HD), BF),
            pltpu.VMEM((KN, HD), F32),
            pltpu.VMEM((KN, HD), F32),
        ],
        compiler_params=pltpu.CompilerParams(vmem_limit_bytes=48 << 20),
        name="attend",
    )(arrived, kpos.astype(F32), qpos.astype(F32), qlow.astype(F32))
    home = lax.all_to_all(back, ctx, 0, 0, tiled=True)

    query_grad, kv_grad = pl.pallas_call(
        collect_kernel,
        out_shape=(
            jax.ShapeDtypeStruct((2, ROWS, HEADS * HD), BF),
            jax.ShapeDtypeStruct((2, ROWS, 2 * HD), BF),
        ),
        grid=(2,),
        in_specs=[pl.BlockSpec((PAIRS, BACK, HD), lambda s: (s, 0, 0))],
        out_specs=(row_spec(HEADS * HD), row_spec(2 * HD)),
        scratch_shapes=[pltpu.VMEM((PAIRS * 16, HD), F32)],
        name="collect",
    )(home)

    flat_grad = kv_grad.reshape(2 * ROWS, 2 * HD)
    grads = lax.all_to_all(
        jnp.broadcast_to(flat_grad[None], (4, 2 * ROWS, 2 * HD)), "x", 0, 0, tiled=True
    )
    part = jnp.zeros((quarter, 2 * HD), F32)
    for step in range(4):
        grad = lax.dynamic_index_in_dim(grads, (x_at - step) % 4, 0, keepdims=False)
        part = part + lax.dot_general(
            pieces[step], grad, (((0,), (0,)), ((), ())), preferred_element_type=F32
        )
    core = lax.axis_index("core")
    halves = part.reshape(16, 2, 32, 2 * HD)
    mine = lax.dynamic_index_in_dim(halves, core, 1, keepdims=False)
    other = lax.dynamic_index_in_dim(halves, 1 - core, 1, keepdims=False)
    mine = mine + lax.ppermute(other, "core", [(0, 1), (1, 0)])
    mine = jnp.sum(lax.all_to_all(mine, ("zl", "y"), 0, 0, tiled=True), axis=0)
    dp = lax.axis_size("zh") * 2
    shares = lax.all_to_all(
        jnp.broadcast_to(mine[None], (dp, 32, 2 * HD)), ("zh", "core"), 0, 0, tiled=True
    )
    weight_grad = jnp.sum(shares.reshape(dp // 2, 64, 2 * HD), axis=0)
    return (query_grad, weight_grad)


def solution(mesh):
    devices = mesh.devices.reshape(4, 4, 4, -1, 2)
    inner = Mesh(devices, ("x", "zl", "y", "zh", "core"))
    ctx, dp = ("x", "zl", "y"), ("zh", "core")
    rows = P(dp, ctx, None)
    whole_rows = P(dp, None)
    return jax.shard_map(
        local,
        mesh=inner,
        in_specs=(rows,) * 6 + (whole_rows,) * 2,
        out_specs=(rows, P(ctx, None)),
        check_vma=False,
    )
```

```python
import math

import jax
import jax.numpy as jnp
from jax import lax
from jax.experimental import pallas as pl
from jax.experimental.pallas import tpu as pltpu
from jax.sharding import Mesh
from jax.sharding import PartitionSpec as P

BF = jnp.bfloat16
F32 = jnp.float32
HEADS = 8
HD = 128
ROWS = 64
CTX = 64
PAIRS = 32
HALO = 16
SEND = 72
BACK = 56
QN = CTX * 2 * HEADS
KH = CTX * HALO
KN = KH + CTX * 2
NEG = -1e30
FAR = 1 << 20
SCALE = 1.0 / math.sqrt(HD)
LOG2E = math.log2(math.e)


def iota(shape, dim):
    return lax.broadcasted_iota(jnp.int32, shape, dim)


def one_hot(condition):
    return jnp.where(condition, 1.0, 0.0).astype(BF)


def dot(a, b):
    return lax.dot_general(a, b, (((1,), (0,)), ((), ())), preferred_element_type=F32)


def dot_t(a, b):
    return lax.dot_general(a, b, (((1,), (1,)), ((), ())), preferred_element_type=F32)


def pack_kernel(q_ref, g_ref, o_ref, k_ref, v_ref, out_ref, split):
    def heads_to_rows(ref, at):
        wide = ref[0].astype(F32)
        for h in range(HEADS):
            split[pl.ds(h, ROWS, stride=HEADS), :] = wide[:, h * HD : (h + 1) * HD]
        out_ref[:, at : at + 16, :] = split[...].reshape(PAIRS, 16, HD).astype(BF)

    heads_to_rows(q_ref, 0)
    heads_to_rows(g_ref, 16)
    product = g_ref[0].astype(F32) * o_ref[0].astype(F32)
    lane = iota((ROWS, HD), 1)
    delta = jnp.zeros((ROWS, HD), F32)
    for h in range(HEADS):
        total = jnp.sum(product[:, h * HD : (h + 1) * HD], axis=1, keepdims=True)
        delta = jnp.where(lane % HEADS == h, total, delta)
    high = delta.astype(BF).astype(F32)
    rest = delta - high
    middle = rest.astype(BF).astype(F32)
    low = rest - middle
    pieces = jnp.where(lane < 8, high, jnp.where(lane < 16, middle, low))
    pieces = jnp.where(lane < 24, -pieces, 0.0).astype(BF)
    keys, values = k_ref[0], v_ref[0]
    target, row = iota((PAIRS * HALO, ROWS), 0), iota((PAIRS * HALO, ROWS), 1)
    window = one_hot(row == 2 * (target // HALO) + target % HALO - HALO)
    out_ref[:, 32:48, :] = dot(window, keys).reshape(PAIRS, HALO, HD).astype(BF)
    out_ref[:, 48:64, :] = dot(window, values).reshape(PAIRS, HALO, HD).astype(BF)
    target, row = iota((PAIRS * 8, ROWS), 0), iota((PAIRS * 8, ROWS), 1)
    slot = target % 8
    here = row == 2 * (target // 8) + slot % 2
    own = dot(one_hot(here & (slot // 2 == 0)), keys)
    own = own + dot(one_hot(here & (slot // 2 == 1)), values)
    own = own + dot(one_hot(here & (slot // 2 == 2)), pieces)
    out_ref[:, 64:72, :] = own.reshape(PAIRS, 8, HD).astype(BF)


def attend_kernel(in_ref, kpos_ref, qpos_ref, qlow_ref, out_ref, keys, values, dkey, dvalue):
    extra = in_ref[:, 64:72, :].astype(F32).reshape(CTX * 8, HD).astype(BF)
    token, source = iota((CTX * 2, CTX * 8), 0), iota((CTX * 2, CTX * 8), 1)
    base = source == (token // 2) * 8 + token % 2

    def picked(offset):
        chosen = source == (token // 2) * 8 + token % 2 + offset
        return dot(one_hot(chosen), extra).astype(BF)

    keys[0:KH, :] = in_ref[:, 32:48, :].reshape(KH, HD)
    keys[KH:KN, :] = picked(0)
    values[0:KH, 0:HD] = in_ref[:, 48:64, :].reshape(KH, HD)
    values[KH:KN, 0:HD] = picked(2)
    values[:, HD : 2 * HD] = one_hot(iota((KN, HD), 1) < 24)
    delta = picked(4)
    kpos = jnp.broadcast_to(kpos_ref[...], (HD, KN)).T
    key_columns = keys[...].astype(F32).T.astype(BF)
    count = 256
    for c in range(QN // count):
        first = c * (count // 16)
        qc = in_ref[first : first + count // 16, 0:16, :].reshape(count, HD)
        gc = in_ref[first : first + count // 16, 16:32, :].reshape(count, HD)
        row, col = iota((count, HD), 0), iota((count, HD), 1)
        spread = dot(one_hot(col == c * (count // HEADS) + row // HEADS), delta)
        spread = jnp.where(col % HEADS == row % HEADS, spread, 0.0).astype(BF)
        scores = dot_t(keys[...], qc)
        at = slice(c * count, (c + 1) * count)
        qpos, qlow = qpos_ref[:, at], qlow_ref[:, at]
        kp = jnp.concatenate([kpos, kpos], axis=1)
        scores = jnp.where((kp <= qpos) & (kp >= qlow), scores, NEG)
        top = jnp.max(scores, axis=0, keepdims=True)
        probs = jnp.exp2((scores - top) * (SCALE * LOG2E))
        probs = probs * (1.0 / jnp.sum(probs, axis=0, keepdims=True))
        change = dot_t(values[...], jnp.concatenate([gc, spread], axis=1))
        sgrad = (probs * change).astype(BF)
        value_part = dot(probs.astype(BF), gc)
        key_part = dot(sgrad, qc)
        if c == 0:
            dvalue[...] = value_part
            dkey[...] = key_part
        else:
            dvalue[...] += value_part
            dkey[...] += key_part
        qgrad = (dot(key_columns, sgrad) * SCALE).T
        out_ref[first : first + count // 16, 0:16, :] = qgrad.reshape(count // 16, 16, HD).astype(BF)
    out_ref[:, 16:32, :] = (dkey[0:KH, :] * SCALE).reshape(CTX, HALO, HD).astype(BF)
    out_ref[:, 32:48, :] = dvalue[0:KH, :].reshape(CTX, HALO, HD).astype(BF)
    source, token = iota((CTX * 8, CTX * 2), 0), iota((CTX * 8, CTX * 2), 1)
    home = (token // 2) * 8 + token % 2
    own = dot(one_hot(source == home), (dkey[KH:KN, :] * SCALE).astype(BF))
    own = own + dot(one_hot(source == home + 2), dvalue[KH:KN, :].astype(BF))
    out_ref[:, 48:56, :] = own.reshape(CTX, 8, HD).astype(BF)


def collect_kernel(in_ref, q_ref, kv_ref, split):
    split[...] = in_ref[:, 0:16, :].astype(F32).reshape(PAIRS * 16, HD)
    for h in range(HEADS):
        q_ref[0, :, h * HD : (h + 1) * HD] = split[pl.ds(h, ROWS, stride=HEADS), :].astype(BF)
    row, source = iota((ROWS, PAIRS * HALO), 0), iota((ROWS, PAIRS * HALO), 1)
    window = one_hot(row == 2 * (source // HALO) + source % HALO - HALO)
    row, source = iota((ROWS, PAIRS * 8), 0), iota((ROWS, PAIRS * 8), 1)
    slot = source % 8
    here = row == 2 * (source // 8) + slot % 2
    extra = in_ref[:, 48:56, :].astype(F32).reshape(PAIRS * 8, HD).astype(BF)
    for part in range(2):
        halo = in_ref[:, 16 + 16 * part : 32 + 16 * part, :].reshape(PAIRS * HALO, HD)
        total = dot(window, halo) + dot(one_hot(here & (slot // 2 == part)), extra)
        for copy in range(8):
            kv_ref[copy, :, part * HD : (part + 1) * HD] = total.astype(BF)


def columns_kernel(in_ref, out_ref, choice):
    narrow, wide = out_ref.shape[2], in_ref.shape[2]

    @pl.when(pl.program_id(0) == 0)
    def _():
        target, source = iota((narrow, wide), 0), iota((narrow, wide), 1)
        base = target % 128 // 32 * 256 + target // 128 * 64 + target % 32
        for core in range(2):
            choice[core] = one_hot(source == base + 32 * core)

    rows = in_ref[...].reshape(2 * ROWS, wide)
    for core in range(2):
        out_ref[0, core] = dot_t(choice[core], rows).astype(BF)


def weigh_kernel(from_ref, *refs):
    piece_refs, grads_ref, out_ref = refs[:8], refs[8], refs[9]
    total = dot(piece_refs[0][...], grads_ref[from_ref[0]])
    for step in range(1, 8):
        total = total + dot(piece_refs[step][...], grads_ref[from_ref[step]])
    out_ref[...] = total


def whole(shape):
    return pl.BlockSpec(shape, lambda *_: (0,) * len(shape))


def local(
    layer_input, queries, key_states, value_states, attn_output, out_grad, doc_ids, positions
):
    ctx = ("x", "zl", "y")
    index = lax.axis_index(ctx)
    sequence, pair = index // PAIRS, index % PAIRS

    model = layer_input.shape[2]
    picked = pl.pallas_call(
        columns_kernel,
        out_shape=jax.ShapeDtypeStruct((4, 2, model // 8, 2 * ROWS), BF),
        grid=(4,),
        in_specs=[pl.BlockSpec((2, ROWS, model // 4), lambda i: (0, 0, i))],
        out_specs=pl.BlockSpec((1, 2, model // 8, 2 * ROWS), lambda i: (i, 0, 0, 0)),
        scratch_shapes=[pltpu.VMEM((2, model // 8, model // 4), BF)],
        name="columns",
    )(layer_input)
    picked = picked.reshape(8, model // 8, 2 * ROWS)
    x_at, core = lax.axis_index("x"), lax.axis_index("core")
    columns, origins = [], []
    for step in range(4):
        for swap in range(2):
            target = (x_at + step) % 4 * 2 + (core + swap) % 2
            piece = lax.dynamic_index_in_dim(picked, target, 0, keepdims=False)
            if step or swap:
                route = [
                    (2 * i + j, (i + step) % 4 * 2 + (j + swap) % 2)
                    for i in range(4)
                    for j in range(2)
                ]
                piece = lax.ppermute(piece, ("x", "core"), route)
            columns.append(piece)
            origins.append((x_at - step) % 4 * 2 + (core + swap) % 2)

    row_spec = lambda width: pl.BlockSpec((1, ROWS, width), lambda s: (s, 0, 0))
    sent = pl.pallas_call(
        pack_kernel,
        out_shape=jax.ShapeDtypeStruct((CTX, SEND, HD), BF),
        grid=(2,),
        in_specs=[row_spec(1024), row_spec(1024), row_spec(1024), row_spec(HD), row_spec(HD)],
        out_specs=pl.BlockSpec((PAIRS, SEND, HD), lambda s: (s, 0, 0)),
        scratch_shapes=[pltpu.VMEM((ROWS * HEADS, HD), F32)],
        name="pack",
    )(queries, out_grad, attn_output, key_states, value_states)
    arrived = lax.all_to_all(sent, ctx, 0, 0, tiled=True)
    arrived, *columns = lax.optimization_barrier((arrived, *columns))

    docs = lax.dynamic_index_in_dim(doc_ids, sequence, 0, keepdims=False)
    places = lax.dynamic_index_in_dim(positions, sequence, 0, keepdims=False).reshape(CTX, ROWS)
    places = jnp.pad(places, ((0, 0), (HALO, 0)), constant_values=FAR)
    places = lax.dynamic_slice_in_dim(places, 2 * pair, HALO + 2, 1)
    own = places[:, HALO:].reshape(CTX * 2)
    kpos = jnp.concatenate([places[:, :HALO].reshape(KH), own])[None, :]
    starts = jnp.sum(docs[None, :] < jnp.arange(16)[:, None], axis=1)
    low = jnp.max(jnp.where(starts[:, None] <= own[None, :], starts[:, None], 0), axis=0)
    qpos = jnp.repeat(own, HEADS)[None, :]
    qlow = jnp.repeat(low, HEADS)[None, :]

    back = pl.pallas_call(
        attend_kernel,
        out_shape=jax.ShapeDtypeStruct((CTX, BACK, HD), BF),
        grid=(1,),
        in_specs=[whole((CTX, SEND, HD)), whole((1, KN)), whole((1, QN)), whole((1, QN))],
        out_specs=whole((CTX, BACK, HD)),
        scratch_shapes=[
            pltpu.VMEM((KN, HD), BF),
            pltpu.VMEM((KN, 2 * HD), BF),
            pltpu.VMEM((KN, HD), F32),
            pltpu.VMEM((KN, HD), F32),
        ],
        compiler_params=pltpu.CompilerParams(vmem_limit_bytes=48 << 20),
        name="attend",
    )(arrived, kpos.astype(F32), qpos.astype(F32), qlow.astype(F32))
    home = lax.all_to_all(back, ctx, 0, 0, tiled=True)

    query_grad, kv_grad = pl.pallas_call(
        collect_kernel,
        out_shape=(
            jax.ShapeDtypeStruct((2, ROWS, HEADS * HD), BF),
            jax.ShapeDtypeStruct((8, 2 * ROWS, 2 * HD), BF),
        ),
        grid=(2,),
        in_specs=[pl.BlockSpec((PAIRS, BACK, HD), lambda s: (s, 0, 0))],
        out_specs=(
            row_spec(HEADS * HD),
            pl.BlockSpec((8, ROWS, 2 * HD), lambda s: (0, s, 0)),
        ),
        scratch_shapes=[pltpu.VMEM((PAIRS * 16, HD), F32)],
        name="collect",
    )(home)

    grads = lax.all_to_all(kv_grad, ("x", "core"), 0, 0, tiled=True)
    vmem = pl.BlockSpec(memory_space=pltpu.VMEM)
    part = pl.pallas_call(
        weigh_kernel,
        out_shape=jax.ShapeDtypeStruct((model // 8, 2 * HD), F32),
        in_specs=[pl.BlockSpec(memory_space=pltpu.SMEM)] + [vmem] * 9,
        out_specs=vmem,
        name="weigh",
    )(jnp.stack(origins), *columns, grads)
    part = lax.all_to_all(part.reshape(4, 128, 2 * HD), "y", 0, 0, tiled=True)
    part = jnp.sum(part, axis=0)
    part = lax.all_to_all(part.reshape(16, 8, 2 * HD), ("zl", "zh"), 0, 0, tiled=True)
    part = jnp.sum(part, axis=0)
    shares = lax.all_to_all(
        jnp.broadcast_to(part[None], (8, 8, 2 * HD)), ("zh", "core"), 0, 0, tiled=True
    )
    weight_grad = shares.reshape(4, 2, 8, 2 * HD).transpose(1, 0, 2, 3).reshape(64, 2 * HD)
    return (query_grad, weight_grad)


def solution(mesh):
    devices = mesh.devices.reshape(4, 4, 4, -1, 2)
    inner = Mesh(devices, ("x", "zl", "y", "zh", "core"))
    ctx, dp = ("x", "zl", "y"), ("zh", "core")
    rows = P(dp, ctx, None)
    whole_rows = P(dp, None)
    return jax.shard_map(
        local,
        mesh=inner,
        in_specs=(rows,) * 6 + (whole_rows,) * 2,
        out_specs=(rows, P(ctx, None)),
        check_vma=False,
    )
```

```python
import math

import jax
import jax.numpy as jnp
from jax import lax
from jax.experimental import pallas as pl
from jax.experimental.pallas import tpu as pltpu
from jax.sharding import Mesh
from jax.sharding import PartitionSpec as P

BF = jnp.bfloat16
F32 = jnp.float32
HEADS = 8
HD = 128
ROWS = 64
CTX = 64
PAIRS = 32
HALO = 16
SEND = 72
BACK = 56
QN = CTX * 2 * HEADS
KH = CTX * HALO
KN = KH + CTX * 2
NEG = -1e30
FAR = 1 << 20
SCALE = 1.0 / math.sqrt(HD)
LOG2E = math.log2(math.e)


def iota(shape, dim):
    return lax.broadcasted_iota(jnp.int32, shape, dim)


def one_hot(condition):
    return jnp.where(condition, 1.0, 0.0).astype(BF)


def dot(a, b):
    return lax.dot_general(a, b, (((1,), (0,)), ((), ())), preferred_element_type=F32)


def dot_t(a, b):
    return lax.dot_general(a, b, (((1,), (1,)), ((), ())), preferred_element_type=F32)


def pack_kernel(q_ref, g_ref, o_ref, k_ref, v_ref, out_ref, split):
    def heads_to_rows(ref, at):
        wide = ref[0].astype(F32)
        for h in range(HEADS):
            split[pl.ds(h, ROWS, stride=HEADS), :] = wide[:, h * HD : (h + 1) * HD]
        out_ref[:, at : at + 16, :] = split[...].reshape(PAIRS, 16, HD).astype(BF)

    heads_to_rows(q_ref, 0)
    heads_to_rows(g_ref, 16)
    product = g_ref[0].astype(F32) * o_ref[0].astype(F32)
    lane = iota((ROWS, HD), 1)
    delta = jnp.zeros((ROWS, HD), F32)
    for h in range(HEADS):
        total = jnp.sum(product[:, h * HD : (h + 1) * HD], axis=1, keepdims=True)
        delta = jnp.where(lane % HEADS == h, total, delta)
    high = delta.astype(BF).astype(F32)
    rest = delta - high
    middle = rest.astype(BF).astype(F32)
    low = rest - middle
    pieces = jnp.where(lane < 8, high, jnp.where(lane < 16, middle, low))
    pieces = jnp.where(lane < 24, -pieces, 0.0).astype(BF)
    keys, values = k_ref[0], v_ref[0]
    target, row = iota((PAIRS * HALO, ROWS), 0), iota((PAIRS * HALO, ROWS), 1)
    window = one_hot(row == 2 * (target // HALO) + target % HALO - HALO)
    out_ref[:, 32:48, :] = dot(window, keys).reshape(PAIRS, HALO, HD).astype(BF)
    out_ref[:, 48:64, :] = dot(window, values).reshape(PAIRS, HALO, HD).astype(BF)
    target, row = iota((PAIRS * 8, ROWS), 0), iota((PAIRS * 8, ROWS), 1)
    slot = target % 8
    here = row == 2 * (target // 8) + slot % 2
    own = dot(one_hot(here & (slot // 2 == 0)), keys)
    own = own + dot(one_hot(here & (slot // 2 == 1)), values)
    own = own + dot(one_hot(here & (slot // 2 == 2)), pieces)
    out_ref[:, 64:72, :] = own.reshape(PAIRS, 8, HD).astype(BF)


def attend_kernel(in_ref, kpos_ref, qpos_ref, qlow_ref, out_ref, keys, values, dkey, dvalue):
    extra = in_ref[:, 64:72, :].astype(F32).reshape(CTX * 8, HD).astype(BF)
    token, source = iota((CTX * 2, CTX * 8), 0), iota((CTX * 2, CTX * 8), 1)
    base = source == (token // 2) * 8 + token % 2

    def picked(offset):
        chosen = source == (token // 2) * 8 + token % 2 + offset
        return dot(one_hot(chosen), extra).astype(BF)

    keys[0:KH, :] = in_ref[:, 32:48, :].reshape(KH, HD)
    keys[KH:KN, :] = picked(0)
    values[0:KH, 0:HD] = in_ref[:, 48:64, :].reshape(KH, HD)
    values[KH:KN, 0:HD] = picked(2)
    values[:, HD : 2 * HD] = one_hot(iota((KN, HD), 1) < 24)
    delta = picked(4)
    kpos = jnp.broadcast_to(kpos_ref[...], (HD, KN)).T
    key_columns = keys[...].astype(F32).T.astype(BF)
    count = 256
    for c in range(QN // count):
        first = c * (count // 16)
        qc = in_ref[first : first + count // 16, 0:16, :].reshape(count, HD)
        gc = in_ref[first : first + count // 16, 16:32, :].reshape(count, HD)
        row, col = iota((count, HD), 0), iota((count, HD), 1)
        spread = dot(one_hot(col == c * (count // HEADS) + row // HEADS), delta)
        spread = jnp.where(col % HEADS == row % HEADS, spread, 0.0).astype(BF)
        scores = dot_t(keys[...], qc)
        at = slice(c * count, (c + 1) * count)
        qpos, qlow = qpos_ref[:, at], qlow_ref[:, at]
        kp = jnp.concatenate([kpos, kpos], axis=1)
        scores = jnp.where((kp <= qpos) & (kp >= qlow), scores, NEG)
        top = jnp.max(scores, axis=0, keepdims=True)
        probs = jnp.exp2((scores - top) * (SCALE * LOG2E))
        probs = probs * (1.0 / jnp.sum(probs, axis=0, keepdims=True))
        change = dot_t(values[...], jnp.concatenate([gc, spread], axis=1))
        sgrad = (probs * change).astype(BF)
        value_part = dot(probs.astype(BF), gc)
        key_part = dot(sgrad, qc)
        if c == 0:
            dvalue[...] = value_part
            dkey[...] = key_part
        else:
            dvalue[...] += value_part
            dkey[...] += key_part
        qgrad = (dot(key_columns, sgrad) * SCALE).T
        out_ref[first : first + count // 16, 0:16, :] = qgrad.reshape(count // 16, 16, HD).astype(BF)
    out_ref[:, 16:32, :] = (dkey[0:KH, :] * SCALE).reshape(CTX, HALO, HD).astype(BF)
    out_ref[:, 32:48, :] = dvalue[0:KH, :].reshape(CTX, HALO, HD).astype(BF)
    source, token = iota((CTX * 8, CTX * 2), 0), iota((CTX * 8, CTX * 2), 1)
    home = (token // 2) * 8 + token % 2
    own = dot(one_hot(source == home), (dkey[KH:KN, :] * SCALE).astype(BF))
    own = own + dot(one_hot(source == home + 2), dvalue[KH:KN, :].astype(BF))
    out_ref[:, 48:56, :] = own.reshape(CTX, 8, HD).astype(BF)


def collect_kernel(in_ref, q_ref, kv_ref, split):
    split[...] = in_ref[:, 0:16, :].astype(F32).reshape(PAIRS * 16, HD)
    for h in range(HEADS):
        q_ref[0, :, h * HD : (h + 1) * HD] = split[pl.ds(h, ROWS, stride=HEADS), :].astype(BF)
    row, source = iota((ROWS, PAIRS * HALO), 0), iota((ROWS, PAIRS * HALO), 1)
    window = one_hot(row == 2 * (source // HALO) + source % HALO - HALO)
    row, source = iota((ROWS, PAIRS * 8), 0), iota((ROWS, PAIRS * 8), 1)
    slot = source % 8
    here = row == 2 * (source // 8) + slot % 2
    extra = in_ref[:, 48:56, :].astype(F32).reshape(PAIRS * 8, HD).astype(BF)
    for part in range(2):
        halo = in_ref[:, 16 + 16 * part : 32 + 16 * part, :].reshape(PAIRS * HALO, HD)
        total = dot(window, halo) + dot(one_hot(here & (slot // 2 == part)), extra)
        for copy in range(4):
            kv_ref[copy, :, part * HD : (part + 1) * HD] = total.astype(BF)


def whole(shape):
    return pl.BlockSpec(shape, lambda *_: (0,) * len(shape))


def local(
    layer_input, queries, key_states, value_states, attn_output, out_grad, doc_ids, positions
):
    ctx = ("x", "zl", "y")
    index = lax.axis_index(ctx)
    sequence, pair = index // PAIRS, index % PAIRS

    quarter = layer_input.shape[2] // 4
    x_at, core = lax.axis_index("x"), lax.axis_index("core")
    flat_input = layer_input.reshape(2 * ROWS, 4 * quarter)
    columns = []
    for step in range(4):
        piece = lax.dynamic_slice_in_dim(flat_input, (x_at + step) % 4 * quarter, quarter, 1)
        if step:
            piece = lax.ppermute(piece, "x", [(i, (i + step) % 4) for i in range(4)])
        columns.append(piece)

    row_spec = lambda width: pl.BlockSpec((1, ROWS, width), lambda s: (s, 0, 0))
    sent = pl.pallas_call(
        pack_kernel,
        out_shape=jax.ShapeDtypeStruct((CTX, SEND, HD), BF),
        grid=(2,),
        in_specs=[row_spec(1024), row_spec(1024), row_spec(1024), row_spec(HD), row_spec(HD)],
        out_specs=pl.BlockSpec((PAIRS, SEND, HD), lambda s: (s, 0, 0)),
        scratch_shapes=[pltpu.VMEM((ROWS * HEADS, HD), F32)],
        name="pack",
    )(queries, out_grad, attn_output, key_states, value_states)
    arrived = lax.all_to_all(sent, ctx, 0, 0, tiled=True)
    arrived, *columns = lax.optimization_barrier((arrived, *columns))

    docs = lax.dynamic_index_in_dim(doc_ids, sequence, 0, keepdims=False)
    places = lax.dynamic_index_in_dim(positions, sequence, 0, keepdims=False).reshape(CTX, ROWS)
    places = jnp.pad(places, ((0, 0), (HALO, 0)), constant_values=FAR)
    places = lax.dynamic_slice_in_dim(places, 2 * pair, HALO + 2, 1)
    own = places[:, HALO:].reshape(CTX * 2)
    kpos = jnp.concatenate([places[:, :HALO].reshape(KH), own])[None, :]
    starts = jnp.sum(docs[None, :] < jnp.arange(16)[:, None], axis=1)
    low = jnp.max(jnp.where(starts[:, None] <= own[None, :], starts[:, None], 0), axis=0)
    qpos = jnp.repeat(own, HEADS)[None, :]
    qlow = jnp.repeat(low, HEADS)[None, :]

    back = pl.pallas_call(
        attend_kernel,
        out_shape=jax.ShapeDtypeStruct((CTX, BACK, HD), BF),
        grid=(1,),
        in_specs=[whole((CTX, SEND, HD)), whole((1, KN)), whole((1, QN)), whole((1, QN))],
        out_specs=whole((CTX, BACK, HD)),
        scratch_shapes=[
            pltpu.VMEM((KN, HD), BF),
            pltpu.VMEM((KN, 2 * HD), BF),
            pltpu.VMEM((KN, HD), F32),
            pltpu.VMEM((KN, HD), F32),
        ],
        compiler_params=pltpu.CompilerParams(vmem_limit_bytes=48 << 20),
        name="attend",
    )(arrived, kpos.astype(F32), qpos.astype(F32), qlow.astype(F32))
    home = lax.all_to_all(back, ctx, 0, 0, tiled=True)

    query_grad, kv_grad = pl.pallas_call(
        collect_kernel,
        out_shape=(
            jax.ShapeDtypeStruct((2, ROWS, HEADS * HD), BF),
            jax.ShapeDtypeStruct((4, 2 * ROWS, 2 * HD), BF),
        ),
        grid=(2,),
        in_specs=[pl.BlockSpec((PAIRS, BACK, HD), lambda s: (s, 0, 0))],
        out_specs=(
            row_spec(HEADS * HD),
            pl.BlockSpec((4, ROWS, 2 * HD), lambda s: (0, s, 0)),
        ),
        scratch_shapes=[pltpu.VMEM((PAIRS * 16, HD), F32)],
        name="collect",
    )(home)

    grads = lax.all_to_all(kv_grad, "x", 0, 0, tiled=True)
    part = jnp.zeros((quarter, 2 * HD), F32)
    for step in range(4):
        grad = lax.dynamic_index_in_dim(grads, (x_at - step) % 4, 0, keepdims=False)
        part = part + lax.dot_general(
            columns[step], grad, (((0,), (0,)), ((), ())), preferred_element_type=F32
        )
    halves = part.reshape(16, 2, 32, 2 * HD)
    mine = lax.dynamic_index_in_dim(halves, core, 1, keepdims=False)
    other = lax.dynamic_index_in_dim(halves, 1 - core, 1, keepdims=False)
    mine = (mine + lax.ppermute(other, "core", [(0, 1), (1, 0)])).astype(BF)
    mine = lax.all_to_all(mine, ("zl", "y"), 0, 0, tiled=True)
    mine = jnp.sum(mine.astype(F32), axis=0)
    mine = lax.all_to_all(
        jnp.broadcast_to(mine[None], (4, 32, 2 * HD)), "zh", 0, 0, tiled=True
    )
    mine = jnp.sum(mine, axis=0)
    weight_grad = lax.all_gather(mine, "core", axis=0, tiled=True)
    return (query_grad, weight_grad)


def solution(mesh):
    devices = mesh.devices.reshape(4, 4, 4, -1, 2)
    inner = Mesh(devices, ("x", "zl", "y", "zh", "core"))
    ctx, dp = ("x", "zl", "y"), ("zh", "core")
    rows = P(dp, ctx, None)
    whole_rows = P(dp, None)
    return jax.shard_map(
        local,
        mesh=inner,
        in_specs=(rows,) * 6 + (whole_rows,) * 2,
        out_specs=(rows, P(ctx, None)),
        check_vma=False,
    )
```

```python
import math

import jax
import jax.numpy as jnp
from jax import lax
from jax.experimental import pallas as pl
from jax.experimental.pallas import tpu as pltpu
from jax.sharding import Mesh
from jax.sharding import PartitionSpec as P

BF = jnp.bfloat16
F32 = jnp.float32
HEADS = 8
HD = 128
ROWS = 64
CTX = 64
PAIRS = 32
HALO = 16
SEND = 72
BACK = 56
QN = CTX * 2 * HEADS
KH = CTX * HALO
KN = KH + CTX * 2
NEG = -1e30
FAR = 1 << 20
SCALE = 1.0 / math.sqrt(HD)
LOG2E = math.log2(math.e)


def iota(shape, dim):
    return lax.broadcasted_iota(jnp.int32, shape, dim)


def one_hot(condition):
    return jnp.where(condition, 1.0, 0.0).astype(BF)


def dot(a, b):
    return lax.dot_general(a, b, (((1,), (0,)), ((), ())), preferred_element_type=F32)


def dot_t(a, b):
    return lax.dot_general(a, b, (((1,), (1,)), ((), ())), preferred_element_type=F32)


def pack_kernel(q_ref, g_ref, o_ref, k_ref, v_ref, out_ref, split):
    def heads_to_rows(ref, at):
        wide = ref[0].astype(F32)
        for h in range(HEADS):
            split[pl.ds(h, ROWS, stride=HEADS), :] = wide[:, h * HD : (h + 1) * HD]
        out_ref[:, at : at + 16, :] = split[...].reshape(PAIRS, 16, HD).astype(BF)

    heads_to_rows(q_ref, 0)
    heads_to_rows(g_ref, 16)
    product = g_ref[0].astype(F32) * o_ref[0].astype(F32)
    lane = iota((ROWS, HD), 1)
    delta = jnp.zeros((ROWS, HD), F32)
    for h in range(HEADS):
        total = jnp.sum(product[:, h * HD : (h + 1) * HD], axis=1, keepdims=True)
        delta = jnp.where(lane % HEADS == h, total, delta)
    high = delta.astype(BF).astype(F32)
    rest = delta - high
    middle = rest.astype(BF).astype(F32)
    low = rest - middle
    pieces = jnp.where(lane < 8, high, jnp.where(lane < 16, middle, low))
    pieces = jnp.where(lane < 24, -pieces, 0.0).astype(BF)
    keys, values = k_ref[0], v_ref[0]
    target, row = iota((PAIRS * HALO, ROWS), 0), iota((PAIRS * HALO, ROWS), 1)
    window = one_hot(row == 2 * (target // HALO) + target % HALO - HALO)
    out_ref[:, 32:48, :] = dot(window, keys).reshape(PAIRS, HALO, HD).astype(BF)
    out_ref[:, 48:64, :] = dot(window, values).reshape(PAIRS, HALO, HD).astype(BF)
    target, row = iota((PAIRS * 8, ROWS), 0), iota((PAIRS * 8, ROWS), 1)
    slot = target % 8
    here = row == 2 * (target // 8) + slot % 2
    own = dot(one_hot(here & (slot // 2 == 0)), keys)
    own = own + dot(one_hot(here & (slot // 2 == 1)), values)
    own = own + dot(one_hot(here & (slot // 2 == 2)), pieces)
    out_ref[:, 64:72, :] = own.reshape(PAIRS, 8, HD).astype(BF)


def attend_kernel(in_ref, kpos_ref, qpos_ref, qlow_ref, out_ref, keys, values, dkey, dvalue):
    extra = in_ref[:, 64:72, :].astype(F32).reshape(CTX * 8, HD).astype(BF)
    token, source = iota((CTX * 2, CTX * 8), 0), iota((CTX * 2, CTX * 8), 1)
    base = source == (token // 2) * 8 + token % 2

    def picked(offset):
        chosen = source == (token // 2) * 8 + token % 2 + offset
        return dot(one_hot(chosen), extra).astype(BF)

    keys[0:KH, :] = in_ref[:, 32:48, :].reshape(KH, HD)
    keys[KH:KN, :] = picked(0)
    values[0:KH, 0:HD] = in_ref[:, 48:64, :].reshape(KH, HD)
    values[KH:KN, 0:HD] = picked(2)
    values[:, HD : 2 * HD] = one_hot(iota((KN, HD), 1) < 24)
    delta = picked(4)
    kpos = jnp.broadcast_to(kpos_ref[...], (HD, KN)).T
    key_columns = keys[...].astype(F32).T.astype(BF)
    count = 256
    for c in range(QN // count):
        first = c * (count // 16)
        qc = in_ref[first : first + count // 16, 0:16, :].reshape(count, HD)
        gc = in_ref[first : first + count // 16, 16:32, :].reshape(count, HD)
        row, col = iota((count, HD), 0), iota((count, HD), 1)
        spread = dot(one_hot(col == c * (count // HEADS) + row // HEADS), delta)
        spread = jnp.where(col % HEADS == row % HEADS, spread, 0.0).astype(BF)
        scores = dot_t(keys[...], qc)
        at = slice(c * count, (c + 1) * count)
        qpos, qlow = qpos_ref[:, at], qlow_ref[:, at]
        kp = jnp.concatenate([kpos, kpos], axis=1)
        scores = jnp.where((kp <= qpos) & (kp >= qlow), scores, NEG)
        top = jnp.max(scores, axis=0, keepdims=True)
        probs = jnp.exp2((scores - top) * (SCALE * LOG2E))
        probs = probs * (1.0 / jnp.sum(probs, axis=0, keepdims=True))
        change = dot_t(values[...], jnp.concatenate([gc, spread], axis=1))
        sgrad = (probs * change).astype(BF)
        value_part = dot(probs.astype(BF), gc)
        key_part = dot(sgrad, qc)
        if c == 0:
            dvalue[...] = value_part
            dkey[...] = key_part
        else:
            dvalue[...] += value_part
            dkey[...] += key_part
        qgrad = (dot(key_columns, sgrad) * SCALE).T
        out_ref[first : first + count // 16, 0:16, :] = qgrad.reshape(count // 16, 16, HD).astype(BF)
    out_ref[:, 16:32, :] = (dkey[0:KH, :] * SCALE).reshape(CTX, HALO, HD).astype(BF)
    out_ref[:, 32:48, :] = dvalue[0:KH, :].reshape(CTX, HALO, HD).astype(BF)
    source, token = iota((CTX * 8, CTX * 2), 0), iota((CTX * 8, CTX * 2), 1)
    home = (token // 2) * 8 + token % 2
    own = dot(one_hot(source == home), (dkey[KH:KN, :] * SCALE).astype(BF))
    own = own + dot(one_hot(source == home + 2), dvalue[KH:KN, :].astype(BF))
    out_ref[:, 48:56, :] = own.reshape(CTX, 8, HD).astype(BF)


def collect_kernel(in_ref, q_ref, kv_ref, split):
    row, source = iota((ROWS, PAIRS * HALO), 0), iota((ROWS, PAIRS * HALO), 1)
    window = one_hot(row == 2 * (source // HALO) + source % HALO - HALO)
    row, source = iota((ROWS, PAIRS * 8), 0), iota((ROWS, PAIRS * 8), 1)
    slot = source % 8
    here = row == 2 * (source // 8) + slot % 2
    for s in range(2):
        mine = slice(s * PAIRS, (s + 1) * PAIRS)
        extra = in_ref[mine, 48:56, :].astype(F32).reshape(PAIRS * 8, HD).astype(BF)
        for part in range(2):
            halo = in_ref[mine, 16 + 16 * part : 32 + 16 * part, :].reshape(PAIRS * HALO, HD)
            total = dot(window, halo) + dot(one_hot(here & (slot // 2 == part)), extra)
            for copy in range(4):
                kv_ref[copy, part, s * ROWS : (s + 1) * ROWS] = total.astype(BF)
        split[...] = in_ref[mine, 0:16, :].astype(F32).reshape(PAIRS * 16, HD)
        for h in range(HEADS):
            q_ref[s, :, h * HD : (h + 1) * HD] = split[pl.ds(h, ROWS, stride=HEADS), :].astype(BF)


def whole(shape):
    return pl.BlockSpec(shape, lambda *_: (0,) * len(shape))


def local(
    layer_input, queries, key_states, value_states, attn_output, out_grad, doc_ids, positions
):
    ctx = ("x", "zl", "y")
    index = lax.axis_index(ctx)
    sequence, pair = index // PAIRS, index % PAIRS

    quarter = layer_input.shape[2] // 4
    x_at, core = lax.axis_index("x"), lax.axis_index("core")
    flat_input = layer_input.reshape(2 * ROWS, 4 * quarter)
    columns = []
    for step in range(4):
        piece = lax.dynamic_slice_in_dim(flat_input, (x_at + step) % 4 * quarter, quarter, 1)
        if step:
            piece = lax.ppermute(piece, "x", [(i, (i + step) % 4) for i in range(4)])
        columns.append(piece)

    row_spec = lambda width: pl.BlockSpec((1, ROWS, width), lambda s: (s, 0, 0))
    sent = pl.pallas_call(
        pack_kernel,
        out_shape=jax.ShapeDtypeStruct((CTX, SEND, HD), BF),
        grid=(2,),
        in_specs=[row_spec(1024), row_spec(1024), row_spec(1024), row_spec(HD), row_spec(HD)],
        out_specs=pl.BlockSpec((PAIRS, SEND, HD), lambda s: (s, 0, 0)),
        scratch_shapes=[pltpu.VMEM((ROWS * HEADS, HD), F32)],
        name="pack",
    )(queries, out_grad, attn_output, key_states, value_states)
    arrived = lax.all_to_all(sent, ctx, 0, 0, tiled=True)
    arrived, *columns = lax.optimization_barrier((arrived, *columns))

    docs = lax.dynamic_index_in_dim(doc_ids, sequence, 0, keepdims=False)
    places = lax.dynamic_index_in_dim(positions, sequence, 0, keepdims=False).reshape(CTX, ROWS)
    places = jnp.pad(places, ((0, 0), (HALO, 0)), constant_values=FAR)
    places = lax.dynamic_slice_in_dim(places, 2 * pair, HALO + 2, 1)
    own = places[:, HALO:].reshape(CTX * 2)
    kpos = jnp.concatenate([places[:, :HALO].reshape(KH), own])[None, :]
    starts = jnp.sum(docs[None, :] < jnp.arange(16)[:, None], axis=1)
    low = jnp.max(jnp.where(starts[:, None] <= own[None, :], starts[:, None], 0), axis=0)
    qpos = jnp.repeat(own, HEADS)[None, :]
    qlow = jnp.repeat(low, HEADS)[None, :]

    back = pl.pallas_call(
        attend_kernel,
        out_shape=jax.ShapeDtypeStruct((CTX, BACK, HD), BF),
        grid=(1,),
        in_specs=[whole((CTX, SEND, HD)), whole((1, KN)), whole((1, QN)), whole((1, QN))],
        out_specs=whole((CTX, BACK, HD)),
        scratch_shapes=[
            pltpu.VMEM((KN, HD), BF),
            pltpu.VMEM((KN, 2 * HD), BF),
            pltpu.VMEM((KN, HD), F32),
            pltpu.VMEM((KN, HD), F32),
        ],
        compiler_params=pltpu.CompilerParams(vmem_limit_bytes=48 << 20),
        name="attend",
    )(arrived, kpos.astype(F32), qpos.astype(F32), qlow.astype(F32))
    home = lax.all_to_all(back, ctx, 0, 0, tiled=True)
    twin = lax.ppermute(jnp.stack(columns), "core", [(0, 1), (1, 0)])
    home, twin = lax.optimization_barrier((home, twin))

    query_grad, kv_grad = pl.pallas_call(
        collect_kernel,
        out_shape=(
            jax.ShapeDtypeStruct((2, ROWS, HEADS * HD), BF),
            jax.ShapeDtypeStruct((4, 2, 2 * ROWS, HD), BF),
        ),
        grid=(1,),
        in_specs=[whole((CTX, BACK, HD))],
        out_specs=(whole((2, ROWS, HEADS * HD)), whole((4, 2, 2 * ROWS, HD))),
        scratch_shapes=[pltpu.VMEM((PAIRS * 16, HD), F32)],
        name="collect",
    )(home)

    grads = lax.all_to_all(
        kv_grad.reshape(8, 2 * ROWS, HD), ("x", "core"), 0, 0, tiled=True
    )
    part = jnp.zeros((quarter, HD), F32)
    for step in range(4):
        for piece, at in ((columns[step], core), (twin[step], 1 - core)):
            grad = lax.dynamic_index_in_dim(
                grads, (x_at - step) % 4 * 2 + at, 0, keepdims=False
            )
            part = part + lax.dot_general(
                piece, grad, (((0,), (0,)), ((), ())), preferred_element_type=F32
            )
    part = part.reshape(16, 64, HD).astype(BF)
    part = lax.all_to_all(part, ("zl", "y"), 0, 0, tiled=True)
    part = jnp.sum(part.astype(F32), axis=0).astype(BF)
    part = lax.all_to_all(jnp.broadcast_to(part[None], (4, 64, HD)), "zh", 0, 0, tiled=True)
    part = jnp.sum(part.astype(F32), axis=0)
    weight_grad = lax.all_gather(part, "core", axis=1, tiled=True)
    return (query_grad, weight_grad)


def solution(mesh):
    devices = mesh.devices.reshape(4, 4, 4, -1, 2)
    inner = Mesh(devices, ("x", "zl", "y", "zh", "core"))
    ctx, dp = ("x", "zl", "y"), ("zh", "core")
    rows = P(dp, ctx, None)
    whole_rows = P(dp, None)
    return jax.shard_map(
        local,
        mesh=inner,
        in_specs=(rows,) * 6 + (whole_rows,) * 2,
        out_specs=(rows, P(ctx, None)),
        check_vma=False,
    )
```

```python
import math

import jax
import jax.numpy as jnp
from jax import lax
from jax.experimental import pallas as pl
from jax.experimental.pallas import tpu as pltpu
from jax.sharding import Mesh
from jax.sharding import PartitionSpec as P

BF = jnp.bfloat16
F32 = jnp.float32
HEADS = 8
HD = 128
ROWS = 64
PEERS = 32
OWN = 4
GROUPS = ROWS // OWN
HALO = 16
SEND = 152
BACK = 112
TOKENS = PEERS * OWN
QN = TOKENS * HEADS
KH = PEERS * HALO
KN = 2 * KH + 2 * TOKENS
NEG = -1e30
FAR = 1 << 20
SCALE = 1.0 / math.sqrt(HD)
LOG2E = math.log2(math.e)


def iota(shape, dim):
    return lax.broadcasted_iota(jnp.int32, shape, dim)


def one_hot(condition):
    return jnp.where(condition, 1.0, 0.0).astype(BF)


def dot(a, b):
    return lax.dot_general(a, b, (((1,), (0,)), ((), ())), preferred_element_type=F32)


def dot_t(a, b):
    return lax.dot_general(a, b, (((1,), (1,)), ((), ())), preferred_element_type=F32)


def window_rows(keys, values):
    target, row = iota((GROUPS * HALO, ROWS), 0), iota((GROUPS * HALO, ROWS), 1)
    window = one_hot(row == OWN * (target // HALO) + target % HALO - HALO)
    target, row = iota((GROUPS * 8, ROWS), 0), iota((GROUPS * 8, ROWS), 1)
    here = row == OWN * (target // 8) + target % OWN
    own = dot(one_hot(here & (target % 8 < OWN)), keys)
    own = own + dot(one_hot(here & (target % 8 >= OWN)), values)
    return (
        dot(window, keys).reshape(GROUPS, HALO, HD).astype(BF),
        dot(window, values).reshape(GROUPS, HALO, HD).astype(BF),
        own.reshape(GROUPS, 8, HD).astype(BF),
    )


def pack_kernel(q_ref, g_ref, o_ref, k_ref, v_ref, out_ref, split):
    def heads_to_rows(ref, at):
        wide = ref[0].astype(F32)
        for h in range(HEADS):
            split[pl.ds(h, ROWS, stride=HEADS), :] = wide[:, h * HD : (h + 1) * HD]
        out_ref[:, at : at + 32, :] = split[...].reshape(GROUPS, 32, HD).astype(BF)

    heads_to_rows(q_ref, 0)
    heads_to_rows(g_ref, 32)
    product = g_ref[0].astype(F32) * o_ref[0].astype(F32)
    lane = iota((ROWS, HD), 1)
    delta = jnp.zeros((ROWS, HD), F32)
    for h in range(HEADS):
        total = jnp.sum(product[:, h * HD : (h + 1) * HD], axis=1, keepdims=True)
        delta = jnp.where(lane % HEADS == h, total, delta)
    high = delta.astype(BF).astype(F32)
    rest = delta - high
    middle = rest.astype(BF).astype(F32)
    low = rest - middle
    pieces = jnp.where(lane < 8, high, jnp.where(lane < 16, middle, low))
    pieces = jnp.where(lane < 24, -pieces, 0.0).astype(BF)
    out_ref[:, 64:80, :], out_ref[:, 80:96, :], out_ref[:, 96:104, :] = window_rows(
        k_ref[0], v_ref[0]
    )
    target, row = iota((GROUPS * 8, ROWS), 0), iota((GROUPS * 8, ROWS), 1)
    here = (row == OWN * (target // 8) + target % OWN) & (target % 8 < OWN)
    out_ref[:, 104:112, :] = dot(one_hot(here), pieces).reshape(GROUPS, 8, HD).astype(BF)


def pack_other_kernel(kv_ref, in_ref, out_ref, block, sem):
    for s in range(2):
        to = slice(s * GROUPS, (s + 1) * GROUPS)
        block[to, 0:16, :], block[to, 16:32, :], block[to, 32:40, :] = window_rows(
            kv_ref[s, :, 0:HD], kv_ref[s, :, HD : 2 * HD]
        )
    copy = pltpu.make_async_copy(block, out_ref.at[:, 112:152, :], sem)
    copy.start()
    copy.wait()


def attend_kernel(in_ref, kpos_ref, qpos_ref, qlow_ref, out_ref, keys, values, dkey, dvalue):
    token, source = iota((TOKENS, PEERS * 8), 0), iota((TOKENS, PEERS * 8), 1)
    home = token // OWN * 8 + token % OWN

    def picked(row, offset):
        extra = in_ref[:, row : row + 8, :].astype(F32).reshape(PEERS * 8, HD).astype(BF)
        return dot(one_hot(source == home + offset), extra).astype(BF)

    for half, (halo, own) in enumerate(((64, 96), (112, 144))):
        to = slice(half * KH, (half + 1) * KH)
        keys[to, :] = in_ref[:, halo : halo + 16, :].reshape(KH, HD)
        values[to, 0:HD] = in_ref[:, halo + 16 : halo + 32, :].reshape(KH, HD)
        to = slice(2 * KH + half * TOKENS, 2 * KH + (half + 1) * TOKENS)
        keys[to, :] = picked(own, 0)
        values[to, 0:HD] = picked(own, OWN)
    values[:, HD : 2 * HD] = one_hot(iota((KN, HD), 1) < 24)
    delta = picked(104, 0)
    kpos = jnp.broadcast_to(kpos_ref[...], (HD, KN)).T
    kpos = jnp.concatenate([kpos, kpos], axis=1)
    key_columns = keys[...].astype(F32).T.astype(BF)
    count = 256
    srcs = count // (OWN * HEADS)
    for c in range(QN // count):
        first = c * srcs
        qc = in_ref[first : first + srcs, 0:32, :].reshape(count, HD)
        gc = in_ref[first : first + srcs, 32:64, :].reshape(count, HD)
        row, col = iota((count, HD), 0), iota((count, HD), 1)
        spread = dot(one_hot(col == c * (count // HEADS) + row // HEADS), delta)
        spread = jnp.where(col % HEADS == row % HEADS, spread, 0.0).astype(BF)
        scores = dot_t(keys[...], qc)
        at = slice(c * count, (c + 1) * count)
        scores = jnp.where((kpos <= qpos_ref[:, at]) & (kpos >= qlow_ref[:, at]), scores, NEG)
        top = jnp.max(scores, axis=0, keepdims=True)
        probs = jnp.exp2((scores - top) * (SCALE * LOG2E))
        probs = probs * (1.0 / jnp.sum(probs, axis=0, keepdims=True))
        change = dot_t(values[...], jnp.concatenate([gc, spread], axis=1))
        sgrad = (probs * change).astype(BF)
        value_part = dot(probs.astype(BF), gc)
        key_part = dot(sgrad, qc)
        if c == 0:
            dvalue[...] = value_part
            dkey[...] = key_part
        else:
            dvalue[...] += value_part
            dkey[...] += key_part
        qgrad = (dot(key_columns, sgrad) * SCALE).T
        out_ref[first : first + srcs, 0:32, :] = qgrad.reshape(srcs, 32, HD).astype(BF)
    source, token = iota((PEERS * 8, TOKENS), 0), iota((PEERS * 8, TOKENS), 1)
    home = token // OWN * 8 + token % OWN
    for half in range(2):
        at = slice(half * KH, (half + 1) * KH)
        halo = 32 + 32 * half
        out_ref[:, halo : halo + 16, :] = (dkey[at, :] * SCALE).reshape(PEERS, HALO, HD).astype(BF)
        out_ref[:, halo + 16 : halo + 32, :] = dvalue[at, :].reshape(PEERS, HALO, HD).astype(BF)
        at = slice(2 * KH + half * TOKENS, 2 * KH + (half + 1) * TOKENS)
        own = dot(one_hot(source == home), (dkey[at, :] * SCALE).astype(BF))
        own = own + dot(one_hot(source == home + OWN), dvalue[at, :].astype(BF))
        own = own.reshape(PEERS, 8, HD).astype(BF)
        out_ref[:, 96 + 8 * half : 104 + 8 * half, :] = own


def collect_kernel(half_ref, in_ref, q_ref, kv_ref, split):
    row, source = iota((ROWS, GROUPS * HALO), 0), iota((ROWS, GROUPS * HALO), 1)
    window = one_hot(row == OWN * (source // HALO) + source % HALO - HALO)
    row, source = iota((ROWS, GROUPS * 8), 0), iota((ROWS, GROUPS * 8), 1)
    here = row == OWN * (source // 8) + source % OWN
    for s in range(2):
        mine = slice(s * GROUPS, (s + 1) * GROUPS)
        for half in range(2):
            slot = half_ref[0] if half == 0 else 1 - half_ref[0]
            extra = in_ref[mine, 96 + 8 * half : 104 + 8 * half, :]
            extra = extra.astype(F32).reshape(GROUPS * 8, HD).astype(BF)
            for part in range(2):
                at = 32 + 32 * half + 16 * part
                halo = in_ref[mine, at : at + 16, :].reshape(GROUPS * HALO, HD)
                total = dot(window, halo)
                total = total + dot(one_hot(here & (source % 8 // OWN == part)), extra)
                for copy in range(4):
                    kv_ref[copy, slot, part, s * ROWS : (s + 1) * ROWS] = total.astype(BF)
        split[...] = in_ref[mine, 0:32, :].astype(F32).reshape(GROUPS * 32, HD)
        for h in range(HEADS):
            q_ref[s, :, h * HD : (h + 1) * HD] = split[pl.ds(h, ROWS, stride=HEADS), :].astype(BF)


def whole(shape):
    return pl.BlockSpec(shape, lambda *_: (0,) * len(shape))


def local(
    layer_input, queries, key_states, value_states, attn_output, out_grad, doc_ids, positions
):
    peers = ("x", "zd", "y")
    index = lax.axis_index(peers)
    half = lax.axis_index("zu")
    sequence, group = index // GROUPS, index % GROUPS

    quarter = layer_input.shape[2] // 4
    x_at, core = lax.axis_index("x"), lax.axis_index("core")
    flat_input = layer_input.reshape(2 * ROWS, 4 * quarter)
    columns = []
    for step in range(4):
        piece = lax.dynamic_slice_in_dim(flat_input, (x_at + step) % 4 * quarter, quarter, 1)
        if step:
            piece = lax.ppermute(piece, "x", [(i, (i + step) % 4) for i in range(4)])
        columns.append(piece)

    row_spec = lambda width: pl.BlockSpec((1, ROWS, width), lambda s: (s, 0, 0))
    other = lax.ppermute(
        jnp.concatenate([key_states, value_states], axis=2), "zu", [(0, 1), (1, 0)]
    )
    sent = pl.pallas_call(
        pack_kernel,
        out_shape=jax.ShapeDtypeStruct((PEERS, SEND, HD), BF),
        grid=(2,),
        in_specs=[row_spec(1024), row_spec(1024), row_spec(1024), row_spec(HD), row_spec(HD)],
        out_specs=pl.BlockSpec((GROUPS, SEND, HD), lambda s: (s, 0, 0)),
        scratch_shapes=[pltpu.VMEM((ROWS * HEADS, HD), F32)],
        name="pack",
    )(queries, out_grad, attn_output, key_states, value_states)
    hbm = pl.BlockSpec(memory_space=pltpu.HBM)
    sent = pl.pallas_call(
        pack_other_kernel,
        out_shape=jax.ShapeDtypeStruct((PEERS, SEND, HD), BF),
        in_specs=[whole((2, ROWS, 2 * HD)), hbm],
        out_specs=hbm,
        scratch_shapes=[pltpu.VMEM((PEERS, 40, HD), BF), pltpu.SemaphoreType.DMA(())],
        input_output_aliases={1: 0},
        grid=(1,),
        compiler_params=pltpu.CompilerParams(vmem_limit_bytes=32 << 20),
        name="pack_other",
    )(other, sent)
    arrived = lax.all_to_all(sent, peers, 0, 0, tiled=True)
    arrived, *columns = lax.optimization_barrier((arrived, *columns))

    docs = lax.dynamic_index_in_dim(doc_ids, sequence, 0, keepdims=False)
    places = lax.dynamic_index_in_dim(positions, sequence, 0, keepdims=False)
    places = places.reshape(4, 2, 8, ROWS)
    places = jnp.pad(places, ((0, 0), (0, 0), (0, 0), (HALO, 0)), constant_values=FAR)
    places = lax.dynamic_slice_in_dim(places, OWN * group, HALO + OWN, 3)
    near = lax.dynamic_index_in_dim(places, half, 1, keepdims=False)
    far = lax.dynamic_index_in_dim(places, 1 - half, 1, keepdims=False)
    own = near[:, :, HALO:].reshape(TOKENS)
    kpos = [near[:, :, :HALO].reshape(KH), far[:, :, :HALO].reshape(KH)]
    kpos = jnp.concatenate(kpos + [own, far[:, :, HALO:].reshape(TOKENS)])[None, :]
    starts = jnp.sum(docs[None, :] < jnp.arange(16)[:, None], axis=1)
    low = jnp.max(jnp.where(starts[:, None] <= own[None, :], starts[:, None], 0), axis=0)
    qpos = jnp.repeat(own, HEADS)[None, :]
    qlow = jnp.repeat(low, HEADS)[None, :]

    back = pl.pallas_call(
        attend_kernel,
        out_shape=jax.ShapeDtypeStruct((PEERS, BACK, HD), BF),
        grid=(1,),
        in_specs=[whole((PEERS, SEND, HD)), whole((1, KN)), whole((1, QN)), whole((1, QN))],
        out_specs=whole((PEERS, BACK, HD)),
        scratch_shapes=[
            pltpu.VMEM((KN, HD), BF),
            pltpu.VMEM((KN, 2 * HD), BF),
            pltpu.VMEM((KN, HD), F32),
            pltpu.VMEM((KN, HD), F32),
        ],
        compiler_params=pltpu.CompilerParams(vmem_limit_bytes=48 << 20),
        name="attend",
    )(arrived, kpos.astype(F32), qpos.astype(F32), qlow.astype(F32))
    home = lax.all_to_all(back, peers, 0, 0, tiled=True)
    twin = lax.ppermute(jnp.stack(columns), "core", [(0, 1), (1, 0)])
    home, twin = lax.optimization_barrier((home, twin))

    query_grad, kv_grad = pl.pallas_call(
        collect_kernel,
        out_shape=(
            jax.ShapeDtypeStruct((2, ROWS, HEADS * HD), BF),
            jax.ShapeDtypeStruct((4, 2, 2, 2 * ROWS, HD), BF),
        ),
        grid=(1,),
        in_specs=[pl.BlockSpec(memory_space=pltpu.SMEM), whole((PEERS, BACK, HD))],
        out_specs=(whole((2, ROWS, HEADS * HD)), whole((4, 2, 2, 2 * ROWS, HD))),
        scratch_shapes=[pltpu.VMEM((GROUPS * 32, HD), F32)],
        compiler_params=pltpu.CompilerParams(vmem_limit_bytes=32 << 20),
        name="collect",
    )(half[None], home)

    grads = lax.all_to_all(
        kv_grad.reshape(16, 2 * ROWS, HD), ("x", "zu", "core"), 0, 0, tiled=True
    )
    grads = jnp.sum(grads.reshape(4, 2, 2, 2 * ROWS, HD).astype(F32), axis=1).astype(BF)
    grads = grads.reshape(8, 2 * ROWS, HD)
    part = jnp.zeros((quarter, HD), F32)
    for step in range(4):
        for piece, at in ((columns[step], core), (twin[step], 1 - core)):
            grad = lax.dynamic_index_in_dim(
                grads, (x_at - step) % 4 * 2 + at, 0, keepdims=False
            )
            part = part + lax.dot_general(
                piece, grad, (((0,), (0,)), ((), ())), preferred_element_type=F32
            )
    part = part.reshape(16, 64, HD).astype(BF)
    part = lax.all_to_all(part, ("zu", "zd", "y"), 0, 0, tiled=True)
    part = jnp.sum(part.astype(F32), axis=0).astype(BF)
    part = lax.all_to_all(jnp.broadcast_to(part[None], (4, 64, HD)), "zh", 0, 0, tiled=True)
    part = jnp.sum(part.astype(F32), axis=0)
    weight_grad = lax.all_gather(part, "core", axis=1, tiled=True)
    return (query_grad, weight_grad)


def solution(mesh):
    devices = mesh.devices.reshape(4, 2, 2, 4, -1, 2)
    inner = Mesh(devices, ("x", "zu", "zd", "y", "zh", "core"))
    ctx, dp = ("x", "zu", "zd", "y"), ("zh", "core")
    rows = P(dp, ctx, None)
    whole_rows = P(dp, None)
    return jax.shard_map(
        local,
        mesh=inner,
        in_specs=(rows,) * 6 + (whole_rows,) * 2,
        out_specs=(rows, P(ctx, None)),
        check_vma=False,
    )
```

```python
import math

import jax
import jax.numpy as jnp
from jax import lax
from jax.experimental import pallas as pl
from jax.experimental.pallas import tpu as pltpu
from jax.sharding import Mesh
from jax.sharding import PartitionSpec as P

BF = jnp.bfloat16
F32 = jnp.float32
HEADS = 8
HD = 128
ROWS = 64
PEERS = 32
OWN = 4
GROUPS = ROWS // OWN
HALO = 16
SEND = 152
BACK = 112
TOKENS = PEERS * OWN
QN = TOKENS * HEADS
KH = PEERS * HALO
KN = 2 * KH + 2 * TOKENS
NEG = -1e30
FAR = 1 << 20
SCALE = 1.0 / math.sqrt(HD)
LOG2E = math.log2(math.e)


def iota(shape, dim):
    return lax.broadcasted_iota(jnp.int32, shape, dim)


def one_hot(condition):
    return jnp.where(condition, 1.0, 0.0).astype(BF)


def dot(a, b):
    return lax.dot_general(a, b, (((1,), (0,)), ((), ())), preferred_element_type=F32)


def dot_t(a, b):
    return lax.dot_general(a, b, (((1,), (1,)), ((), ())), preferred_element_type=F32)


def window_rows(keys, values):
    target, row = iota((GROUPS * HALO, ROWS), 0), iota((GROUPS * HALO, ROWS), 1)
    window = one_hot(row == OWN * (target // HALO) + target % HALO - HALO)
    target, row = iota((GROUPS * 8, ROWS), 0), iota((GROUPS * 8, ROWS), 1)
    here = row == OWN * (target // 8) + target % OWN
    own = dot(one_hot(here & (target % 8 < OWN)), keys)
    own = own + dot(one_hot(here & (target % 8 >= OWN)), values)
    return (
        dot(window, keys).reshape(GROUPS, HALO, HD).astype(BF),
        dot(window, values).reshape(GROUPS, HALO, HD).astype(BF),
        own.reshape(GROUPS, 8, HD).astype(BF),
    )


def pack_kernel(q_ref, g_ref, o_ref, k_ref, v_ref, out_ref, split):
    def heads_to_rows(ref, at):
        wide = ref[0].astype(F32)
        for h in range(HEADS):
            split[pl.ds(h, ROWS, stride=HEADS), :] = wide[:, h * HD : (h + 1) * HD]
        out_ref[:, at : at + 32, :] = split[...].reshape(GROUPS, 32, HD).astype(BF)

    heads_to_rows(q_ref, 0)
    heads_to_rows(g_ref, 32)
    product = g_ref[0].astype(F32) * o_ref[0].astype(F32)
    lane = iota((ROWS, HD), 1)
    delta = jnp.zeros((ROWS, HD), F32)
    for h in range(HEADS):
        total = jnp.sum(product[:, h * HD : (h + 1) * HD], axis=1, keepdims=True)
        delta = jnp.where(lane % HEADS == h, total, delta)
    high = delta.astype(BF).astype(F32)
    rest = delta - high
    middle = rest.astype(BF).astype(F32)
    low = rest - middle
    pieces = jnp.where(lane < 8, high, jnp.where(lane < 16, middle, low))
    pieces = jnp.where(lane < 24, -pieces, 0.0).astype(BF)
    out_ref[:, 64:80, :], out_ref[:, 80:96, :], out_ref[:, 96:104, :] = window_rows(
        k_ref[0], v_ref[0]
    )
    target, row = iota((GROUPS * 8, ROWS), 0), iota((GROUPS * 8, ROWS), 1)
    here = (row == OWN * (target // 8) + target % OWN) & (target % 8 < OWN)
    out_ref[:, 104:112, :] = dot(one_hot(here), pieces).reshape(GROUPS, 8, HD).astype(BF)


def pack_other_kernel(kv_ref, in_ref, out_ref, block, sem):
    for s in range(2):
        to = slice(s * GROUPS, (s + 1) * GROUPS)
        block[to, 0:16, :], block[to, 16:32, :], block[to, 32:40, :] = window_rows(
            kv_ref[s, :, 0:HD], kv_ref[s, :, HD : 2 * HD]
        )
    copy = pltpu.make_async_copy(block, out_ref.at[:, 112:152, :], sem)
    copy.start()
    copy.wait()


def attend_kernel(in_ref, kpos_ref, qpos_ref, qlow_ref, out_ref, keys, values, dkey, dvalue):
    token, source = iota((TOKENS, PEERS * 8), 0), iota((TOKENS, PEERS * 8), 1)
    home = token // OWN * 8 + token % OWN

    def picked(row, offset):
        extra = in_ref[:, row : row + 8, :].astype(F32).reshape(PEERS * 8, HD).astype(BF)
        return dot(one_hot(source == home + offset), extra).astype(BF)

    for half, (halo, own) in enumerate(((64, 96), (112, 144))):
        to = slice(half * KH, (half + 1) * KH)
        keys[to, :] = in_ref[:, halo : halo + 16, :].reshape(KH, HD)
        values[to, 0:HD] = in_ref[:, halo + 16 : halo + 32, :].reshape(KH, HD)
        to = slice(2 * KH + half * TOKENS, 2 * KH + (half + 1) * TOKENS)
        keys[to, :] = picked(own, 0)
        values[to, 0:HD] = picked(own, OWN)
    values[:, HD : 2 * HD] = one_hot(iota((KN, HD), 1) < 24)
    delta = picked(104, 0)
    kpos = jnp.broadcast_to(kpos_ref[...], (HD, KN)).T
    kpos = jnp.concatenate([kpos, kpos], axis=1)
    key_columns = keys[...].astype(F32).T.astype(BF)
    count = 256
    srcs = count // (OWN * HEADS)
    for c in range(QN // count):
        first = c * srcs
        qc = in_ref[first : first + srcs, 0:32, :].reshape(count, HD)
        gc = in_ref[first : first + srcs, 32:64, :].reshape(count, HD)
        row, col = iota((count, HD), 0), iota((count, HD), 1)
        spread = dot(one_hot(col == c * (count // HEADS) + row // HEADS), delta)
        spread = jnp.where(col % HEADS == row % HEADS, spread, 0.0).astype(BF)
        scores = dot_t(keys[...], qc)
        at = slice(c * count, (c + 1) * count)
        scores = jnp.where((kpos <= qpos_ref[:, at]) & (kpos >= qlow_ref[:, at]), scores, NEG)
        top = jnp.max(scores, axis=0, keepdims=True)
        probs = jnp.exp2((scores - top) * (SCALE * LOG2E))
        probs = probs * (1.0 / jnp.sum(probs, axis=0, keepdims=True))
        change = dot_t(values[...], jnp.concatenate([gc, spread], axis=1))
        sgrad = (probs * change).astype(BF)
        value_part = dot(probs.astype(BF), gc)
        key_part = dot(sgrad, qc)
        if c == 0:
            dvalue[...] = value_part
            dkey[...] = key_part
        else:
            dvalue[...] += value_part
            dkey[...] += key_part
        qgrad = (dot(key_columns, sgrad) * SCALE).T
        out_ref[first : first + srcs, 0:32, :] = qgrad.reshape(srcs, 32, HD).astype(BF)
    source, token = iota((PEERS * 8, TOKENS), 0), iota((PEERS * 8, TOKENS), 1)
    home = token // OWN * 8 + token % OWN
    for half in range(2):
        at = slice(half * KH, (half + 1) * KH)
        halo = 32 + 32 * half
        out_ref[:, halo : halo + 16, :] = (dkey[at, :] * SCALE).reshape(PEERS, HALO, HD).astype(BF)
        out_ref[:, halo + 16 : halo + 32, :] = dvalue[at, :].reshape(PEERS, HALO, HD).astype(BF)
        at = slice(2 * KH + half * TOKENS, 2 * KH + (half + 1) * TOKENS)
        own = dot(one_hot(source == home), (dkey[at, :] * SCALE).astype(BF))
        own = own + dot(one_hot(source == home + OWN), dvalue[at, :].astype(BF))
        own = own.reshape(PEERS, 8, HD).astype(BF)
        out_ref[:, 96 + 8 * half : 104 + 8 * half, :] = own


def collect_kernel(in_ref, q_ref, near_ref, far_ref, split):
    row, source = iota((ROWS, GROUPS * HALO), 0), iota((ROWS, GROUPS * HALO), 1)
    window = one_hot(row == OWN * (source // HALO) + source % HALO - HALO)
    row, source = iota((ROWS, GROUPS * 8), 0), iota((ROWS, GROUPS * 8), 1)
    here = row == OWN * (source // 8) + source % OWN
    for s in range(2):
        mine = slice(s * GROUPS, (s + 1) * GROUPS)
        for half in range(2):
            extra = in_ref[mine, 96 + 8 * half : 104 + 8 * half, :]
            extra = extra.astype(F32).reshape(GROUPS * 8, HD).astype(BF)
            for part in range(2):
                at = 32 + 32 * half + 16 * part
                halo = in_ref[mine, at : at + 16, :].reshape(GROUPS * HALO, HD)
                total = dot(window, halo)
                total = total + dot(one_hot(here & (source % 8 // OWN == part)), extra)
                to = near_ref if half == 0 else far_ref
                to[part, s * ROWS : (s + 1) * ROWS] = total.astype(to.dtype)
        split[...] = in_ref[mine, 0:32, :].astype(F32).reshape(GROUPS * 32, HD)
        for h in range(HEADS):
            q_ref[s, :, h * HD : (h + 1) * HD] = split[pl.ds(h, ROWS, stride=HEADS), :].astype(BF)


def whole(shape):
    return pl.BlockSpec(shape, lambda *_: (0,) * len(shape))


def local(
    layer_input, queries, key_states, value_states, attn_output, out_grad, doc_ids, positions
):
    peers = ("x", "zd", "y")
    index = lax.axis_index(peers)
    half = lax.axis_index("zu")
    sequence, group = index // GROUPS, index % GROUPS

    quarter = layer_input.shape[2] // 4
    x_at, core = lax.axis_index("x"), lax.axis_index("core")
    flat_input = layer_input.reshape(2 * ROWS, 4 * quarter)
    columns = [
        lax.dynamic_slice_in_dim(flat_input, (x_at + step) % 4 * quarter, quarter, 1)
        for step in range(4)
    ]

    def along_x(step):
        return lax.ppermute(columns[step], "x", [(i, (i + step) % 4) for i in range(4)])

    def other_core(x):
        return lax.ppermute(x, "core", [(0, 1), (1, 0)])

    columns[1], columns[3] = along_x(1), along_x(3)

    row_spec = lambda width: pl.BlockSpec((1, ROWS, width), lambda s: (s, 0, 0))
    other = lax.ppermute(
        jnp.concatenate([key_states, value_states], axis=2), "zu", [(0, 1), (1, 0)]
    )
    sent = pl.pallas_call(
        pack_kernel,
        out_shape=jax.ShapeDtypeStruct((PEERS, SEND, HD), BF),
        grid=(2,),
        in_specs=[row_spec(1024), row_spec(1024), row_spec(1024), row_spec(HD), row_spec(HD)],
        out_specs=pl.BlockSpec((GROUPS, SEND, HD), lambda s: (s, 0, 0)),
        scratch_shapes=[pltpu.VMEM((ROWS * HEADS, HD), F32)],
        name="pack",
    )(queries, out_grad, attn_output, key_states, value_states)
    hbm = pl.BlockSpec(memory_space=pl.ANY)
    sent = pl.pallas_call(
        pack_other_kernel,
        out_shape=jax.ShapeDtypeStruct((PEERS, SEND, HD), BF),
        in_specs=[pl.BlockSpec(memory_space=pltpu.VMEM), hbm],
        out_specs=hbm,
        scratch_shapes=[pltpu.VMEM((PEERS, 40, HD), BF), pltpu.SemaphoreType.DMA(())],
        input_output_aliases={1: 0},
        name="pack_other",
    )(other, sent)
    arrived = lax.all_to_all(sent, peers, 0, 0, tiled=True)
    arrived, *columns = lax.optimization_barrier((arrived, *columns))
    columns[2] = along_x(2)

    docs = lax.dynamic_index_in_dim(doc_ids, sequence, 0, keepdims=False)
    places = lax.dynamic_index_in_dim(positions, sequence, 0, keepdims=False)
    places = places.reshape(4, 2, 8, ROWS)
    places = jnp.pad(places, ((0, 0), (0, 0), (0, 0), (HALO, 0)), constant_values=FAR)
    places = lax.dynamic_slice_in_dim(places, OWN * group, HALO + OWN, 3)
    near = lax.dynamic_index_in_dim(places, half, 1, keepdims=False)
    far = lax.dynamic_index_in_dim(places, 1 - half, 1, keepdims=False)
    own = near[:, :, HALO:].reshape(TOKENS)
    kpos = [near[:, :, :HALO].reshape(KH), far[:, :, :HALO].reshape(KH)]
    kpos = jnp.concatenate(kpos + [own, far[:, :, HALO:].reshape(TOKENS)])[None, :]
    starts = jnp.sum(docs[None, :] < jnp.arange(16)[:, None], axis=1)
    low = jnp.max(jnp.where(starts[:, None] <= own[None, :], starts[:, None], 0), axis=0)
    qpos = jnp.repeat(own, HEADS)[None, :]
    qlow = jnp.repeat(low, HEADS)[None, :]

    back = pl.pallas_call(
        attend_kernel,
        out_shape=jax.ShapeDtypeStruct((PEERS, BACK, HD), BF),
        grid=(1,),
        in_specs=[whole((PEERS, SEND, HD)), whole((1, KN)), whole((1, QN)), whole((1, QN))],
        out_specs=whole((PEERS, BACK, HD)),
        scratch_shapes=[
            pltpu.VMEM((KN, HD), BF),
            pltpu.VMEM((KN, 2 * HD), BF),
            pltpu.VMEM((KN, HD), F32),
            pltpu.VMEM((KN, HD), F32),
        ],
        compiler_params=pltpu.CompilerParams(vmem_limit_bytes=48 << 20),
        name="attend",
    )(arrived, kpos.astype(F32), qpos.astype(F32), qlow.astype(F32))
    home = lax.all_to_all(back, peers, 0, 0, tiled=True)
    twin = other_core(jnp.stack([columns[0], columns[1], columns[3]]))
    home, twin, columns[2] = lax.optimization_barrier((home, twin, columns[2]))
    twin = [twin[0], twin[1], other_core(columns[2]), twin[2]]

    query_grad, near_grad, far_grad = pl.pallas_call(
        collect_kernel,
        out_shape=(
            jax.ShapeDtypeStruct((2, ROWS, HEADS * HD), BF),
            jax.ShapeDtypeStruct((2, 2 * ROWS, HD), F32),
            jax.ShapeDtypeStruct((2, 2 * ROWS, HD), BF),
        ),
        grid=(1,),
        in_specs=[whole((PEERS, BACK, HD))],
        out_specs=(
            whole((2, ROWS, HEADS * HD)),
            whole((2, 2 * ROWS, HD)),
            whole((2, 2 * ROWS, HD)),
        ),
        scratch_shapes=[pltpu.VMEM((GROUPS * 32, HD), F32)],
        compiler_params=pltpu.CompilerParams(vmem_limit_bytes=32 << 20),
        name="collect",
    )(home)
    kv_grad = (near_grad + lax.ppermute(far_grad, "zu", [(0, 1), (1, 0)])).astype(BF)

    kv_grad = jnp.broadcast_to(kv_grad[None], (4, 2, 2 * ROWS, HD))
    grads = lax.all_to_all(
        kv_grad.reshape(8, 2 * ROWS, HD), ("x", "core"), 0, 0, tiled=True
    )
    part = jnp.zeros((quarter, HD), F32)
    for step in range(4):
        for piece, at in ((columns[step], core), (twin[step], 1 - core)):
            grad = lax.dynamic_index_in_dim(
                grads, (x_at - step) % 4 * 2 + at, 0, keepdims=False
            )
            part = part + lax.dot_general(
                piece, grad, (((0,), (0,)), ((), ())), preferred_element_type=F32
            )
    part = part.reshape(16, 64, HD).astype(BF)
    part = lax.all_to_all(part, ("zu", "zd", "y"), 0, 0, tiled=True)
    part = jnp.sum(part.astype(F32), axis=0).astype(BF)
    part = lax.all_to_all(jnp.broadcast_to(part[None], (4, 64, HD)), "zh", 0, 0, tiled=True)
    part = jnp.sum(part.astype(F32), axis=0)
    weight_grad = lax.all_gather(part, "core", axis=1, tiled=True)
    return (query_grad, weight_grad)


def solution(mesh):
    devices = mesh.devices.reshape(4, 2, 2, 4, -1, 2)
    inner = Mesh(devices, ("x", "zu", "zd", "y", "zh", "core"))
    ctx, dp = ("x", "zu", "zd", "y"), ("zh", "core")
    rows = P(dp, ctx, None)
    whole_rows = P(dp, None)
    return jax.shard_map(
        local,
        mesh=inner,
        in_specs=(rows,) * 6 + (whole_rows,) * 2,
        out_specs=(rows, P(ctx, None)),
        check_vma=False,
    )
```

```python
import math

import jax
import jax.numpy as jnp
from jax import lax
from jax.experimental import pallas as pl
from jax.experimental.pallas import tpu as pltpu
from jax.sharding import Mesh
from jax.sharding import PartitionSpec as P

BF = jnp.bfloat16
F32 = jnp.float32
HEADS = 8
HD = 128
ROWS = 64
PEERS = 32
OWN = 4
GROUPS = ROWS // OWN
HALO = 16
SEND = 152
BACK = 112
TOKENS = PEERS * OWN
QN = TOKENS * HEADS
KH = PEERS * HALO
KN = 2 * KH + 2 * TOKENS
NEG = -1e30
FAR = 1 << 20
SCALE = 1.0 / math.sqrt(HD)
LOG2E = math.log2(math.e)


def iota(shape, dim):
    return lax.broadcasted_iota(jnp.int32, shape, dim)


def one_hot(condition):
    return jnp.where(condition, 1.0, 0.0).astype(BF)


def dot(a, b):
    return lax.dot_general(a, b, (((1,), (0,)), ((), ())), preferred_element_type=F32)


def dot_t(a, b):
    return lax.dot_general(a, b, (((1,), (1,)), ((), ())), preferred_element_type=F32)


def window_rows(keys, values):
    target, row = iota((GROUPS * HALO, ROWS), 0), iota((GROUPS * HALO, ROWS), 1)
    window = one_hot(row == OWN * (target // HALO) + target % HALO - HALO)
    target, row = iota((GROUPS * 8, ROWS), 0), iota((GROUPS * 8, ROWS), 1)
    here = row == OWN * (target // 8) + target % OWN
    own = dot(one_hot(here & (target % 8 < OWN)), keys)
    own = own + dot(one_hot(here & (target % 8 >= OWN)), values)
    return (
        dot(window, keys).reshape(GROUPS, HALO, HD).astype(BF),
        dot(window, values).reshape(GROUPS, HALO, HD).astype(BF),
        own.reshape(GROUPS, 8, HD).astype(BF),
    )


def pack_kernel(q_ref, g_ref, o_ref, k_ref, v_ref, out_ref, split):
    def heads_to_rows(ref, at):
        wide = ref[0].astype(F32)
        for h in range(HEADS):
            split[pl.ds(h, ROWS, stride=HEADS), :] = wide[:, h * HD : (h + 1) * HD]
        out_ref[:, at : at + 32, :] = split[...].reshape(GROUPS, 32, HD).astype(BF)

    heads_to_rows(q_ref, 0)
    heads_to_rows(g_ref, 32)
    product = g_ref[0].astype(F32) * o_ref[0].astype(F32)
    lane = iota((ROWS, HD), 1)
    delta = jnp.zeros((ROWS, HD), F32)
    for h in range(HEADS):
        total = jnp.sum(product[:, h * HD : (h + 1) * HD], axis=1, keepdims=True)
        delta = jnp.where(lane % HEADS == h, total, delta)
    high = delta.astype(BF).astype(F32)
    rest = delta - high
    middle = rest.astype(BF).astype(F32)
    low = rest - middle
    pieces = jnp.where(lane < 8, high, jnp.where(lane < 16, middle, low))
    pieces = jnp.where(lane < 24, -pieces, 0.0).astype(BF)
    out_ref[:, 64:80, :], out_ref[:, 80:96, :], out_ref[:, 96:104, :] = window_rows(
        k_ref[0], v_ref[0]
    )
    target, row = iota((GROUPS * 8, ROWS), 0), iota((GROUPS * 8, ROWS), 1)
    here = (row == OWN * (target // 8) + target % OWN) & (target % 8 < OWN)
    out_ref[:, 104:112, :] = dot(one_hot(here), pieces).reshape(GROUPS, 8, HD).astype(BF)


def pack_other_kernel(kv_ref, in_ref, out_ref, block, sem):
    for s in range(2):
        to = slice(s * GROUPS, (s + 1) * GROUPS)
        block[to, 0:16, :], block[to, 16:32, :], block[to, 32:40, :] = window_rows(
            kv_ref[s, :, 0:HD], kv_ref[s, :, HD : 2 * HD]
        )
    copy = pltpu.make_async_copy(block, out_ref.at[:, 112:152, :], sem)
    copy.start()
    copy.wait()


def attend_kernel(in_ref, kpos_ref, qpos_ref, qlow_ref, out_ref, keys, values, dkey, dvalue):
    token, source = iota((TOKENS, PEERS * 8), 0), iota((TOKENS, PEERS * 8), 1)
    home = token // OWN * 8 + token % OWN

    def picked(row, offset):
        extra = in_ref[:, row : row + 8, :].astype(F32).reshape(PEERS * 8, HD).astype(BF)
        return dot(one_hot(source == home + offset), extra).astype(BF)

    for half, (halo, own) in enumerate(((64, 96), (112, 144))):
        to = slice(half * KH, (half + 1) * KH)
        keys[to, :] = in_ref[:, halo : halo + 16, :].reshape(KH, HD)
        values[to, 0:HD] = in_ref[:, halo + 16 : halo + 32, :].reshape(KH, HD)
        to = slice(2 * KH + half * TOKENS, 2 * KH + (half + 1) * TOKENS)
        keys[to, :] = picked(own, 0)
        values[to, 0:HD] = picked(own, OWN)
    values[:, HD : 2 * HD] = one_hot(iota((KN, HD), 1) < 24)
    delta = picked(104, 0)
    kpos = jnp.broadcast_to(kpos_ref[...], (HD, KN)).T
    kpos = jnp.concatenate([kpos, kpos], axis=1)
    key_columns = keys[...].astype(F32).T.astype(BF)
    count = 256
    srcs = count // (OWN * HEADS)
    for c in range(QN // count):
        first = c * srcs
        qc = in_ref[first : first + srcs, 0:32, :].reshape(count, HD)
        gc = in_ref[first : first + srcs, 32:64, :].reshape(count, HD)
        row, col = iota((count, HD), 0), iota((count, HD), 1)
        spread = dot(one_hot(col == c * (count // HEADS) + row // HEADS), delta)
        spread = jnp.where(col % HEADS == row % HEADS, spread, 0.0).astype(BF)
        scores = dot_t(keys[...], qc)
        at = slice(c * count, (c + 1) * count)
        scores = jnp.where((kpos <= qpos_ref[:, at]) & (kpos >= qlow_ref[:, at]), scores, NEG)
        top = jnp.max(scores, axis=0, keepdims=True)
        probs = jnp.exp2((scores - top) * (SCALE * LOG2E))
        probs = probs * (1.0 / jnp.sum(probs, axis=0, keepdims=True))
        change = dot_t(values[...], jnp.concatenate([gc, spread], axis=1))
        sgrad = (probs * change).astype(BF)
        value_part = dot(probs.astype(BF), gc)
        key_part = dot(sgrad, qc)
        if c == 0:
            dvalue[...] = value_part
            dkey[...] = key_part
        else:
            dvalue[...] += value_part
            dkey[...] += key_part
        qgrad = (dot(key_columns, sgrad) * SCALE).T
        out_ref[first : first + srcs, 0:32, :] = qgrad.reshape(srcs, 32, HD).astype(BF)
    source, token = iota((PEERS * 8, TOKENS), 0), iota((PEERS * 8, TOKENS), 1)
    home = token // OWN * 8 + token % OWN
    for half in range(2):
        at = slice(half * KH, (half + 1) * KH)
        halo = 32 + 32 * half
        out_ref[:, halo : halo + 16, :] = (dkey[at, :] * SCALE).reshape(PEERS, HALO, HD).astype(BF)
        out_ref[:, halo + 16 : halo + 32, :] = dvalue[at, :].reshape(PEERS, HALO, HD).astype(BF)
        at = slice(2 * KH + half * TOKENS, 2 * KH + (half + 1) * TOKENS)
        own = dot(one_hot(source == home), (dkey[at, :] * SCALE).astype(BF))
        own = own + dot(one_hot(source == home + OWN), dvalue[at, :].astype(BF))
        own = own.reshape(PEERS, 8, HD).astype(BF)
        out_ref[:, 96 + 8 * half : 104 + 8 * half, :] = own


def collect_kernel(in_ref, q_ref, near_ref, far_ref, split):
    row, source = iota((ROWS, GROUPS * HALO), 0), iota((ROWS, GROUPS * HALO), 1)
    window = one_hot(row == OWN * (source // HALO) + source % HALO - HALO)
    row, source = iota((ROWS, GROUPS * 8), 0), iota((ROWS, GROUPS * 8), 1)
    here = row == OWN * (source // 8) + source % OWN
    for s in range(2):
        mine = slice(s * GROUPS, (s + 1) * GROUPS)
        for half in range(2):
            extra = in_ref[mine, 96 + 8 * half : 104 + 8 * half, :]
            extra = extra.astype(F32).reshape(GROUPS * 8, HD).astype(BF)
            for part in range(2):
                at = 32 + 32 * half + 16 * part
                halo = in_ref[mine, at : at + 16, :].reshape(GROUPS * HALO, HD)
                total = dot(window, halo)
                total = total + dot(one_hot(here & (source % 8 // OWN == part)), extra)
                to = near_ref if half == 0 else far_ref
                to[part, s * ROWS : (s + 1) * ROWS] = total.astype(to.dtype)
        split[...] = in_ref[mine, 0:32, :].astype(F32).reshape(GROUPS * 32, HD)
        for h in range(HEADS):
            q_ref[s, :, h * HD : (h + 1) * HD] = split[pl.ds(h, ROWS, stride=HEADS), :].astype(BF)


def whole(shape):
    return pl.BlockSpec(shape, lambda *_: (0,) * len(shape))


def local(
    layer_input, queries, key_states, value_states, attn_output, out_grad, doc_ids, positions
):
    peers = ("xu", "xd", "zd", "y")
    index = lax.axis_index(peers)
    half = lax.axis_index("zu")
    sequence, group = index // GROUPS, index % GROUPS

    wide = layer_input.shape[2] // 2
    low_bit, core = lax.axis_index("xd"), lax.axis_index("core")
    flat_input = layer_input.reshape(2 * ROWS, 2 * wide)

    def swapped(array, axis):
        return lax.ppermute(array, axis, [(0, 1), (1, 0)])

    def columns_of(bit):
        first = bit * (wide // 2)
        parts = [
            lax.dynamic_slice_in_dim(flat_input, first + high * wide, wide // 2, 1)
            for high in range(2)
        ]
        return jnp.stack(parts)

    columns = [columns_of(low_bit), swapped(columns_of(1 - low_bit), "xd")]

    row_spec = lambda width: pl.BlockSpec((1, ROWS, width), lambda s: (s, 0, 0))
    other = swapped(jnp.concatenate([key_states, value_states], axis=2), "zu")
    sent = pl.pallas_call(
        pack_kernel,
        out_shape=jax.ShapeDtypeStruct((PEERS, SEND, HD), BF),
        grid=(2,),
        in_specs=[row_spec(1024), row_spec(1024), row_spec(1024), row_spec(HD), row_spec(HD)],
        out_specs=pl.BlockSpec((GROUPS, SEND, HD), lambda s: (s, 0, 0)),
        scratch_shapes=[pltpu.VMEM((ROWS * HEADS, HD), F32)],
        name="pack",
    )(queries, out_grad, attn_output, key_states, value_states)
    hbm = pl.BlockSpec(memory_space=pl.ANY)
    sent = pl.pallas_call(
        pack_other_kernel,
        out_shape=jax.ShapeDtypeStruct((PEERS, SEND, HD), BF),
        in_specs=[pl.BlockSpec(memory_space=pltpu.VMEM), hbm],
        out_specs=hbm,
        scratch_shapes=[pltpu.VMEM((PEERS, 40, HD), BF), pltpu.SemaphoreType.DMA(())],
        input_output_aliases={1: 0},
        name="pack_other",
    )(other, sent)
    arrived = lax.all_to_all(sent, peers, 0, 0, tiled=True)
    arrived, *columns = lax.optimization_barrier((arrived, *columns))

    docs = lax.dynamic_index_in_dim(doc_ids, sequence, 0, keepdims=False)
    places = lax.dynamic_index_in_dim(positions, sequence, 0, keepdims=False)
    places = places.reshape(4, 2, 8, ROWS)
    places = jnp.pad(places, ((0, 0), (0, 0), (0, 0), (HALO, 0)), constant_values=FAR)
    places = lax.dynamic_slice_in_dim(places, OWN * group, HALO + OWN, 3)
    near = lax.dynamic_index_in_dim(places, half, 1, keepdims=False)
    far = lax.dynamic_index_in_dim(places, 1 - half, 1, keepdims=False)
    own = near[:, :, HALO:].reshape(TOKENS)
    kpos = [near[:, :, :HALO].reshape(KH), far[:, :, :HALO].reshape(KH)]
    kpos = jnp.concatenate(kpos + [own, far[:, :, HALO:].reshape(TOKENS)])[None, :]
    starts = jnp.sum(docs[None, :] < jnp.arange(16)[:, None], axis=1)
    low = jnp.max(jnp.where(starts[:, None] <= own[None, :], starts[:, None], 0), axis=0)
    qpos = jnp.repeat(own, HEADS)[None, :]
    qlow = jnp.repeat(low, HEADS)[None, :]

    back = pl.pallas_call(
        attend_kernel,
        out_shape=jax.ShapeDtypeStruct((PEERS, BACK, HD), BF),
        grid=(1,),
        in_specs=[whole((PEERS, SEND, HD)), whole((1, KN)), whole((1, QN)), whole((1, QN))],
        out_specs=whole((PEERS, BACK, HD)),
        scratch_shapes=[
            pltpu.VMEM((KN, HD), BF),
            pltpu.VMEM((KN, 2 * HD), BF),
            pltpu.VMEM((KN, HD), F32),
            pltpu.VMEM((KN, HD), F32),
        ],
        compiler_params=pltpu.CompilerParams(vmem_limit_bytes=48 << 20),
        name="attend",
    )(arrived, kpos.astype(F32), qpos.astype(F32), qlow.astype(F32))
    home = lax.all_to_all(back, peers, 0, 0, tiled=True)
    twin = swapped(jnp.stack(columns), "core")
    home, twin = lax.optimization_barrier((home, twin))

    query_grad, near_grad, far_grad = pl.pallas_call(
        collect_kernel,
        out_shape=(
            jax.ShapeDtypeStruct((2, ROWS, HEADS * HD), BF),
            jax.ShapeDtypeStruct((2, 2 * ROWS, HD), F32),
            jax.ShapeDtypeStruct((2, 2 * ROWS, HD), BF),
        ),
        grid=(1,),
        in_specs=[whole((PEERS, BACK, HD))],
        out_specs=(
            whole((2, ROWS, HEADS * HD)),
            whole((2, 2 * ROWS, HD)),
            whole((2, 2 * ROWS, HD)),
        ),
        scratch_shapes=[pltpu.VMEM((GROUPS * 32, HD), F32)],
        compiler_params=pltpu.CompilerParams(vmem_limit_bytes=32 << 20),
        name="collect",
    )(home)
    kv_grad = (near_grad + swapped(far_grad, "zu")).astype(BF)

    kv_grad = jnp.broadcast_to(kv_grad[None], (2, 2, 2 * ROWS, HD))
    grads = lax.all_to_all(
        kv_grad.reshape(4, 2 * ROWS, HD), ("xd", "core"), 0, 0, tiled=True
    )
    part = jnp.zeros((2, wide // 2, HD), F32)
    for bit, pair in ((low_bit, 0), (1 - low_bit, 1)):
        for piece, at in ((columns[pair], core), (twin[pair], 1 - core)):
            grad = lax.dynamic_index_in_dim(grads, bit * 2 + at, 0, keepdims=False)
            part = part + lax.dot_general(
                piece, grad, (((1,), (0,)), ((), ())), preferred_element_type=F32
            )
    part = part.reshape(32, 64, HD).astype(BF)
    part = lax.all_to_all(part, ("xu", "zu", "zd", "y"), 0, 0, tiled=True)
    part = jnp.sum(part.astype(F32), axis=0).astype(BF)
    part = lax.all_to_all(jnp.broadcast_to(part[None], (4, 64, HD)), "zh", 0, 0, tiled=True)
    part = jnp.sum(part.astype(F32), axis=0)
    weight_grad = lax.all_gather(part, "core", axis=1, tiled=True)
    return (query_grad, weight_grad)


def solution(mesh):
    devices = mesh.devices.reshape(2, 2, 2, 2, 4, -1, 2)
    inner = Mesh(devices, ("xu", "xd", "zu", "zd", "y", "zh", "core"))
    ctx, dp = ("xu", "xd", "zu", "zd", "y"), ("zh", "core")
    rows = P(dp, ctx, None)
    whole_rows = P(dp, None)
    return jax.shard_map(
        local,
        mesh=inner,
        in_specs=(rows,) * 6 + (whole_rows,) * 2,
        out_specs=(rows, P(ctx, None)),
        check_vma=False,
    )
```

```python
import math

import jax
import jax.numpy as jnp
from jax import lax
from jax.experimental import pallas as pl
from jax.experimental.pallas import tpu as pltpu
from jax.sharding import Mesh
from jax.sharding import PartitionSpec as P

BF = jnp.bfloat16
F32 = jnp.float32
HEADS = 8
HD = 128
ROWS = 64
PEERS = 32
OWN = 4
GROUPS = ROWS // OWN
HALO = 16
SEND = 152
BACK = 112
TOKENS = PEERS * OWN
QN = TOKENS * HEADS
KH = PEERS * HALO
KN = 2 * KH + 2 * TOKENS
NEG = -1e30
FAR = 1 << 20
SCALE = 1.0 / math.sqrt(HD)
LOG2E = math.log2(math.e)


def iota(shape, dim):
    return lax.broadcasted_iota(jnp.int32, shape, dim)


def one_hot(condition):
    return jnp.where(condition, 1.0, 0.0).astype(BF)


def dot(a, b):
    return lax.dot_general(a, b, (((1,), (0,)), ((), ())), preferred_element_type=F32)


def dot_t(a, b):
    return lax.dot_general(a, b, (((1,), (1,)), ((), ())), preferred_element_type=F32)


def window_rows(keys, values):
    target, row = iota((GROUPS * HALO, ROWS), 0), iota((GROUPS * HALO, ROWS), 1)
    window = one_hot(row == OWN * (target // HALO) + target % HALO - HALO)
    target, row = iota((GROUPS * 8, ROWS), 0), iota((GROUPS * 8, ROWS), 1)
    here = row == OWN * (target // 8) + target % OWN
    own = dot(one_hot(here & (target % 8 < OWN)), keys)
    own = own + dot(one_hot(here & (target % 8 >= OWN)), values)
    return (
        dot(window, keys).reshape(GROUPS, HALO, HD).astype(BF),
        dot(window, values).reshape(GROUPS, HALO, HD).astype(BF),
        own.reshape(GROUPS, 8, HD).astype(BF),
    )


def pack_kernel(q_ref, g_ref, o_ref, k_ref, v_ref, out_ref, split):
    def heads_to_rows(ref, at):
        wide = ref[0].astype(F32)
        for h in range(HEADS):
            split[pl.ds(h, ROWS, stride=HEADS), :] = wide[:, h * HD : (h + 1) * HD]
        out_ref[:, at : at + 32, :] = split[...].reshape(GROUPS, 32, HD).astype(BF)

    heads_to_rows(q_ref, 0)
    heads_to_rows(g_ref, 32)
    product = g_ref[0].astype(F32) * o_ref[0].astype(F32)
    lane = iota((ROWS, HD), 1)
    delta = jnp.zeros((ROWS, HD), F32)
    for h in range(HEADS):
        total = jnp.sum(product[:, h * HD : (h + 1) * HD], axis=1, keepdims=True)
        delta = jnp.where(lane % HEADS == h, total, delta)
    high = delta.astype(BF).astype(F32)
    rest = delta - high
    middle = rest.astype(BF).astype(F32)
    low = rest - middle
    pieces = jnp.where(lane < 8, high, jnp.where(lane < 16, middle, low))
    pieces = jnp.where(lane < 24, -pieces, 0.0).astype(BF)
    out_ref[:, 64:80, :], out_ref[:, 80:96, :], out_ref[:, 96:104, :] = window_rows(
        k_ref[0], v_ref[0]
    )
    target, row = iota((GROUPS * 8, ROWS), 0), iota((GROUPS * 8, ROWS), 1)
    here = (row == OWN * (target // 8) + target % OWN) & (target % 8 < OWN)
    out_ref[:, 104:112, :] = dot(one_hot(here), pieces).reshape(GROUPS, 8, HD).astype(BF)


def pack_other_kernel(kv_ref, in_ref, out_ref, block, sem):
    for s in range(2):
        to = slice(s * GROUPS, (s + 1) * GROUPS)
        block[to, 0:16, :], block[to, 16:32, :], block[to, 32:40, :] = window_rows(
            kv_ref[s, :, 0:HD], kv_ref[s, :, HD : 2 * HD]
        )
    copy = pltpu.make_async_copy(block, out_ref.at[:, 112:152, :], sem)
    copy.start()
    copy.wait()


def attend_kernel(in_ref, kpos_ref, qpos_ref, qlow_ref, out_ref, keys, values, dkey, dvalue):
    token, source = iota((TOKENS, PEERS * 8), 0), iota((TOKENS, PEERS * 8), 1)
    home = token // OWN * 8 + token % OWN

    def picked(row, offset):
        extra = in_ref[:, row : row + 8, :].astype(F32).reshape(PEERS * 8, HD).astype(BF)
        return dot(one_hot(source == home + offset), extra).astype(BF)

    for half, (halo, own) in enumerate(((64, 96), (112, 144))):
        to = slice(half * KH, (half + 1) * KH)
        keys[to, :] = in_ref[:, halo : halo + 16, :].reshape(KH, HD)
        values[to, 0:HD] = in_ref[:, halo + 16 : halo + 32, :].reshape(KH, HD)
        to = slice(2 * KH + half * TOKENS, 2 * KH + (half + 1) * TOKENS)
        keys[to, :] = picked(own, 0)
        values[to, 0:HD] = picked(own, OWN)
    values[:, HD : 2 * HD] = one_hot(iota((KN, HD), 1) < 24)
    delta = picked(104, 0)
    kpos = jnp.broadcast_to(kpos_ref[...], (HD, KN)).T
    kpos = jnp.concatenate([kpos, kpos], axis=1)
    key_columns = keys[...].astype(F32).T.astype(BF)
    count = 256
    srcs = count // (OWN * HEADS)
    for c in range(QN // count):
        first = c * srcs
        qc = in_ref[first : first + srcs, 0:32, :].reshape(count, HD)
        gc = in_ref[first : first + srcs, 32:64, :].reshape(count, HD)
        row, col = iota((count, HD), 0), iota((count, HD), 1)
        spread = dot(one_hot(col == c * (count // HEADS) + row // HEADS), delta)
        spread = jnp.where(col % HEADS == row % HEADS, spread, 0.0).astype(BF)
        scores = dot_t(keys[...], qc)
        at = slice(c * count, (c + 1) * count)
        scores = jnp.where((kpos <= qpos_ref[:, at]) & (kpos >= qlow_ref[:, at]), scores, NEG)
        top = jnp.max(scores, axis=0, keepdims=True)
        probs = jnp.exp2((scores - top) * (SCALE * LOG2E))
        probs = probs * (1.0 / jnp.sum(probs, axis=0, keepdims=True))
        change = dot_t(values[...], jnp.concatenate([gc, spread], axis=1))
        sgrad = (probs * change).astype(BF)
        value_part = dot(probs.astype(BF), gc)
        key_part = dot(sgrad, qc)
        if c == 0:
            dvalue[...] = value_part
            dkey[...] = key_part
        else:
            dvalue[...] += value_part
            dkey[...] += key_part
        qgrad = (dot(key_columns, sgrad) * SCALE).T
        out_ref[first : first + srcs, 0:32, :] = qgrad.reshape(srcs, 32, HD).astype(BF)
    source, token = iota((PEERS * 8, TOKENS), 0), iota((PEERS * 8, TOKENS), 1)
    home = token // OWN * 8 + token % OWN
    for half in range(2):
        at = slice(half * KH, (half + 1) * KH)
        halo = 32 + 32 * half
        out_ref[:, halo : halo + 16, :] = (dkey[at, :] * SCALE).reshape(PEERS, HALO, HD).astype(BF)
        out_ref[:, halo + 16 : halo + 32, :] = dvalue[at, :].reshape(PEERS, HALO, HD).astype(BF)
        at = slice(2 * KH + half * TOKENS, 2 * KH + (half + 1) * TOKENS)
        own = dot(one_hot(source == home), (dkey[at, :] * SCALE).astype(BF))
        own = own + dot(one_hot(source == home + OWN), dvalue[at, :].astype(BF))
        own = own.reshape(PEERS, 8, HD).astype(BF)
        out_ref[:, 96 + 8 * half : 104 + 8 * half, :] = own


def collect_kernel(in_ref, q_ref, near_ref, far_ref, split):
    row, source = iota((ROWS, GROUPS * HALO), 0), iota((ROWS, GROUPS * HALO), 1)
    window = one_hot(row == OWN * (source // HALO) + source % HALO - HALO)
    row, source = iota((ROWS, GROUPS * 8), 0), iota((ROWS, GROUPS * 8), 1)
    here = row == OWN * (source // 8) + source % OWN
    for s in range(2):
        mine = slice(s * GROUPS, (s + 1) * GROUPS)
        for half in range(2):
            extra = in_ref[mine, 96 + 8 * half : 104 + 8 * half, :]
            extra = extra.astype(F32).reshape(GROUPS * 8, HD).astype(BF)
            for part in range(2):
                at = 32 + 32 * half + 16 * part
                halo = in_ref[mine, at : at + 16, :].reshape(GROUPS * HALO, HD)
                total = dot(window, halo)
                total = total + dot(one_hot(here & (source % 8 // OWN == part)), extra)
                to = near_ref if half == 0 else far_ref
                to[part, s * ROWS : (s + 1) * ROWS] = total.astype(to.dtype)
        split[...] = in_ref[mine, 0:32, :].astype(F32).reshape(GROUPS * 32, HD)
        for h in range(HEADS):
            q_ref[s, :, h * HD : (h + 1) * HD] = split[pl.ds(h, ROWS, stride=HEADS), :].astype(BF)


def whole(shape):
    return pl.BlockSpec(shape, lambda *_: (0,) * len(shape))


def local(
    layer_input, queries, key_states, value_states, attn_output, out_grad, doc_ids, positions
):
    peers = ("x", "zd", "y")
    index = lax.axis_index(peers)
    half = lax.axis_index("zu")
    sequence, group = index // GROUPS, index % GROUPS

    quarter = layer_input.shape[2] // 4
    x_at, core = lax.axis_index("x"), lax.axis_index("core")
    flat_input = layer_input.reshape(2 * ROWS, 4 * quarter)
    columns = [
        lax.dynamic_slice_in_dim(flat_input, (x_at + step) % 4 * quarter, quarter, 1)
        for step in range(4)
    ]

    def along_x(step):
        return lax.ppermute(columns[step], "x", [(i, (i + step) % 4) for i in range(4)])

    def other_core(x):
        return lax.ppermute(x, "core", [(0, 1), (1, 0)])

    columns[1], columns[3] = along_x(1), along_x(3)

    row_spec = lambda width: pl.BlockSpec((1, ROWS, width), lambda s: (s, 0, 0))
    other = lax.ppermute(
        jnp.concatenate([key_states, value_states], axis=2), "zu", [(0, 1), (1, 0)]
    )
    sent = pl.pallas_call(
        pack_kernel,
        out_shape=jax.ShapeDtypeStruct((PEERS, SEND, HD), BF),
        grid=(2,),
        in_specs=[row_spec(1024), row_spec(1024), row_spec(1024), row_spec(HD), row_spec(HD)],
        out_specs=pl.BlockSpec((GROUPS, SEND, HD), lambda s: (s, 0, 0)),
        scratch_shapes=[pltpu.VMEM((ROWS * HEADS, HD), F32)],
        name="pack",
    )(queries, out_grad, attn_output, key_states, value_states)
    hbm = pl.BlockSpec(memory_space=pl.ANY)
    sent = pl.pallas_call(
        pack_other_kernel,
        out_shape=jax.ShapeDtypeStruct((PEERS, SEND, HD), BF),
        in_specs=[pl.BlockSpec(memory_space=pltpu.VMEM), hbm],
        out_specs=hbm,
        scratch_shapes=[pltpu.VMEM((PEERS, 40, HD), BF), pltpu.SemaphoreType.DMA(())],
        input_output_aliases={1: 0},
        name="pack_other",
    )(other, sent)
    arrived = lax.all_to_all(sent, peers, 0, 0, tiled=True)
    arrived, columns[2] = lax.optimization_barrier((arrived, columns[2]))
    columns[2] = along_x(2)

    docs = lax.dynamic_index_in_dim(doc_ids, sequence, 0, keepdims=False)
    places = lax.dynamic_index_in_dim(positions, sequence, 0, keepdims=False)
    places = places.reshape(4, 2, 8, ROWS)
    places = jnp.pad(places, ((0, 0), (0, 0), (0, 0), (HALO, 0)), constant_values=FAR)
    places = lax.dynamic_slice_in_dim(places, OWN * group, HALO + OWN, 3)
    near = lax.dynamic_index_in_dim(places, half, 1, keepdims=False)
    far = lax.dynamic_index_in_dim(places, 1 - half, 1, keepdims=False)
    own = near[:, :, HALO:].reshape(TOKENS)
    kpos = [near[:, :, :HALO].reshape(KH), far[:, :, :HALO].reshape(KH)]
    kpos = jnp.concatenate(kpos + [own, far[:, :, HALO:].reshape(TOKENS)])[None, :]
    starts = jnp.sum(docs[None, :] < jnp.arange(16)[:, None], axis=1)
    low = jnp.max(jnp.where(starts[:, None] <= own[None, :], starts[:, None], 0), axis=0)
    qpos = jnp.repeat(own, HEADS)[None, :]
    qlow = jnp.repeat(low, HEADS)[None, :]

    back = pl.pallas_call(
        attend_kernel,
        out_shape=jax.ShapeDtypeStruct((PEERS, BACK, HD), BF),
        grid=(1,),
        in_specs=[whole((PEERS, SEND, HD)), whole((1, KN)), whole((1, QN)), whole((1, QN))],
        out_specs=whole((PEERS, BACK, HD)),
        scratch_shapes=[
            pltpu.VMEM((KN, HD), BF),
            pltpu.VMEM((KN, 2 * HD), BF),
            pltpu.VMEM((KN, HD), F32),
            pltpu.VMEM((KN, HD), F32),
        ],
        compiler_params=pltpu.CompilerParams(vmem_limit_bytes=48 << 20),
        name="attend",
    )(arrived, kpos.astype(F32), qpos.astype(F32), qlow.astype(F32))
    back, columns[1], columns[3] = lax.optimization_barrier((back, columns[1], columns[3]))
    home = lax.all_to_all(back, peers, 0, 0, tiled=True)
    twin = other_core(jnp.stack([columns[0], columns[1], columns[3]]))
    home, twin = lax.optimization_barrier((home, twin))

    query_grad, near_grad, far_grad = pl.pallas_call(
        collect_kernel,
        out_shape=(
            jax.ShapeDtypeStruct((2, ROWS, HEADS * HD), BF),
            jax.ShapeDtypeStruct((2, 2 * ROWS, HD), F32),
            jax.ShapeDtypeStruct((2, 2 * ROWS, HD), BF),
        ),
        grid=(1,),
        in_specs=[whole((PEERS, BACK, HD))],
        out_specs=(
            whole((2, ROWS, HEADS * HD)),
            whole((2, 2 * ROWS, HD)),
            whole((2, 2 * ROWS, HD)),
        ),
        scratch_shapes=[pltpu.VMEM((GROUPS * 32, HD), F32)],
        compiler_params=pltpu.CompilerParams(vmem_limit_bytes=32 << 20),
        name="collect",
    )(home)
    far_grad = lax.ppermute(far_grad, "zu", [(0, 1), (1, 0)])
    far_grad, columns[2] = lax.optimization_barrier((far_grad, columns[2]))
    twin = [twin[0], twin[1], other_core(columns[2]), twin[2]]
    kv_grad = (near_grad + far_grad).astype(BF)

    kv_grad = jnp.broadcast_to(kv_grad[None], (4, 2, 2 * ROWS, HD))
    grads = lax.all_to_all(
        kv_grad.reshape(8, 2 * ROWS, HD), ("x", "core"), 0, 0, tiled=True
    )
    part = jnp.zeros((quarter, HD), F32)
    for step in range(4):
        for piece, at in ((columns[step], core), (twin[step], 1 - core)):
            grad = lax.dynamic_index_in_dim(
                grads, (x_at - step) % 4 * 2 + at, 0, keepdims=False
            )
            part = part + lax.dot_general(
                piece, grad, (((0,), (0,)), ((), ())), preferred_element_type=F32
            )
    part = part.reshape(16, 64, HD).astype(BF)
    part = lax.all_to_all(part, ("zu", "zd", "y"), 0, 0, tiled=True)
    part = jnp.sum(part.astype(F32), axis=0).astype(BF)
    part = lax.all_to_all(
        jnp.broadcast_to(part[None], (8, 64, HD)), ("zh", "core"), 0, 0, tiled=True
    )
    part = jnp.sum(part.reshape(4, 2, 64, HD).astype(F32), axis=0)
    weight_grad = part.transpose(1, 0, 2).reshape(64, 2 * HD)
    return (query_grad, weight_grad)


def solution(mesh):
    devices = mesh.devices.reshape(4, 2, 2, 4, -1, 2)
    inner = Mesh(devices, ("x", "zu", "zd", "y", "zh", "core"))
    ctx, dp = ("x", "zu", "zd", "y"), ("zh", "core")
    rows = P(dp, ctx, None)
    whole_rows = P(dp, None)
    return jax.shard_map(
        local,
        mesh=inner,
        in_specs=(rows,) * 6 + (whole_rows,) * 2,
        out_specs=(rows, P(ctx, None)),
        check_vma=False,
    )
```

```python
import math

import jax
import jax.numpy as jnp
from jax import lax
from jax.experimental import pallas as pl
from jax.experimental.pallas import tpu as pltpu
from jax.sharding import Mesh
from jax.sharding import PartitionSpec as P

BF = jnp.bfloat16
F32 = jnp.float32
HEADS = 8
HD = 128
ROWS = 64
PEERS = 32
OWN = 4
GROUPS = ROWS // OWN
HALO = 16
SEND = 152
BACK = 112
TOKENS = PEERS * OWN
QN = TOKENS * HEADS
KH = PEERS * HALO
KN = 2 * KH + 2 * TOKENS
NEG = -1e30
FAR = 1 << 20
SCALE = 1.0 / math.sqrt(HD)
LOG2E = math.log2(math.e)


def iota(shape, dim):
    return lax.broadcasted_iota(jnp.int32, shape, dim)


def one_hot(condition):
    return jnp.where(condition, 1.0, 0.0).astype(BF)


def dot(a, b):
    return lax.dot_general(a, b, (((1,), (0,)), ((), ())), preferred_element_type=F32)


def dot_t(a, b):
    return lax.dot_general(a, b, (((1,), (1,)), ((), ())), preferred_element_type=F32)


def window_rows(keys, values):
    target, row = iota((GROUPS * HALO, ROWS), 0), iota((GROUPS * HALO, ROWS), 1)
    window = one_hot(row == OWN * (target // HALO) + target % HALO - HALO)
    target, row = iota((GROUPS * 8, ROWS), 0), iota((GROUPS * 8, ROWS), 1)
    here = row == OWN * (target // 8) + target % OWN
    own = dot(one_hot(here & (target % 8 < OWN)), keys)
    own = own + dot(one_hot(here & (target % 8 >= OWN)), values)
    return (
        dot(window, keys).reshape(GROUPS, HALO, HD).astype(BF),
        dot(window, values).reshape(GROUPS, HALO, HD).astype(BF),
        own.reshape(GROUPS, 8, HD).astype(BF),
    )


def pack_kernel(q_ref, g_ref, o_ref, k_ref, v_ref, out_ref, split):
    def heads_to_rows(ref, at):
        wide = ref[0].astype(F32)
        for h in range(HEADS):
            split[pl.ds(h, ROWS, stride=HEADS), :] = wide[:, h * HD : (h + 1) * HD]
        out_ref[:, at : at + 32, :] = split[...].reshape(GROUPS, 32, HD).astype(BF)

    heads_to_rows(q_ref, 0)
    heads_to_rows(g_ref, 32)
    product = g_ref[0].astype(F32) * o_ref[0].astype(F32)
    lane = iota((ROWS, HD), 1)
    delta = jnp.zeros((ROWS, HD), F32)
    for h in range(HEADS):
        total = jnp.sum(product[:, h * HD : (h + 1) * HD], axis=1, keepdims=True)
        delta = jnp.where(lane % HEADS == h, total, delta)
    high = delta.astype(BF).astype(F32)
    rest = delta - high
    middle = rest.astype(BF).astype(F32)
    low = rest - middle
    pieces = jnp.where(lane < 8, high, jnp.where(lane < 16, middle, low))
    pieces = jnp.where(lane < 24, -pieces, 0.0).astype(BF)
    out_ref[:, 64:80, :], out_ref[:, 80:96, :], out_ref[:, 96:104, :] = window_rows(
        k_ref[0], v_ref[0]
    )
    target, row = iota((GROUPS * 8, ROWS), 0), iota((GROUPS * 8, ROWS), 1)
    here = (row == OWN * (target // 8) + target % OWN) & (target % 8 < OWN)
    out_ref[:, 104:112, :] = dot(one_hot(here), pieces).reshape(GROUPS, 8, HD).astype(BF)


def pack_other_kernel(kv_ref, in_ref, out_ref, block, sem):
    for s in range(2):
        to = slice(s * GROUPS, (s + 1) * GROUPS)
        block[to, 0:16, :], block[to, 16:32, :], block[to, 32:40, :] = window_rows(
            kv_ref[s, :, 0:HD], kv_ref[s, :, HD : 2 * HD]
        )
    copy = pltpu.make_async_copy(block, out_ref.at[:, 112:152, :], sem)
    copy.start()
    copy.wait()


def attend_kernel(in_ref, kpos_ref, qpos_ref, qlow_ref, out_ref, keys, values, dkey, dvalue):
    token, source = iota((TOKENS, PEERS * 8), 0), iota((TOKENS, PEERS * 8), 1)
    home = token // OWN * 8 + token % OWN

    def picked(row, offset):
        extra = in_ref[:, row : row + 8, :].astype(F32).reshape(PEERS * 8, HD).astype(BF)
        return dot(one_hot(source == home + offset), extra).astype(BF)

    for half, (halo, own) in enumerate(((64, 96), (112, 144))):
        to = slice(half * KH, (half + 1) * KH)
        keys[to, :] = in_ref[:, halo : halo + 16, :].reshape(KH, HD)
        values[to, 0:HD] = in_ref[:, halo + 16 : halo + 32, :].reshape(KH, HD)
        to = slice(2 * KH + half * TOKENS, 2 * KH + (half + 1) * TOKENS)
        keys[to, :] = picked(own, 0)
        values[to, 0:HD] = picked(own, OWN)
    values[:, HD : 2 * HD] = one_hot(iota((KN, HD), 1) < 24)
    delta = picked(104, 0)
    kpos = jnp.broadcast_to(kpos_ref[...], (HD, KN)).T
    kpos = jnp.concatenate([kpos, kpos], axis=1)
    key_columns = keys[...].astype(F32).T.astype(BF)
    count = 256
    srcs = count // (OWN * HEADS)
    for c in range(QN // count):
        first = c * srcs
        qc = in_ref[first : first + srcs, 0:32, :].reshape(count, HD)
        gc = in_ref[first : first + srcs, 32:64, :].reshape(count, HD)
        row, col = iota((count, HD), 0), iota((count, HD), 1)
        spread = dot(one_hot(col == c * (count // HEADS) + row // HEADS), delta)
        spread = jnp.where(col % HEADS == row % HEADS, spread, 0.0).astype(BF)
        scores = dot_t(keys[...], qc)
        at = slice(c * count, (c + 1) * count)
        scores = jnp.where((kpos <= qpos_ref[:, at]) & (kpos >= qlow_ref[:, at]), scores, NEG)
        top = jnp.max(scores, axis=0, keepdims=True)
        probs = jnp.exp2((scores - top) * (SCALE * LOG2E))
        probs = probs * (1.0 / jnp.sum(probs, axis=0, keepdims=True))
        change = dot_t(values[...], jnp.concatenate([gc, spread], axis=1))
        sgrad = (probs * change).astype(BF)
        value_part = dot(probs.astype(BF), gc)
        key_part = dot(sgrad, qc)
        if c == 0:
            dvalue[...] = value_part
            dkey[...] = key_part
        else:
            dvalue[...] += value_part
            dkey[...] += key_part
        qgrad = (dot(key_columns, sgrad) * SCALE).T
        out_ref[first : first + srcs, 0:32, :] = qgrad.reshape(srcs, 32, HD).astype(BF)
    source, token = iota((PEERS * 8, TOKENS), 0), iota((PEERS * 8, TOKENS), 1)
    home = token // OWN * 8 + token % OWN
    for half in range(2):
        at = slice(half * KH, (half + 1) * KH)
        halo = 32 + 32 * half
        out_ref[:, halo : halo + 16, :] = (dkey[at, :] * SCALE).reshape(PEERS, HALO, HD).astype(BF)
        out_ref[:, halo + 16 : halo + 32, :] = dvalue[at, :].reshape(PEERS, HALO, HD).astype(BF)
        at = slice(2 * KH + half * TOKENS, 2 * KH + (half + 1) * TOKENS)
        own = dot(one_hot(source == home), (dkey[at, :] * SCALE).astype(BF))
        own = own + dot(one_hot(source == home + OWN), dvalue[at, :].astype(BF))
        own = own.reshape(PEERS, 8, HD).astype(BF)
        out_ref[:, 96 + 8 * half : 104 + 8 * half, :] = own


def collect_kernel(in_ref, q_ref, near_ref, far_ref, split):
    row, source = iota((ROWS, GROUPS * HALO), 0), iota((ROWS, GROUPS * HALO), 1)
    window = one_hot(row == OWN * (source // HALO) + source % HALO - HALO)
    row, source = iota((ROWS, GROUPS * 8), 0), iota((ROWS, GROUPS * 8), 1)
    here = row == OWN * (source // 8) + source % OWN
    for s in range(2):
        mine = slice(s * GROUPS, (s + 1) * GROUPS)
        for half in range(2):
            extra = in_ref[mine, 96 + 8 * half : 104 + 8 * half, :]
            extra = extra.astype(F32).reshape(GROUPS * 8, HD).astype(BF)
            for part in range(2):
                at = 32 + 32 * half + 16 * part
                halo = in_ref[mine, at : at + 16, :].reshape(GROUPS * HALO, HD)
                total = dot(window, halo)
                total = total + dot(one_hot(here & (source % 8 // OWN == part)), extra)
                to = near_ref if half == 0 else far_ref
                to[part, s * ROWS : (s + 1) * ROWS] = total.astype(to.dtype)
        split[...] = in_ref[mine, 0:32, :].astype(F32).reshape(GROUPS * 32, HD)
        for h in range(HEADS):
            q_ref[s, :, h * HD : (h + 1) * HD] = split[pl.ds(h, ROWS, stride=HEADS), :].astype(BF)


def whole(shape):
    return pl.BlockSpec(shape, lambda *_: (0,) * len(shape))


def local(
    layer_input, queries, key_states, value_states, attn_output, out_grad, doc_ids, positions
):
    peers = ("x", "zd", "y")
    index = lax.axis_index(peers)
    half = lax.axis_index("zu")
    sequence, group = index // GROUPS, index % GROUPS

    quarter = layer_input.shape[2] // 4
    x_at, core = lax.axis_index("x"), lax.axis_index("core")
    flat_input = layer_input.reshape(2 * ROWS, 4 * quarter)
    columns = [
        lax.dynamic_slice_in_dim(flat_input, (x_at + step) % 4 * quarter, quarter, 1)
        for step in range(4)
    ]

    def along_x(step):
        return lax.ppermute(columns[step], "x", [(i, (i + step) % 4) for i in range(4)])

    def other_core(x):
        return lax.ppermute(x, "core", [(0, 1), (1, 0)])

    columns[1], columns[3] = along_x(1), along_x(3)

    row_spec = lambda width: pl.BlockSpec((1, ROWS, width), lambda s: (s, 0, 0))
    other = lax.ppermute(
        jnp.concatenate([key_states, value_states], axis=2), "zu", [(0, 1), (1, 0)]
    )
    sent = pl.pallas_call(
        pack_kernel,
        out_shape=jax.ShapeDtypeStruct((PEERS, SEND, HD), BF),
        grid=(2,),
        in_specs=[row_spec(1024), row_spec(1024), row_spec(1024), row_spec(HD), row_spec(HD)],
        out_specs=pl.BlockSpec((GROUPS, SEND, HD), lambda s: (s, 0, 0)),
        scratch_shapes=[pltpu.VMEM((ROWS * HEADS, HD), F32)],
        name="pack",
    )(queries, out_grad, attn_output, key_states, value_states)
    hbm = pl.BlockSpec(memory_space=pltpu.HBM)
    sent = pl.pallas_call(
        pack_other_kernel,
        out_shape=jax.ShapeDtypeStruct((PEERS, SEND, HD), BF),
        in_specs=[whole((2, ROWS, 2 * HD)), hbm],
        out_specs=hbm,
        scratch_shapes=[pltpu.VMEM((PEERS, 40, HD), BF), pltpu.SemaphoreType.DMA(())],
        input_output_aliases={1: 0},
        grid=(1,),
        compiler_params=pltpu.CompilerParams(vmem_limit_bytes=8 << 20),
        name="pack_other",
    )(other, pltpu.with_memory_space_constraint(sent, pltpu.HBM))
    arrived = lax.all_to_all(sent, peers, 0, 0, tiled=True)
    arrived, columns[2] = lax.optimization_barrier((arrived, columns[2]))
    columns[2] = along_x(2)

    docs = lax.dynamic_index_in_dim(doc_ids, sequence, 0, keepdims=False)
    places = lax.dynamic_index_in_dim(positions, sequence, 0, keepdims=False)
    places = places.reshape(4, 2, 8, ROWS)
    places = jnp.pad(places, ((0, 0), (0, 0), (0, 0), (HALO, 0)), constant_values=FAR)
    places = lax.dynamic_slice_in_dim(places, OWN * group, HALO + OWN, 3)
    near = lax.dynamic_index_in_dim(places, half, 1, keepdims=False)
    far = lax.dynamic_index_in_dim(places, 1 - half, 1, keepdims=False)
    own = near[:, :, HALO:].reshape(TOKENS)
    kpos = [near[:, :, :HALO].reshape(KH), far[:, :, :HALO].reshape(KH)]
    kpos = jnp.concatenate(kpos + [own, far[:, :, HALO:].reshape(TOKENS)])[None, :]
    starts = jnp.sum(docs[None, :] < jnp.arange(16)[:, None], axis=1)
    low = jnp.max(jnp.where(starts[:, None] <= own[None, :], starts[:, None], 0), axis=0)
    qpos = jnp.repeat(own, HEADS)[None, :]
    qlow = jnp.repeat(low, HEADS)[None, :]

    back = pl.pallas_call(
        attend_kernel,
        out_shape=jax.ShapeDtypeStruct((PEERS, BACK, HD), BF),
        grid=(1,),
        in_specs=[whole((PEERS, SEND, HD)), whole((1, KN)), whole((1, QN)), whole((1, QN))],
        out_specs=whole((PEERS, BACK, HD)),
        scratch_shapes=[
            pltpu.VMEM((KN, HD), BF),
            pltpu.VMEM((KN, 2 * HD), BF),
            pltpu.VMEM((KN, HD), F32),
            pltpu.VMEM((KN, HD), F32),
        ],
        compiler_params=pltpu.CompilerParams(vmem_limit_bytes=24 << 20),
        name="attend",
    )(arrived, kpos.astype(F32), qpos.astype(F32), qlow.astype(F32))
    first_twin = other_core(columns[0])
    back, columns[1], columns[3], first_twin = lax.optimization_barrier(
        (back, columns[1], columns[3], first_twin)
    )
    home = lax.all_to_all(back, peers, 0, 0, tiled=True)
    twin = [first_twin, other_core(columns[1]), other_core(columns[3])]
    home, *twin = lax.optimization_barrier((home, *twin))

    query_grad, near_grad, far_grad = pl.pallas_call(
        collect_kernel,
        out_shape=(
            jax.ShapeDtypeStruct((2, ROWS, HEADS * HD), BF),
            jax.ShapeDtypeStruct((2, 2 * ROWS, HD), F32),
            jax.ShapeDtypeStruct((2, 2 * ROWS, HD), BF),
        ),
        grid=(1,),
        in_specs=[whole((PEERS, BACK, HD))],
        out_specs=(
            whole((2, ROWS, HEADS * HD)),
            whole((2, 2 * ROWS, HD)),
            whole((2, 2 * ROWS, HD)),
        ),
        scratch_shapes=[pltpu.VMEM((GROUPS * 32, HD), F32)],
        compiler_params=pltpu.CompilerParams(vmem_limit_bytes=8 << 20),
        name="collect",
    )(home)
    far_grad = lax.ppermute(far_grad, "zu", [(0, 1), (1, 0)])
    far_grad, columns[2] = lax.optimization_barrier((far_grad, columns[2]))
    twin = [twin[0], twin[1], other_core(columns[2]), twin[2]]
    kv_grad = (near_grad + far_grad).astype(BF)

    kv_grad = jnp.broadcast_to(kv_grad[None], (4, 2, 2 * ROWS, HD))
    grads = lax.all_to_all(
        kv_grad.reshape(8, 2 * ROWS, HD), ("x", "core"), 0, 0, tiled=True
    )
    part = jnp.zeros((quarter, HD), F32)
    for step in range(4):
        for piece, at in ((columns[step], core), (twin[step], 1 - core)):
            grad = lax.dynamic_index_in_dim(
                grads, (x_at - step) % 4 * 2 + at, 0, keepdims=False
            )
            part = part + lax.dot_general(
                piece, grad, (((0,), (0,)), ((), ())), preferred_element_type=F32
            )
    part = part.reshape(16, 64, HD).astype(BF)
    part = lax.all_to_all(part, ("zu", "zd", "y"), 0, 0, tiled=True)
    part = jnp.sum(part.astype(F32), axis=0).astype(BF)
    part = lax.all_to_all(
        jnp.broadcast_to(part[None], (8, 64, HD)), ("zh", "core"), 0, 0, tiled=True
    )
    part = jnp.sum(part.reshape(4, 2, 64, HD).astype(F32), axis=0)
    weight_grad = part.transpose(1, 0, 2).reshape(64, 2 * HD)
    return (query_grad, weight_grad)


def solution(mesh):
    devices = mesh.devices.reshape(4, 2, 2, 4, -1, 2)
    inner = Mesh(devices, ("x", "zu", "zd", "y", "zh", "core"))
    ctx, dp = ("x", "zu", "zd", "y"), ("zh", "core")
    rows = P(dp, ctx, None)
    whole_rows = P(dp, None)
    return jax.shard_map(
        local,
        mesh=inner,
        in_specs=(rows,) * 6 + (whole_rows,) * 2,
        out_specs=(rows, P(ctx, None)),
        check_vma=False,
    )
```

```python
import math

import jax
import jax.numpy as jnp
from jax import lax
from jax.experimental import pallas as pl
from jax.experimental.pallas import tpu as pltpu
from jax.sharding import Mesh
from jax.sharding import PartitionSpec as P

BF = jnp.bfloat16
F32 = jnp.float32
HEADS = 8
HD = 128
ROWS = 64
PEERS = 32
OWN = 4
GROUPS = ROWS // OWN
HALO = 16
SEND = 152
BACK = 112
TOKENS = PEERS * OWN
QN = TOKENS * HEADS
KH = PEERS * HALO
KN = 2 * KH + 2 * TOKENS
NEG = -1e30
FAR = 1 << 20
SCALE = 1.0 / math.sqrt(HD)
LOG2E = math.log2(math.e)


def iota(shape, dim):
    return lax.broadcasted_iota(jnp.int32, shape, dim)


def one_hot(condition):
    return jnp.where(condition, 1.0, 0.0).astype(BF)


def dot(a, b):
    return lax.dot_general(a, b, (((1,), (0,)), ((), ())), preferred_element_type=F32)


def dot_t(a, b):
    return lax.dot_general(a, b, (((1,), (1,)), ((), ())), preferred_element_type=F32)


def window_rows(keys, values):
    target, row = iota((GROUPS * HALO, ROWS), 0), iota((GROUPS * HALO, ROWS), 1)
    window = one_hot(row == OWN * (target // HALO) + target % HALO - HALO)
    target, row = iota((GROUPS * 8, ROWS), 0), iota((GROUPS * 8, ROWS), 1)
    here = row == OWN * (target // 8) + target % OWN
    own = dot(one_hot(here & (target % 8 < OWN)), keys)
    own = own + dot(one_hot(here & (target % 8 >= OWN)), values)
    return (
        dot(window, keys).reshape(GROUPS, HALO, HD).astype(BF),
        dot(window, values).reshape(GROUPS, HALO, HD).astype(BF),
        own.reshape(GROUPS, 8, HD).astype(BF),
    )


def pack_kernel(q_ref, g_ref, o_ref, k_ref, v_ref, out_ref, split):
    def heads_to_rows(ref, at):
        wide = ref[0].astype(F32)
        for h in range(HEADS):
            split[pl.ds(h, ROWS, stride=HEADS), :] = wide[:, h * HD : (h + 1) * HD]
        out_ref[:, at : at + 32, :] = split[...].reshape(GROUPS, 32, HD).astype(BF)

    heads_to_rows(q_ref, 0)
    heads_to_rows(g_ref, 32)
    product = g_ref[0].astype(F32) * o_ref[0].astype(F32)
    lane = iota((ROWS, HD), 1)
    delta = jnp.zeros((ROWS, HD), F32)
    for h in range(HEADS):
        total = jnp.sum(product[:, h * HD : (h + 1) * HD], axis=1, keepdims=True)
        delta = jnp.where(lane % HEADS == h, total, delta)
    high = delta.astype(BF).astype(F32)
    rest = delta - high
    middle = rest.astype(BF).astype(F32)
    low = rest - middle
    pieces = jnp.where(lane < 8, high, jnp.where(lane < 16, middle, low))
    pieces = jnp.where(lane < 24, -pieces, 0.0).astype(BF)
    out_ref[:, 64:80, :], out_ref[:, 80:96, :], out_ref[:, 96:104, :] = window_rows(
        k_ref[0], v_ref[0]
    )
    target, row = iota((GROUPS * 8, ROWS), 0), iota((GROUPS * 8, ROWS), 1)
    here = (row == OWN * (target // 8) + target % OWN) & (target % 8 < OWN)
    out_ref[:, 104:112, :] = dot(one_hot(here), pieces).reshape(GROUPS, 8, HD).astype(BF)


def pack_other_kernel(kv_ref, in_ref, out_ref, block, sem):
    for s in range(2):
        to = slice(s * GROUPS, (s + 1) * GROUPS)
        block[to, 0:16, :], block[to, 16:32, :], block[to, 32:40, :] = window_rows(
            kv_ref[s, :, 0:HD], kv_ref[s, :, HD : 2 * HD]
        )
    copy = pltpu.make_async_copy(block, out_ref.at[:, 112:152, :], sem)
    copy.start()
    copy.wait()


def attend_kernel(in_ref, kpos_ref, qpos_ref, qlow_ref, out_ref, keys, values, dkey, dvalue):
    token, source = iota((TOKENS, PEERS * 8), 0), iota((TOKENS, PEERS * 8), 1)
    home = token // OWN * 8 + token % OWN

    def picked(row, offset):
        extra = in_ref[:, row : row + 8, :].astype(F32).reshape(PEERS * 8, HD).astype(BF)
        return dot(one_hot(source == home + offset), extra).astype(BF)

    for half, (halo, own) in enumerate(((64, 96), (112, 144))):
        to = slice(half * KH, (half + 1) * KH)
        keys[to, :] = in_ref[:, halo : halo + 16, :].reshape(KH, HD)
        values[to, 0:HD] = in_ref[:, halo + 16 : halo + 32, :].reshape(KH, HD)
        to = slice(2 * KH + half * TOKENS, 2 * KH + (half + 1) * TOKENS)
        keys[to, :] = picked(own, 0)
        values[to, 0:HD] = picked(own, OWN)
    values[:, HD : 2 * HD] = one_hot(iota((KN, HD), 1) < 24)
    delta = picked(104, 0)
    kpos = jnp.broadcast_to(kpos_ref[...], (HD, KN)).T
    kpos = jnp.concatenate([kpos, kpos], axis=1)
    key_columns = keys[...].astype(F32).T.astype(BF)
    count = 256
    srcs = count // (OWN * HEADS)
    for c in range(QN // count):
        first = c * srcs
        qc = in_ref[first : first + srcs, 0:32, :].reshape(count, HD)
        gc = in_ref[first : first + srcs, 32:64, :].reshape(count, HD)
        row, col = iota((count, HD), 0), iota((count, HD), 1)
        spread = dot(one_hot(col == c * (count // HEADS) + row // HEADS), delta)
        spread = jnp.where(col % HEADS == row % HEADS, spread, 0.0).astype(BF)
        scores = dot_t(keys[...], qc)
        at = slice(c * count, (c + 1) * count)
        scores = jnp.where((kpos <= qpos_ref[:, at]) & (kpos >= qlow_ref[:, at]), scores, NEG)
        top = jnp.max(scores, axis=0, keepdims=True)
        probs = jnp.exp2((scores - top) * (SCALE * LOG2E))
        probs = probs * (1.0 / jnp.sum(probs, axis=0, keepdims=True))
        change = dot_t(values[...], jnp.concatenate([gc, spread], axis=1))
        sgrad = (probs * change).astype(BF)
        value_part = dot(probs.astype(BF), gc)
        key_part = dot(sgrad, qc)
        if c == 0:
            dvalue[...] = value_part
            dkey[...] = key_part
        else:
            dvalue[...] += value_part
            dkey[...] += key_part
        qgrad = (dot(key_columns, sgrad) * SCALE).T
        out_ref[first : first + srcs, 0:32, :] = qgrad.reshape(srcs, 32, HD).astype(BF)
    source, token = iota((PEERS * 8, TOKENS), 0), iota((PEERS * 8, TOKENS), 1)
    home = token // OWN * 8 + token % OWN
    for half in range(2):
        at = slice(half * KH, (half + 1) * KH)
        halo = 32 + 32 * half
        out_ref[:, halo : halo + 16, :] = (dkey[at, :] * SCALE).reshape(PEERS, HALO, HD).astype(BF)
        out_ref[:, halo + 16 : halo + 32, :] = dvalue[at, :].reshape(PEERS, HALO, HD).astype(BF)
        at = slice(2 * KH + half * TOKENS, 2 * KH + (half + 1) * TOKENS)
        own = dot(one_hot(source == home), (dkey[at, :] * SCALE).astype(BF))
        own = own + dot(one_hot(source == home + OWN), dvalue[at, :].astype(BF))
        own = own.reshape(PEERS, 8, HD).astype(BF)
        out_ref[:, 96 + 8 * half : 104 + 8 * half, :] = own


def collect_kernel(in_ref, q_ref, near_ref, far_ref, split):
    row, source = iota((ROWS, GROUPS * HALO), 0), iota((ROWS, GROUPS * HALO), 1)
    window = one_hot(row == OWN * (source // HALO) + source % HALO - HALO)
    row, source = iota((ROWS, GROUPS * 8), 0), iota((ROWS, GROUPS * 8), 1)
    here = row == OWN * (source // 8) + source % OWN
    for s in range(2):
        mine = slice(s * GROUPS, (s + 1) * GROUPS)
        for half in range(2):
            extra = in_ref[mine, 96 + 8 * half : 104 + 8 * half, :]
            extra = extra.astype(F32).reshape(GROUPS * 8, HD).astype(BF)
            for part in range(2):
                at = 32 + 32 * half + 16 * part
                halo = in_ref[mine, at : at + 16, :].reshape(GROUPS * HALO, HD)
                total = dot(window, halo)
                total = total + dot(one_hot(here & (source % 8 // OWN == part)), extra)
                to = near_ref if half == 0 else far_ref
                to[part, s * ROWS : (s + 1) * ROWS] = total.astype(to.dtype)
        split[...] = in_ref[mine, 0:32, :].astype(F32).reshape(GROUPS * 32, HD)
        for h in range(HEADS):
            q_ref[s, :, h * HD : (h + 1) * HD] = split[pl.ds(h, ROWS, stride=HEADS), :].astype(BF)


def spread_kernel(near_ref, far_ref, out_ref):
    total = (near_ref[...] + far_ref[...].astype(F32)).astype(BF)
    for copy in range(4):
        out_ref[2 * copy : 2 * copy + 2] = total


def whole(shape):
    return pl.BlockSpec(shape, lambda *_: (0,) * len(shape))


def local(
    layer_input, queries, key_states, value_states, attn_output, out_grad, doc_ids, positions
):
    peers = ("x", "zd", "y")
    index = lax.axis_index(peers)
    half = lax.axis_index("zu")
    sequence, group = index // GROUPS, index % GROUPS

    quarter = layer_input.shape[2] // 4
    x_at, core = lax.axis_index("x"), lax.axis_index("core")
    flat_input = layer_input.reshape(2 * ROWS, 4 * quarter)
    columns = [
        lax.dynamic_slice_in_dim(flat_input, (x_at + step) % 4 * quarter, quarter, 1)
        for step in range(4)
    ]

    def along_x(step):
        return lax.ppermute(columns[step], "x", [(i, (i + step) % 4) for i in range(4)])

    def other_core(x):
        return lax.ppermute(x, "core", [(0, 1), (1, 0)])


    row_spec = lambda width: pl.BlockSpec((1, ROWS, width), lambda s: (s, 0, 0))
    other = lax.ppermute(
        jnp.concatenate([key_states, value_states], axis=2), "zu", [(0, 1), (1, 0)]
    )
    sent = pl.pallas_call(
        pack_kernel,
        out_shape=jax.ShapeDtypeStruct((PEERS, SEND, HD), BF),
        grid=(2,),
        in_specs=[row_spec(1024), row_spec(1024), row_spec(1024), row_spec(HD), row_spec(HD)],
        out_specs=pl.BlockSpec((GROUPS, SEND, HD), lambda s: (s, 0, 0)),
        scratch_shapes=[pltpu.VMEM((ROWS * HEADS, HD), F32)],
        name="pack",
    )(queries, out_grad, attn_output, key_states, value_states)
    hbm = pl.BlockSpec(memory_space=pltpu.HBM)
    sent = pl.pallas_call(
        pack_other_kernel,
        out_shape=jax.ShapeDtypeStruct((PEERS, SEND, HD), BF),
        in_specs=[whole((2, ROWS, 2 * HD)), hbm],
        out_specs=hbm,
        scratch_shapes=[pltpu.VMEM((PEERS, 40, HD), BF), pltpu.SemaphoreType.DMA(())],
        input_output_aliases={1: 0},
        grid=(1,),
        compiler_params=pltpu.CompilerParams(vmem_limit_bytes=8 << 20),
        name="pack_other",
    )(other, pltpu.with_memory_space_constraint(sent, pltpu.HBM))
    arrived = lax.all_to_all(sent, peers, 0, 0, tiled=True)
    arrived, columns[2] = lax.optimization_barrier((arrived, columns[2]))
    columns[2] = along_x(2)

    docs = lax.dynamic_index_in_dim(doc_ids, sequence, 0, keepdims=False)
    places = lax.dynamic_index_in_dim(positions, sequence, 0, keepdims=False)
    places = places.reshape(4, 2, 8, ROWS)
    places = jnp.pad(places, ((0, 0), (0, 0), (0, 0), (HALO, 0)), constant_values=FAR)
    places = lax.dynamic_slice_in_dim(places, OWN * group, HALO + OWN, 3)
    near = lax.dynamic_index_in_dim(places, half, 1, keepdims=False)
    far = lax.dynamic_index_in_dim(places, 1 - half, 1, keepdims=False)
    own = near[:, :, HALO:].reshape(TOKENS)
    kpos = [near[:, :, :HALO].reshape(KH), far[:, :, :HALO].reshape(KH)]
    kpos = jnp.concatenate(kpos + [own, far[:, :, HALO:].reshape(TOKENS)])[None, :]
    starts = jnp.sum(docs[None, :] < jnp.arange(16)[:, None], axis=1)
    low = jnp.max(jnp.where(starts[:, None] <= own[None, :], starts[:, None], 0), axis=0)
    qpos = jnp.repeat(own, HEADS)[None, :]
    qlow = jnp.repeat(low, HEADS)[None, :]
    kpos, qpos, qlow = kpos.astype(F32), qpos.astype(F32), qlow.astype(F32)
    kpos, qlow, columns[0], columns[1], columns[3] = lax.optimization_barrier(
        (kpos, qlow, columns[0], columns[1], columns[3])
    )
    columns[1], columns[3] = along_x(1), along_x(3)

    back = pl.pallas_call(
        attend_kernel,
        out_shape=jax.ShapeDtypeStruct((PEERS, BACK, HD), BF),
        grid=(1,),
        in_specs=[whole((PEERS, SEND, HD)), whole((1, KN)), whole((1, QN)), whole((1, QN))],
        out_specs=whole((PEERS, BACK, HD)),
        scratch_shapes=[
            pltpu.VMEM((KN, HD), BF),
            pltpu.VMEM((KN, 2 * HD), BF),
            pltpu.VMEM((KN, HD), F32),
            pltpu.VMEM((KN, HD), F32),
        ],
        compiler_params=pltpu.CompilerParams(vmem_limit_bytes=16 << 20),
        name="attend",
    )(arrived, kpos, qpos, qlow)
    first_twin = other_core(columns[0])
    back, columns[1], columns[3], first_twin = lax.optimization_barrier(
        (back, columns[1], columns[3], first_twin)
    )
    home = lax.all_to_all(back, peers, 0, 0, tiled=True)
    twin = [first_twin, other_core(columns[1]), other_core(columns[3])]
    home, *twin = lax.optimization_barrier((home, *twin))

    query_grad, near_grad, far_grad = pl.pallas_call(
        collect_kernel,
        out_shape=(
            jax.ShapeDtypeStruct((2, ROWS, HEADS * HD), BF),
            jax.ShapeDtypeStruct((2, 2 * ROWS, HD), F32),
            jax.ShapeDtypeStruct((2, 2 * ROWS, HD), BF),
        ),
        grid=(1,),
        in_specs=[whole((PEERS, BACK, HD))],
        out_specs=(
            whole((2, ROWS, HEADS * HD)),
            whole((2, 2 * ROWS, HD)),
            whole((2, 2 * ROWS, HD)),
        ),
        scratch_shapes=[pltpu.VMEM((GROUPS * 32, HD), F32)],
        compiler_params=pltpu.CompilerParams(vmem_limit_bytes=8 << 20),
        name="collect",
    )(home)
    far_grad = lax.ppermute(far_grad, "zu", [(0, 1), (1, 0)])
    far_grad, columns[2] = lax.optimization_barrier((far_grad, columns[2]))
    twin = [twin[0], twin[1], other_core(columns[2]), twin[2]]
    kv_grad = pl.pallas_call(
        spread_kernel,
        out_shape=jax.ShapeDtypeStruct((8, 2 * ROWS, HD), BF),
        grid=(1,),
        in_specs=[whole((2, 2 * ROWS, HD)), whole((2, 2 * ROWS, HD))],
        out_specs=whole((8, 2 * ROWS, HD)),
        compiler_params=pltpu.CompilerParams(vmem_limit_bytes=4 << 20),
        name="spread",
    )(near_grad, far_grad)
    grads = lax.all_to_all(kv_grad, ("x", "core"), 0, 0, tiled=True)
    part = jnp.zeros((quarter, HD), F32)
    for step in range(4):
        for piece, at in ((columns[step], core), (twin[step], 1 - core)):
            grad = lax.dynamic_index_in_dim(
                grads, (x_at - step) % 4 * 2 + at, 0, keepdims=False
            )
            part = part + lax.dot_general(
                piece, grad, (((0,), (0,)), ((), ())), preferred_element_type=F32
            )
    part = part.reshape(16, 64, HD).astype(BF)
    part = lax.all_to_all(part, ("zu", "zd", "y"), 0, 0, tiled=True)
    part = jnp.sum(part.astype(F32), axis=0).astype(BF)
    part = lax.all_to_all(
        jnp.broadcast_to(part[None], (8, 64, HD)), ("zh", "core"), 0, 0, tiled=True
    )
    part = jnp.sum(part.reshape(4, 2, 64, HD).astype(F32), axis=0)
    weight_grad = part.transpose(1, 0, 2).reshape(64, 2 * HD)
    return (query_grad, weight_grad)


def solution(mesh):
    devices = mesh.devices.reshape(4, 2, 2, 4, -1, 2)
    inner = Mesh(devices, ("x", "zu", "zd", "y", "zh", "core"))
    ctx, dp = ("x", "zu", "zd", "y"), ("zh", "core")
    rows = P(dp, ctx, None)
    whole_rows = P(dp, None)
    return jax.shard_map(
        local,
        mesh=inner,
        in_specs=(rows,) * 6 + (whole_rows,) * 2,
        out_specs=(rows, P(ctx, None)),
        check_vma=False,
    )
```

```python
import math

import jax
import jax.numpy as jnp
from jax import lax
from jax.experimental import pallas as pl
from jax.experimental.pallas import tpu as pltpu
from jax.sharding import Mesh
from jax.sharding import PartitionSpec as P

BF = jnp.bfloat16
F32 = jnp.float32
HEADS = 8
HD = 128
ROWS = 64
PEERS = 32
OWN = 4
GROUPS = ROWS // OWN
HALO = 16
SEND = 152
BACK = 112
TOKENS = PEERS * OWN
QN = TOKENS * HEADS
KH = PEERS * HALO
KN = 2 * KH + 2 * TOKENS
NEG = -1e30
FAR = 1 << 20
SCALE = 1.0 / math.sqrt(HD)
LOG2E = math.log2(math.e)


def iota(shape, dim):
    return lax.broadcasted_iota(jnp.int32, shape, dim)


def one_hot(condition):
    return jnp.where(condition, 1.0, 0.0).astype(BF)


def dot(a, b):
    return lax.dot_general(a, b, (((1,), (0,)), ((), ())), preferred_element_type=F32)


def dot_t(a, b):
    return lax.dot_general(a, b, (((1,), (1,)), ((), ())), preferred_element_type=F32)


def window_rows(keys, values):
    target, row = iota((GROUPS * HALO, ROWS), 0), iota((GROUPS * HALO, ROWS), 1)
    window = one_hot(row == OWN * (target // HALO) + target % HALO - HALO)
    target, row = iota((GROUPS * 8, ROWS), 0), iota((GROUPS * 8, ROWS), 1)
    here = row == OWN * (target // 8) + target % OWN
    own = dot(one_hot(here & (target % 8 < OWN)), keys)
    own = own + dot(one_hot(here & (target % 8 >= OWN)), values)
    return (
        dot(window, keys).reshape(GROUPS, HALO, HD).astype(BF),
        dot(window, values).reshape(GROUPS, HALO, HD).astype(BF),
        own.reshape(GROUPS, 8, HD).astype(BF),
    )


def pack_kernel(q_ref, g_ref, o_ref, k_ref, v_ref, out_ref, split):
    def heads_to_rows(ref, at):
        wide = ref[0].astype(F32)
        for h in range(HEADS):
            split[pl.ds(h, ROWS, stride=HEADS), :] = wide[:, h * HD : (h + 1) * HD]
        out_ref[:, at : at + 32, :] = split[...].reshape(GROUPS, 32, HD).astype(BF)

    heads_to_rows(q_ref, 0)
    heads_to_rows(g_ref, 32)
    product = g_ref[0].astype(F32) * o_ref[0].astype(F32)
    lane = iota((ROWS, HD), 1)
    delta = jnp.zeros((ROWS, HD), F32)
    for h in range(HEADS):
        total = jnp.sum(product[:, h * HD : (h + 1) * HD], axis=1, keepdims=True)
        delta = jnp.where(lane % HEADS == h, total, delta)
    high = delta.astype(BF).astype(F32)
    rest = delta - high
    middle = rest.astype(BF).astype(F32)
    low = rest - middle
    pieces = jnp.where(lane < 8, high, jnp.where(lane < 16, middle, low))
    pieces = jnp.where(lane < 24, -pieces, 0.0).astype(BF)
    out_ref[:, 64:80, :], out_ref[:, 80:96, :], out_ref[:, 96:104, :] = window_rows(
        k_ref[0], v_ref[0]
    )
    target, row = iota((GROUPS * 8, ROWS), 0), iota((GROUPS * 8, ROWS), 1)
    here = (row == OWN * (target // 8) + target % OWN) & (target % 8 < OWN)
    out_ref[:, 104:112, :] = dot(one_hot(here), pieces).reshape(GROUPS, 8, HD).astype(BF)


def pack_other_kernel(kv_ref, in_ref, out_ref, block, sem):
    for s in range(2):
        to = slice(s * GROUPS, (s + 1) * GROUPS)
        block[to, 0:16, :], block[to, 16:32, :], block[to, 32:40, :] = window_rows(
            kv_ref[s, :, 0:HD], kv_ref[s, :, HD : 2 * HD]
        )
    copy = pltpu.make_async_copy(block, out_ref.at[:, 112:152, :], sem)
    copy.start()
    copy.wait()


def attend_kernel(in_ref, kpos_ref, qpos_ref, qlow_ref, out_ref, keys, values, dkey, dvalue):
    token, source = iota((TOKENS, PEERS * 8), 0), iota((TOKENS, PEERS * 8), 1)
    home = token // OWN * 8 + token % OWN

    def picked(row, offset):
        extra = in_ref[:, row : row + 8, :].astype(F32).reshape(PEERS * 8, HD).astype(BF)
        return dot(one_hot(source == home + offset), extra).astype(BF)

    for half, (halo, own) in enumerate(((64, 96), (112, 144))):
        to = slice(half * KH, (half + 1) * KH)
        keys[to, :] = in_ref[:, halo : halo + 16, :].reshape(KH, HD)
        values[to, 0:HD] = in_ref[:, halo + 16 : halo + 32, :].reshape(KH, HD)
        to = slice(2 * KH + half * TOKENS, 2 * KH + (half + 1) * TOKENS)
        keys[to, :] = picked(own, 0)
        values[to, 0:HD] = picked(own, OWN)
    values[:, HD : 2 * HD] = one_hot(iota((KN, HD), 1) < 24)
    delta = picked(104, 0)
    kpos = jnp.broadcast_to(kpos_ref[...], (HD, KN)).T
    key_columns = keys[...].astype(F32).T.astype(BF)
    count = 512
    kpos = jnp.concatenate([kpos] * (count // HD), axis=1)
    srcs = count // (OWN * HEADS)
    for c in range(QN // count):
        first = c * srcs
        qc = in_ref[first : first + srcs, 0:32, :].reshape(count, HD)
        gc = in_ref[first : first + srcs, 32:64, :].reshape(count, HD)
        row, col = iota((count, HD), 0), iota((count, HD), 1)
        spread = dot(one_hot(col == c * (count // HEADS) + row // HEADS), delta)
        spread = jnp.where(col % HEADS == row % HEADS, spread, 0.0).astype(BF)
        scores = dot_t(keys[...], qc)
        at = slice(c * count, (c + 1) * count)
        scores = jnp.where((kpos <= qpos_ref[:, at]) & (kpos >= qlow_ref[:, at]), scores, NEG)
        top = jnp.max(scores, axis=0, keepdims=True)
        probs = jnp.exp2((scores - top) * (SCALE * LOG2E))
        probs = probs * (1.0 / jnp.sum(probs, axis=0, keepdims=True))
        change = dot_t(values[...], jnp.concatenate([gc, spread], axis=1))
        sgrad = (probs * change).astype(BF)
        value_part = dot(probs.astype(BF), gc)
        key_part = dot(sgrad, qc)
        if c == 0:
            dvalue[...] = value_part
            dkey[...] = key_part
        else:
            dvalue[...] += value_part
            dkey[...] += key_part
        qgrad = (dot(key_columns, sgrad) * SCALE).T
        out_ref[first : first + srcs, 0:32, :] = qgrad.reshape(srcs, 32, HD).astype(BF)
    source, token = iota((PEERS * 8, TOKENS), 0), iota((PEERS * 8, TOKENS), 1)
    home = token // OWN * 8 + token % OWN
    for half in range(2):
        at = slice(half * KH, (half + 1) * KH)
        halo = 32 + 32 * half
        out_ref[:, halo : halo + 16, :] = (dkey[at, :] * SCALE).reshape(PEERS, HALO, HD).astype(BF)
        out_ref[:, halo + 16 : halo + 32, :] = dvalue[at, :].reshape(PEERS, HALO, HD).astype(BF)
        at = slice(2 * KH + half * TOKENS, 2 * KH + (half + 1) * TOKENS)
        own = dot(one_hot(source == home), (dkey[at, :] * SCALE).astype(BF))
        own = own + dot(one_hot(source == home + OWN), dvalue[at, :].astype(BF))
        own = own.reshape(PEERS, 8, HD).astype(BF)
        out_ref[:, 96 + 8 * half : 104 + 8 * half, :] = own


def collect_kernel(in_ref, q_ref, near_ref, far_ref, split):
    row, source = iota((ROWS, GROUPS * HALO), 0), iota((ROWS, GROUPS * HALO), 1)
    window = one_hot(row == OWN * (source // HALO) + source % HALO - HALO)
    row, source = iota((ROWS, GROUPS * 8), 0), iota((ROWS, GROUPS * 8), 1)
    here = row == OWN * (source // 8) + source % OWN
    for s in range(2):
        mine = slice(s * GROUPS, (s + 1) * GROUPS)
        for half in range(2):
            extra = in_ref[mine, 96 + 8 * half : 104 + 8 * half, :]
            extra = extra.astype(F32).reshape(GROUPS * 8, HD).astype(BF)
            for part in range(2):
                at = 32 + 32 * half + 16 * part
                halo = in_ref[mine, at : at + 16, :].reshape(GROUPS * HALO, HD)
                total = dot(window, halo)
                total = total + dot(one_hot(here & (source % 8 // OWN == part)), extra)
                to = near_ref if half == 0 else far_ref
                to[part, s * ROWS : (s + 1) * ROWS] = total.astype(to.dtype)
        split[...] = in_ref[mine, 0:32, :].astype(F32).reshape(GROUPS * 32, HD)
        for h in range(HEADS):
            q_ref[s, :, h * HD : (h + 1) * HD] = split[pl.ds(h, ROWS, stride=HEADS), :].astype(BF)


def spread_kernel(near_ref, far_ref, out_ref):
    total = (near_ref[...] + far_ref[...].astype(F32)).astype(BF)
    for copy in range(4):
        out_ref[2 * copy : 2 * copy + 2] = total


def finish_kernel(in_ref, out_ref):
    for core in range(2):
        total = in_ref[core].astype(F32)
        for replica in range(1, in_ref.shape[0] // 2):
            total = total + in_ref[2 * replica + core].astype(F32)
        out_ref[:, core * HD : (core + 1) * HD] = total


def whole(shape):
    return pl.BlockSpec(shape, lambda *_: (0,) * len(shape))


def local(
    layer_input, queries, key_states, value_states, attn_output, out_grad, doc_ids, positions
):
    peers = ("x", "zd", "y")
    index = lax.axis_index(peers)
    half = lax.axis_index("zu")
    sequence, group = index // GROUPS, index % GROUPS

    quarter = layer_input.shape[2] // 4
    x_at, core = lax.axis_index("x"), lax.axis_index("core")
    flat_input = layer_input.reshape(2 * ROWS, 4 * quarter)
    columns = [
        lax.dynamic_slice_in_dim(flat_input, (x_at + step) % 4 * quarter, quarter, 1)
        for step in range(4)
    ]

    def along_x(step):
        return lax.ppermute(columns[step], "x", [(i, (i + step) % 4) for i in range(4)])

    def other_core(x):
        return lax.ppermute(x, "core", [(0, 1), (1, 0)])


    row_spec = lambda width: pl.BlockSpec((1, ROWS, width), lambda s: (s, 0, 0))
    other = lax.ppermute(
        jnp.concatenate([key_states, value_states], axis=2), "zu", [(0, 1), (1, 0)]
    )
    sent = pl.pallas_call(
        pack_kernel,
        out_shape=jax.ShapeDtypeStruct((PEERS, SEND, HD), BF),
        grid=(2,),
        in_specs=[row_spec(1024), row_spec(1024), row_spec(1024), row_spec(HD), row_spec(HD)],
        out_specs=pl.BlockSpec((GROUPS, SEND, HD), lambda s: (s, 0, 0)),
        scratch_shapes=[pltpu.VMEM((ROWS * HEADS, HD), F32)],
        name="pack",
    )(queries, out_grad, attn_output, key_states, value_states)
    hbm = pl.BlockSpec(memory_space=pltpu.HBM)
    sent = pl.pallas_call(
        pack_other_kernel,
        out_shape=jax.ShapeDtypeStruct((PEERS, SEND, HD), BF),
        in_specs=[whole((2, ROWS, 2 * HD)), hbm],
        out_specs=hbm,
        scratch_shapes=[pltpu.VMEM((PEERS, 40, HD), BF), pltpu.SemaphoreType.DMA(())],
        input_output_aliases={1: 0},
        grid=(1,),
        compiler_params=pltpu.CompilerParams(vmem_limit_bytes=8 << 20),
        name="pack_other",
    )(other, pltpu.with_memory_space_constraint(sent, pltpu.HBM))
    arrived = lax.all_to_all(sent, peers, 0, 0, tiled=True)
    arrived, columns[2] = lax.optimization_barrier((arrived, columns[2]))
    columns[2] = along_x(2)

    docs = lax.dynamic_index_in_dim(doc_ids, sequence, 0, keepdims=False)
    places = lax.dynamic_index_in_dim(positions, sequence, 0, keepdims=False)
    places = places.reshape(4, 2, 8, ROWS)
    places = jnp.pad(places, ((0, 0), (0, 0), (0, 0), (HALO, 0)), constant_values=FAR)
    places = lax.dynamic_slice_in_dim(places, OWN * group, HALO + OWN, 3)
    near = lax.dynamic_index_in_dim(places, half, 1, keepdims=False)
    far = lax.dynamic_index_in_dim(places, 1 - half, 1, keepdims=False)
    own = near[:, :, HALO:].reshape(TOKENS)
    kpos = [near[:, :, :HALO].reshape(KH), far[:, :, :HALO].reshape(KH)]
    kpos = jnp.concatenate(kpos + [own, far[:, :, HALO:].reshape(TOKENS)])[None, :]
    starts = jnp.sum(docs[None, :] < jnp.arange(16)[:, None], axis=1)
    low = jnp.max(jnp.where(starts[:, None] <= own[None, :], starts[:, None], 0), axis=0)
    qpos = jnp.repeat(own, HEADS)[None, :]
    qlow = jnp.repeat(low, HEADS)[None, :]
    kpos, qpos, qlow = kpos.astype(F32), qpos.astype(F32), qlow.astype(F32)
    kpos, qlow, columns[0], columns[1], columns[3] = lax.optimization_barrier(
        (kpos, qlow, columns[0], columns[1], columns[3])
    )
    columns[1], columns[3] = along_x(1), along_x(3)

    back = pl.pallas_call(
        attend_kernel,
        out_shape=jax.ShapeDtypeStruct((PEERS, BACK, HD), BF),
        grid=(1,),
        in_specs=[whole((PEERS, SEND, HD)), whole((1, KN)), whole((1, QN)), whole((1, QN))],
        out_specs=whole((PEERS, BACK, HD)),
        scratch_shapes=[
            pltpu.VMEM((KN, HD), BF),
            pltpu.VMEM((KN, 2 * HD), BF),
            pltpu.VMEM((KN, HD), F32),
            pltpu.VMEM((KN, HD), F32),
        ],
        compiler_params=pltpu.CompilerParams(vmem_limit_bytes=24 << 20),
        name="attend",
    )(arrived, kpos, qpos, qlow)
    first_twin = other_core(columns[0])
    back, columns[1], columns[3], first_twin = lax.optimization_barrier(
        (back, columns[1], columns[3], first_twin)
    )
    home = lax.all_to_all(back, peers, 0, 0, tiled=True)
    twin = [first_twin, other_core(columns[1]), other_core(columns[3])]
    home, *twin = lax.optimization_barrier((home, *twin))

    query_grad, near_grad, far_grad = pl.pallas_call(
        collect_kernel,
        out_shape=(
            jax.ShapeDtypeStruct((2, ROWS, HEADS * HD), BF),
            jax.ShapeDtypeStruct((2, 2 * ROWS, HD), F32),
            jax.ShapeDtypeStruct((2, 2 * ROWS, HD), BF),
        ),
        grid=(1,),
        in_specs=[whole((PEERS, BACK, HD))],
        out_specs=(
            whole((2, ROWS, HEADS * HD)),
            whole((2, 2 * ROWS, HD)),
            whole((2, 2 * ROWS, HD)),
        ),
        scratch_shapes=[pltpu.VMEM((GROUPS * 32, HD), F32)],
        compiler_params=pltpu.CompilerParams(vmem_limit_bytes=8 << 20),
        name="collect",
    )(home)
    far_grad = lax.ppermute(far_grad, "zu", [(0, 1), (1, 0)])
    far_grad, columns[2] = lax.optimization_barrier((far_grad, columns[2]))
    kv_grad = pl.pallas_call(
        spread_kernel,
        out_shape=jax.ShapeDtypeStruct((8, 2 * ROWS, HD), BF),
        grid=(1,),
        in_specs=[whole((2, 2 * ROWS, HD)), whole((2, 2 * ROWS, HD))],
        out_specs=whole((8, 2 * ROWS, HD)),
        compiler_params=pltpu.CompilerParams(vmem_limit_bytes=4 << 20),
        name="spread",
    )(near_grad, far_grad)
    twin = [twin[0], twin[1], other_core(columns[2]), twin[2]]
    grads = lax.all_to_all(kv_grad, ("x", "core"), 0, 0, tiled=True)
    part = jnp.zeros((quarter, HD), F32)
    for step in range(4):
        for piece, at in ((columns[step], core), (twin[step], 1 - core)):
            grad = lax.dynamic_index_in_dim(
                grads, (x_at - step) % 4 * 2 + at, 0, keepdims=False
            )
            part = part + lax.dot_general(
                piece, grad, (((0,), (0,)), ((), ())), preferred_element_type=F32
            )
    part = part.reshape(16, 64, HD).astype(BF)
    part = lax.all_to_all(part, ("zu", "zd", "y"), 0, 0, tiled=True)
    part = jnp.sum(part.astype(F32), axis=0).astype(BF)
    part = lax.all_to_all(
        jnp.broadcast_to(part[None], (8, 64, HD)), ("zh", "core"), 0, 0, tiled=True
    )
    weight_grad = pl.pallas_call(
        finish_kernel,
        out_shape=jax.ShapeDtypeStruct((64, 2 * HD), F32),
        in_specs=[pl.BlockSpec(memory_space=pltpu.VMEM)],
        out_specs=pl.BlockSpec(memory_space=pltpu.VMEM),
        compiler_params=pltpu.CompilerParams(vmem_limit_bytes=4 << 20),
        name="finish",
    )(part)
    return (query_grad, weight_grad)


def solution(mesh):
    devices = mesh.devices.reshape(4, 2, 2, 4, -1, 2)
    inner = Mesh(devices, ("x", "zu", "zd", "y", "zh", "core"))
    ctx, dp = ("x", "zu", "zd", "y"), ("zh", "core")
    rows = P(dp, ctx, None)
    whole_rows = P(dp, None)
    return jax.shard_map(
        local,
        mesh=inner,
        in_specs=(rows,) * 6 + (whole_rows,) * 2,
        out_specs=(rows, P(ctx, None)),
        check_vma=False,
    )
```

```python
import math

import jax
import jax.numpy as jnp
from jax import lax
from jax.experimental import pallas as pl
from jax.experimental.pallas import tpu as pltpu
from jax.sharding import Mesh
from jax.sharding import PartitionSpec as P

BF = jnp.bfloat16
F32 = jnp.float32
HEADS = 8
HD = 128
ROWS = 64
PEERS = 32
OWN = 4
GROUPS = ROWS // OWN
HALO = 16
SEND = 152
BACK = 112
TOKENS = PEERS * OWN
QN = TOKENS * HEADS
KH = PEERS * HALO
KN = 2 * KH + 2 * TOKENS
NEG = -1e30
FAR = 1 << 20
SCALE = 1.0 / math.sqrt(HD)
LOG2E = math.log2(math.e)


def iota(shape, dim):
    return lax.broadcasted_iota(jnp.int32, shape, dim)


def one_hot(condition):
    return jnp.where(condition, 1.0, 0.0).astype(BF)


def dot(a, b):
    return lax.dot_general(a, b, (((1,), (0,)), ((), ())), preferred_element_type=F32)


def dot_t(a, b):
    return lax.dot_general(a, b, (((1,), (1,)), ((), ())), preferred_element_type=F32)


def window_rows(keys, values):
    target, row = iota((GROUPS * HALO, ROWS), 0), iota((GROUPS * HALO, ROWS), 1)
    window = one_hot(row == OWN * (target // HALO) + target % HALO - HALO)
    target, row = iota((GROUPS * 8, ROWS), 0), iota((GROUPS * 8, ROWS), 1)
    here = row == OWN * (target // 8) + target % OWN
    own = dot(one_hot(here & (target % 8 < OWN)), keys)
    own = own + dot(one_hot(here & (target % 8 >= OWN)), values)
    return (
        dot(window, keys).reshape(GROUPS, HALO, HD).astype(BF),
        dot(window, values).reshape(GROUPS, HALO, HD).astype(BF),
        own.reshape(GROUPS, 8, HD).astype(BF),
    )


def pack_kernel(q_ref, g_ref, o_ref, k_ref, v_ref, out_ref, split):
    def heads_to_rows(ref, at):
        wide = ref[0].astype(F32)
        for h in range(HEADS):
            split[pl.ds(h, ROWS, stride=HEADS), :] = wide[:, h * HD : (h + 1) * HD]
        out_ref[:, at : at + 32, :] = split[...].reshape(GROUPS, 32, HD).astype(BF)

    heads_to_rows(q_ref, 0)
    heads_to_rows(g_ref, 32)
    product = g_ref[0].astype(F32) * o_ref[0].astype(F32)
    lane = iota((ROWS, HD), 1)
    delta = jnp.zeros((ROWS, HD), F32)
    for h in range(HEADS):
        total = jnp.sum(product[:, h * HD : (h + 1) * HD], axis=1, keepdims=True)
        delta = jnp.where(lane % HEADS == h, total, delta)
    high = delta.astype(BF).astype(F32)
    rest = delta - high
    middle = rest.astype(BF).astype(F32)
    low = rest - middle
    pieces = jnp.where(lane < 8, high, jnp.where(lane < 16, middle, low))
    pieces = jnp.where(lane < 24, -pieces, 0.0).astype(BF)
    out_ref[:, 64:80, :], out_ref[:, 80:96, :], out_ref[:, 96:104, :] = window_rows(
        k_ref[0], v_ref[0]
    )
    target, row = iota((GROUPS * 8, ROWS), 0), iota((GROUPS * 8, ROWS), 1)
    here = (row == OWN * (target // 8) + target % OWN) & (target % 8 < OWN)
    out_ref[:, 104:112, :] = dot(one_hot(here), pieces).reshape(GROUPS, 8, HD).astype(BF)


def pack_other_kernel(kv_ref, in_ref, out_ref, block, sem):
    for s in range(2):
        to = slice(s * GROUPS, (s + 1) * GROUPS)
        block[to, 0:16, :], block[to, 16:32, :], block[to, 32:40, :] = window_rows(
            kv_ref[s, :, 0:HD], kv_ref[s, :, HD : 2 * HD]
        )
    copy = pltpu.make_async_copy(block, out_ref.at[:, 112:152, :], sem)
    copy.start()
    copy.wait()


def attend_kernel(in_ref, kpos_ref, qpos_ref, qlow_ref, out_ref, keys, values, dkey, dvalue):
    token, source = iota((TOKENS, PEERS * 8), 0), iota((TOKENS, PEERS * 8), 1)
    home = token // OWN * 8 + token % OWN

    def picked(row, offset):
        extra = in_ref[:, row : row + 8, :].astype(F32).reshape(PEERS * 8, HD).astype(BF)
        return dot(one_hot(source == home + offset), extra).astype(BF)

    for half, (halo, own) in enumerate(((64, 96), (112, 144))):
        to = slice(half * KH, (half + 1) * KH)
        keys[to, :] = in_ref[:, halo : halo + 16, :].reshape(KH, HD)
        values[to, 0:HD] = in_ref[:, halo + 16 : halo + 32, :].reshape(KH, HD)
        to = slice(2 * KH + half * TOKENS, 2 * KH + (half + 1) * TOKENS)
        keys[to, :] = picked(own, 0)
        values[to, 0:HD] = picked(own, OWN)
    values[:, HD : 2 * HD] = one_hot(iota((KN, HD), 1) < 24)
    delta = picked(104, 0)
    kpos = jnp.broadcast_to(kpos_ref[...], (HD, KN)).T
    key_columns = keys[...].astype(F32).T.astype(BF)
    count = 512
    kpos = jnp.concatenate([kpos] * (count // HD), axis=1)
    srcs = count // (OWN * HEADS)
    for c in range(QN // count):
        first = c * srcs
        qc = in_ref[first : first + srcs, 0:32, :].reshape(count, HD)
        gc = in_ref[first : first + srcs, 32:64, :].reshape(count, HD)
        row, col = iota((count, HD), 0), iota((count, HD), 1)
        spread = dot(one_hot(col == c * (count // HEADS) + row // HEADS), delta)
        spread = jnp.where(col % HEADS == row % HEADS, spread, 0.0).astype(BF)
        scores = dot_t(keys[...], qc)
        at = slice(c * count, (c + 1) * count)
        scores = jnp.where((kpos <= qpos_ref[:, at]) & (kpos >= qlow_ref[:, at]), scores, NEG)
        top = jnp.max(scores, axis=0, keepdims=True)
        probs = jnp.exp2((scores - top) * (SCALE * LOG2E))
        probs = probs * (1.0 / jnp.sum(probs, axis=0, keepdims=True))
        change = dot_t(values[...], jnp.concatenate([gc, spread], axis=1))
        sgrad = (probs * change).astype(BF)
        value_part = dot(probs.astype(BF), gc)
        key_part = dot(sgrad, qc)
        if c == 0:
            dvalue[...] = value_part
            dkey[...] = key_part
        else:
            dvalue[...] += value_part
            dkey[...] += key_part
        qgrad = (dot(key_columns, sgrad) * SCALE).T
        out_ref[first : first + srcs, 0:32, :] = qgrad.reshape(srcs, 32, HD).astype(BF)
    source, token = iota((PEERS * 8, TOKENS), 0), iota((PEERS * 8, TOKENS), 1)
    home = token // OWN * 8 + token % OWN
    for half in range(2):
        at = slice(half * KH, (half + 1) * KH)
        halo = 32 + 32 * half
        out_ref[:, halo : halo + 16, :] = (dkey[at, :] * SCALE).reshape(PEERS, HALO, HD).astype(BF)
        out_ref[:, halo + 16 : halo + 32, :] = dvalue[at, :].reshape(PEERS, HALO, HD).astype(BF)
        at = slice(2 * KH + half * TOKENS, 2 * KH + (half + 1) * TOKENS)
        own = dot(one_hot(source == home), (dkey[at, :] * SCALE).astype(BF))
        own = own + dot(one_hot(source == home + OWN), dvalue[at, :].astype(BF))
        own = own.reshape(PEERS, 8, HD).astype(BF)
        out_ref[:, 96 + 8 * half : 104 + 8 * half, :] = own


def collect_kernel(in_ref, q_ref, near_ref, far_ref, split):
    row, source = iota((ROWS, GROUPS * HALO), 0), iota((ROWS, GROUPS * HALO), 1)
    window = one_hot(row == OWN * (source // HALO) + source % HALO - HALO)
    row, source = iota((ROWS, GROUPS * 8), 0), iota((ROWS, GROUPS * 8), 1)
    here = row == OWN * (source // 8) + source % OWN
    for s in range(2):
        mine = slice(s * GROUPS, (s + 1) * GROUPS)
        for half in range(2):
            extra = in_ref[mine, 96 + 8 * half : 104 + 8 * half, :]
            extra = extra.astype(F32).reshape(GROUPS * 8, HD).astype(BF)
            for part in range(2):
                at = 32 + 32 * half + 16 * part
                halo = in_ref[mine, at : at + 16, :].reshape(GROUPS * HALO, HD)
                total = dot(window, halo)
                total = total + dot(one_hot(here & (source % 8 // OWN == part)), extra)
                to = near_ref if half == 0 else far_ref
                to[part, s * ROWS : (s + 1) * ROWS] = total.astype(to.dtype)
        split[...] = in_ref[mine, 0:32, :].astype(F32).reshape(GROUPS * 32, HD)
        for h in range(HEADS):
            q_ref[s, :, h * HD : (h + 1) * HD] = split[pl.ds(h, ROWS, stride=HEADS), :].astype(BF)


def spread_kernel(near_ref, far_ref, out_ref):
    total = (near_ref[...] + far_ref[...].astype(F32)).astype(BF)
    for copy in range(4):
        out_ref[2 * copy : 2 * copy + 2] = total


def finish_kernel(in_ref, out_ref):
    for core in range(2):
        total = in_ref[core].astype(F32)
        for replica in range(1, in_ref.shape[0] // 2):
            total = total + in_ref[2 * replica + core].astype(F32)
        out_ref[:, core * HD : (core + 1) * HD] = total


def whole(shape):
    return pl.BlockSpec(shape, lambda *_: (0,) * len(shape))


def local(
    layer_input, queries, key_states, value_states, attn_output, out_grad, doc_ids, positions
):
    peers = ("x", "zd", "y")
    index = lax.axis_index(peers)
    half = lax.axis_index("zu")
    sequence, group = index // GROUPS, index % GROUPS

    quarter = layer_input.shape[2] // 4
    x_at, core = lax.axis_index("x"), lax.axis_index("core")
    flat_input = layer_input.reshape(2 * ROWS, 4 * quarter)
    columns = [
        lax.dynamic_slice_in_dim(flat_input, (x_at + step) % 4 * quarter, quarter, 1)
        for step in range(4)
    ]

    def along_x(step):
        return lax.ppermute(columns[step], "x", [(i, (i + step) % 4) for i in range(4)])

    def other_core(x):
        return lax.ppermute(x, "core", [(0, 1), (1, 0)])


    row_spec = lambda width: pl.BlockSpec((1, ROWS, width), lambda s: (s, 0, 0))
    other = lax.ppermute(
        jnp.concatenate([key_states, value_states], axis=2), "zu", [(0, 1), (1, 0)]
    )
    sent = pl.pallas_call(
        pack_kernel,
        out_shape=jax.ShapeDtypeStruct((PEERS, SEND, HD), BF),
        grid=(2,),
        in_specs=[row_spec(1024), row_spec(1024), row_spec(1024), row_spec(HD), row_spec(HD)],
        out_specs=pl.BlockSpec((GROUPS, SEND, HD), lambda s: (s, 0, 0)),
        scratch_shapes=[pltpu.VMEM((ROWS * HEADS, HD), F32)],
        name="pack",
    )(queries, out_grad, attn_output, key_states, value_states)
    hbm = pl.BlockSpec(memory_space=pltpu.HBM)
    sent = pl.pallas_call(
        pack_other_kernel,
        out_shape=jax.ShapeDtypeStruct((PEERS, SEND, HD), BF),
        in_specs=[whole((2, ROWS, 2 * HD)), hbm],
        out_specs=hbm,
        scratch_shapes=[pltpu.VMEM((PEERS, 40, HD), BF), pltpu.SemaphoreType.DMA(())],
        input_output_aliases={1: 0},
        grid=(1,),
        compiler_params=pltpu.CompilerParams(vmem_limit_bytes=8 << 20),
        name="pack_other",
    )(other, pltpu.with_memory_space_constraint(sent, pltpu.HBM))
    arrived = lax.all_to_all(sent, peers, 0, 0, tiled=True)
    arrived, columns[2] = lax.optimization_barrier((arrived, columns[2]))
    columns[2] = along_x(2)

    docs = lax.dynamic_index_in_dim(doc_ids, sequence, 0, keepdims=False)
    places = lax.dynamic_index_in_dim(positions, sequence, 0, keepdims=False)
    places = places.reshape(4, 2, 8, ROWS)
    places = jnp.pad(places, ((0, 0), (0, 0), (0, 0), (HALO, 0)), constant_values=FAR)
    places = lax.dynamic_slice_in_dim(places, OWN * group, HALO + OWN, 3)
    near = lax.dynamic_index_in_dim(places, half, 1, keepdims=False)
    far = lax.dynamic_index_in_dim(places, 1 - half, 1, keepdims=False)
    own = near[:, :, HALO:].reshape(TOKENS)
    kpos = [near[:, :, :HALO].reshape(KH), far[:, :, :HALO].reshape(KH)]
    kpos = jnp.concatenate(kpos + [own, far[:, :, HALO:].reshape(TOKENS)])[None, :]
    starts = jnp.sum(docs[None, :] < jnp.arange(16)[:, None], axis=1)
    low = jnp.max(jnp.where(starts[:, None] <= own[None, :], starts[:, None], 0), axis=0)
    qpos = jnp.repeat(own, HEADS)[None, :]
    qlow = jnp.repeat(low, HEADS)[None, :]
    kpos, qpos, qlow = kpos.astype(F32), qpos.astype(F32), qlow.astype(F32)
    kpos, qlow, columns[0], columns[1], columns[3] = lax.optimization_barrier(
        (kpos, qlow, columns[0], columns[1], columns[3])
    )
    columns[1], columns[3] = along_x(1), along_x(3)

    back = pl.pallas_call(
        attend_kernel,
        out_shape=jax.ShapeDtypeStruct((PEERS, BACK, HD), BF),
        grid=(1,),
        in_specs=[whole((PEERS, SEND, HD)), whole((1, KN)), whole((1, QN)), whole((1, QN))],
        out_specs=whole((PEERS, BACK, HD)),
        scratch_shapes=[
            pltpu.VMEM((KN, HD), BF),
            pltpu.VMEM((KN, 2 * HD), BF),
            pltpu.VMEM((KN, HD), F32),
            pltpu.VMEM((KN, HD), F32),
        ],
        compiler_params=pltpu.CompilerParams(vmem_limit_bytes=24 << 20),
        name="attend",
    )(arrived, kpos, qpos, qlow)
    first_twin = other_core(columns[0])
    back, columns[1], columns[3], first_twin = lax.optimization_barrier(
        (back, columns[1], columns[3], first_twin)
    )
    home = lax.all_to_all(back, peers, 0, 0, tiled=True)
    twin = [first_twin, other_core(columns[1]), other_core(columns[3])]
    home, *twin = lax.optimization_barrier((home, *twin))

    query_grad, near_grad, far_grad = pl.pallas_call(
        collect_kernel,
        out_shape=(
            jax.ShapeDtypeStruct((2, ROWS, HEADS * HD), BF),
            jax.ShapeDtypeStruct((2, 2 * ROWS, HD), F32),
            jax.ShapeDtypeStruct((2, 2 * ROWS, HD), BF),
        ),
        grid=(1,),
        in_specs=[whole((PEERS, BACK, HD))],
        out_specs=(
            whole((2, ROWS, HEADS * HD)),
            whole((2, 2 * ROWS, HD)),
            whole((2, 2 * ROWS, HD)),
        ),
        scratch_shapes=[pltpu.VMEM((GROUPS * 32, HD), F32)],
        compiler_params=pltpu.CompilerParams(vmem_limit_bytes=8 << 20),
        name="collect",
    )(home)
    far_grad = lax.ppermute(far_grad, "zu", [(0, 1), (1, 0)])
    kv_grad = pl.pallas_call(
        spread_kernel,
        out_shape=jax.ShapeDtypeStruct((8, 2 * ROWS, HD), BF),
        grid=(1,),
        in_specs=[whole((2, 2 * ROWS, HD)), whole((2, 2 * ROWS, HD))],
        out_specs=whole((8, 2 * ROWS, HD)),
        compiler_params=pltpu.CompilerParams(vmem_limit_bytes=4 << 20),
        name="spread",
    )(near_grad, far_grad)
    twin = [twin[0], twin[1], other_core(columns[2]), twin[2]]
    grads = lax.all_to_all(kv_grad, ("x", "core"), 0, 0, tiled=True)
    part = jnp.zeros((quarter, HD), F32)
    for step in range(4):
        for piece, at in ((columns[step], core), (twin[step], 1 - core)):
            grad = lax.dynamic_index_in_dim(
                grads, (x_at - step) % 4 * 2 + at, 0, keepdims=False
            )
            part = part + lax.dot_general(
                piece, grad, (((0,), (0,)), ((), ())), preferred_element_type=F32
            )
    part = part.reshape(16, 64, HD).astype(BF)
    part = lax.all_to_all(part, ("zu", "zd", "y"), 0, 0, tiled=True)
    part = jnp.sum(part.astype(F32), axis=0).astype(BF)
    part = lax.all_to_all(
        jnp.broadcast_to(part[None], (8, 64, HD)), ("zh", "core"), 0, 0, tiled=True
    )
    weight_grad = pl.pallas_call(
        finish_kernel,
        out_shape=jax.ShapeDtypeStruct((64, 2 * HD), F32),
        in_specs=[pl.BlockSpec(memory_space=pltpu.VMEM)],
        out_specs=pl.BlockSpec(memory_space=pltpu.VMEM),
        compiler_params=pltpu.CompilerParams(vmem_limit_bytes=4 << 20),
        name="finish",
    )(part)
    return (query_grad, weight_grad)


def solution(mesh):
    devices = mesh.devices.reshape(4, 2, 2, 4, -1, 2)
    inner = Mesh(devices, ("x", "zu", "zd", "y", "zh", "core"))
    ctx, dp = ("x", "zu", "zd", "y"), ("zh", "core")
    rows = P(dp, ctx, None)
    whole_rows = P(dp, None)
    return jax.shard_map(
        local,
        mesh=inner,
        in_specs=(rows,) * 6 + (whole_rows,) * 2,
        out_specs=(rows, P(ctx, None)),
        check_vma=False,
    )
```

```python
import math

import jax
import jax.numpy as jnp
from jax import lax
from jax.experimental import pallas as pl
from jax.experimental.pallas import tpu as pltpu
from jax.sharding import Mesh
from jax.sharding import PartitionSpec as P

BF = jnp.bfloat16
F32 = jnp.float32
HEADS = 8
HD = 128
ROWS = 64
PEERS = 32
OWN = 4
GROUPS = ROWS // OWN
HALO = 16
SEND = 152
BACK = 112
TOKENS = PEERS * OWN
QN = TOKENS * HEADS
KH = PEERS * HALO
KN = 2 * KH + 2 * TOKENS
NEG = -1e30
FAR = 1 << 20
SCALE = 1.0 / math.sqrt(HD)
LOG2E = math.log2(math.e)


def iota(shape, dim):
    return lax.broadcasted_iota(jnp.int32, shape, dim)


def one_hot(condition):
    return jnp.where(condition, 1.0, 0.0).astype(BF)


def dot(a, b):
    return lax.dot_general(a, b, (((1,), (0,)), ((), ())), preferred_element_type=F32)


def dot_t(a, b):
    return lax.dot_general(a, b, (((1,), (1,)), ((), ())), preferred_element_type=F32)


def window_rows(keys, values):
    target, row = iota((GROUPS * HALO, ROWS), 0), iota((GROUPS * HALO, ROWS), 1)
    window = one_hot(row == OWN * (target // HALO) + target % HALO - HALO)
    target, row = iota((GROUPS * 8, ROWS), 0), iota((GROUPS * 8, ROWS), 1)
    here = row == OWN * (target // 8) + target % OWN
    own = dot(one_hot(here & (target % 8 < OWN)), keys)
    own = own + dot(one_hot(here & (target % 8 >= OWN)), values)
    return (
        dot(window, keys).reshape(GROUPS, HALO, HD).astype(BF),
        dot(window, values).reshape(GROUPS, HALO, HD).astype(BF),
        own.reshape(GROUPS, 8, HD).astype(BF),
    )


def pack_kernel(q_ref, g_ref, o_ref, k_ref, v_ref, out_ref, split):
    def heads_to_rows(ref, at):
        wide = ref[0].astype(F32)
        for h in range(HEADS):
            split[pl.ds(h, ROWS, stride=HEADS), :] = wide[:, h * HD : (h + 1) * HD]
        out_ref[:, at : at + 32, :] = split[...].reshape(GROUPS, 32, HD).astype(BF)

    heads_to_rows(q_ref, 0)
    heads_to_rows(g_ref, 32)
    product = g_ref[0].astype(F32) * o_ref[0].astype(F32)
    lane = iota((ROWS, HD), 1)
    delta = jnp.zeros((ROWS, HD), F32)
    for h in range(HEADS):
        total = jnp.sum(product[:, h * HD : (h + 1) * HD], axis=1, keepdims=True)
        delta = jnp.where(lane % HEADS == h, total, delta)
    high = delta.astype(BF).astype(F32)
    rest = delta - high
    middle = rest.astype(BF).astype(F32)
    low = rest - middle
    pieces = jnp.where(lane < 8, high, jnp.where(lane < 16, middle, low))
    pieces = jnp.where(lane < 24, -pieces, 0.0).astype(BF)
    out_ref[:, 64:80, :], out_ref[:, 80:96, :], out_ref[:, 96:104, :] = window_rows(
        k_ref[0], v_ref[0]
    )
    target, row = iota((GROUPS * 8, ROWS), 0), iota((GROUPS * 8, ROWS), 1)
    here = (row == OWN * (target // 8) + target % OWN) & (target % 8 < OWN)
    out_ref[:, 104:112, :] = dot(one_hot(here), pieces).reshape(GROUPS, 8, HD).astype(BF)


def pack_other_kernel(kv_ref, in_ref, out_ref, block, sem):
    for s in range(2):
        to = slice(s * GROUPS, (s + 1) * GROUPS)
        block[to, 0:16, :], block[to, 16:32, :], block[to, 32:40, :] = window_rows(
            kv_ref[s, :, 0:HD], kv_ref[s, :, HD : 2 * HD]
        )
    copy = pltpu.make_async_copy(block, out_ref.at[:, 112:152, :], sem)
    copy.start()
    copy.wait()


def attend_kernel(in_ref, kpos_ref, qpos_ref, qlow_ref, out_ref, keys, values, dkey, dvalue):
    token, source = iota((TOKENS, PEERS * 8), 0), iota((TOKENS, PEERS * 8), 1)
    home = token // OWN * 8 + token % OWN

    def picked(row, offset):
        extra = in_ref[:, row : row + 8, :].astype(F32).reshape(PEERS * 8, HD).astype(BF)
        return dot(one_hot(source == home + offset), extra).astype(BF)

    for half, (halo, own) in enumerate(((64, 96), (112, 144))):
        to = slice(half * KH, (half + 1) * KH)
        keys[to, :] = in_ref[:, halo : halo + 16, :].reshape(KH, HD)
        values[to, 0:HD] = in_ref[:, halo + 16 : halo + 32, :].reshape(KH, HD)
        to = slice(2 * KH + half * TOKENS, 2 * KH + (half + 1) * TOKENS)
        keys[to, :] = picked(own, 0)
        values[to, 0:HD] = picked(own, OWN)
    values[:, HD : 2 * HD] = one_hot(iota((KN, HD), 1) < 24)
    delta = picked(104, 0)
    kpos = jnp.broadcast_to(kpos_ref[...], (HD, KN)).T
    key_columns = keys[...].T
    count = 512
    kpos = jnp.concatenate([kpos] * (count // HD), axis=1)
    srcs = count // (OWN * HEADS)
    for c in range(QN // count):
        first = c * srcs
        qc = in_ref[first : first + srcs, 0:32, :].reshape(count, HD)
        gc = in_ref[first : first + srcs, 32:64, :].reshape(count, HD)
        row, col = iota((count, HD), 0), iota((count, HD), 1)
        spread = dot(one_hot(col == c * (count // HEADS) + row // HEADS), delta)
        spread = jnp.where(col % HEADS == row % HEADS, spread, 0.0).astype(BF)
        scores = dot_t(keys[...], qc)
        at = slice(c * count, (c + 1) * count)
        scores = jnp.where((kpos <= qpos_ref[:, at]) & (kpos >= qlow_ref[:, at]), scores, NEG)
        top = jnp.max(scores, axis=0, keepdims=True)
        probs = jnp.exp2((scores - top) * (SCALE * LOG2E))
        probs = probs * (1.0 / jnp.sum(probs, axis=0, keepdims=True))
        change = dot_t(values[...], jnp.concatenate([gc, spread], axis=1))
        sgrad = (probs * change).astype(BF)
        value_part = dot(probs.astype(BF), gc)
        key_part = dot(sgrad, qc)
        if c == 0:
            dvalue[...] = value_part
            dkey[...] = key_part
        else:
            dvalue[...] += value_part
            dkey[...] += key_part
        qgrad = (dot(key_columns, sgrad) * SCALE).T
        out_ref[first : first + srcs, 0:32, :] = qgrad.reshape(srcs, 32, HD).astype(BF)
    source, token = iota((PEERS * 8, TOKENS), 0), iota((PEERS * 8, TOKENS), 1)
    home = token // OWN * 8 + token % OWN
    for half in range(2):
        at = slice(half * KH, (half + 1) * KH)
        halo = 32 + 32 * half
        out_ref[:, halo : halo + 16, :] = (dkey[at, :] * SCALE).reshape(PEERS, HALO, HD).astype(BF)
        out_ref[:, halo + 16 : halo + 32, :] = dvalue[at, :].reshape(PEERS, HALO, HD).astype(BF)
        at = slice(2 * KH + half * TOKENS, 2 * KH + (half + 1) * TOKENS)
        own = dot(one_hot(source == home), (dkey[at, :] * SCALE).astype(BF))
        own = own + dot(one_hot(source == home + OWN), dvalue[at, :].astype(BF))
        own = own.reshape(PEERS, 8, HD).astype(BF)
        out_ref[:, 96 + 8 * half : 104 + 8 * half, :] = own


def collect_kernel(in_ref, q_ref, near_ref, far_ref, split):
    row, source = iota((ROWS, GROUPS * HALO), 0), iota((ROWS, GROUPS * HALO), 1)
    window = one_hot(row == OWN * (source // HALO) + source % HALO - HALO)
    row, source = iota((ROWS, GROUPS * 8), 0), iota((ROWS, GROUPS * 8), 1)
    here = row == OWN * (source // 8) + source % OWN
    for s in range(2):
        mine = slice(s * GROUPS, (s + 1) * GROUPS)
        for half in range(2):
            extra = in_ref[mine, 96 + 8 * half : 104 + 8 * half, :]
            extra = extra.astype(F32).reshape(GROUPS * 8, HD).astype(BF)
            for part in range(2):
                at = 32 + 32 * half + 16 * part
                halo = in_ref[mine, at : at + 16, :].reshape(GROUPS * HALO, HD)
                total = dot(window, halo)
                total = total + dot(one_hot(here & (source % 8 // OWN == part)), extra)
                to = near_ref if half == 0 else far_ref
                to[part, s * ROWS : (s + 1) * ROWS] = total.astype(to.dtype)
        split[...] = in_ref[mine, 0:32, :].astype(F32).reshape(GROUPS * 32, HD)
        for h in range(HEADS):
            q_ref[s, :, h * HD : (h + 1) * HD] = split[pl.ds(h, ROWS, stride=HEADS), :].astype(BF)


def spread_kernel(near_ref, far_ref, out_ref):
    total = (near_ref[...] + far_ref[...].astype(F32)).astype(BF)
    for copy in range(4):
        out_ref[2 * copy : 2 * copy + 2] = total


def finish_kernel(in_ref, out_ref):
    for core in range(2):
        total = in_ref[core].astype(F32)
        for replica in range(1, in_ref.shape[0] // 2):
            total = total + in_ref[2 * replica + core].astype(F32)
        out_ref[:, core * HD : (core + 1) * HD] = total


def whole(shape):
    return pl.BlockSpec(shape, lambda *_: (0,) * len(shape))


def local(
    layer_input, queries, key_states, value_states, attn_output, out_grad, doc_ids, positions
):
    peers = ("x", "zd", "y")
    index = lax.axis_index(peers)
    half = lax.axis_index("zu")
    sequence, group = index // GROUPS, index % GROUPS

    quarter = layer_input.shape[2] // 4
    x_at, core = lax.axis_index("x"), lax.axis_index("core")
    flat_input = layer_input.reshape(2 * ROWS, 4 * quarter)
    columns = [
        lax.dynamic_slice_in_dim(flat_input, (x_at + step) % 4 * quarter, quarter, 1)
        for step in range(4)
    ]

    def along_x(step):
        return lax.ppermute(columns[step], "x", [(i, (i + step) % 4) for i in range(4)])

    def other_core(x):
        return lax.ppermute(x, "core", [(0, 1), (1, 0)])


    row_spec = lambda width: pl.BlockSpec((1, ROWS, width), lambda s: (s, 0, 0))
    other = lax.ppermute(
        jnp.concatenate([key_states, value_states], axis=2), "zu", [(0, 1), (1, 0)]
    )
    sent = pl.pallas_call(
        pack_kernel,
        out_shape=jax.ShapeDtypeStruct((PEERS, SEND, HD), BF),
        grid=(2,),
        in_specs=[row_spec(1024), row_spec(1024), row_spec(1024), row_spec(HD), row_spec(HD)],
        out_specs=pl.BlockSpec((GROUPS, SEND, HD), lambda s: (s, 0, 0)),
        scratch_shapes=[pltpu.VMEM((ROWS * HEADS, HD), F32)],
        name="pack",
    )(queries, out_grad, attn_output, key_states, value_states)
    hbm = pl.BlockSpec(memory_space=pltpu.HBM)
    sent = pl.pallas_call(
        pack_other_kernel,
        out_shape=jax.ShapeDtypeStruct((PEERS, SEND, HD), BF),
        in_specs=[whole((2, ROWS, 2 * HD)), hbm],
        out_specs=hbm,
        scratch_shapes=[pltpu.VMEM((PEERS, 40, HD), BF), pltpu.SemaphoreType.DMA(())],
        input_output_aliases={1: 0},
        grid=(1,),
        compiler_params=pltpu.CompilerParams(vmem_limit_bytes=8 << 20),
        name="pack_other",
    )(other, pltpu.with_memory_space_constraint(sent, pltpu.HBM))
    arrived = lax.all_to_all(sent, peers, 0, 0, tiled=True)
    arrived, columns[2] = lax.optimization_barrier((arrived, columns[2]))
    columns[2] = along_x(2)

    docs = lax.dynamic_index_in_dim(doc_ids, sequence, 0, keepdims=False)
    places = lax.dynamic_index_in_dim(positions, sequence, 0, keepdims=False)
    places = places.reshape(4, 2, 8, ROWS)
    places = jnp.pad(places, ((0, 0), (0, 0), (0, 0), (HALO, 0)), constant_values=FAR)
    places = lax.dynamic_slice_in_dim(places, OWN * group, HALO + OWN, 3)
    near = lax.dynamic_index_in_dim(places, half, 1, keepdims=False)
    far = lax.dynamic_index_in_dim(places, 1 - half, 1, keepdims=False)
    own = near[:, :, HALO:].reshape(TOKENS)
    kpos = [near[:, :, :HALO].reshape(KH), far[:, :, :HALO].reshape(KH)]
    kpos = jnp.concatenate(kpos + [own, far[:, :, HALO:].reshape(TOKENS)])[None, :]
    starts = jnp.sum(docs[None, :] < jnp.arange(16)[:, None], axis=1)
    low = jnp.max(jnp.where(starts[:, None] <= own[None, :], starts[:, None], 0), axis=0)
    qpos = jnp.repeat(own, HEADS)[None, :]
    qlow = jnp.repeat(low, HEADS)[None, :]
    kpos, qpos, qlow = kpos.astype(F32), qpos.astype(F32), qlow.astype(F32)
    kpos, qlow, columns[0], columns[1], columns[3] = lax.optimization_barrier(
        (kpos, qlow, columns[0], columns[1], columns[3])
    )
    columns[1], columns[3] = along_x(1), along_x(3)

    back = pl.pallas_call(
        attend_kernel,
        out_shape=jax.ShapeDtypeStruct((PEERS, BACK, HD), BF),
        grid=(1,),
        in_specs=[whole((PEERS, SEND, HD)), whole((1, KN)), whole((1, QN)), whole((1, QN))],
        out_specs=whole((PEERS, BACK, HD)),
        scratch_shapes=[
            pltpu.VMEM((KN, HD), BF),
            pltpu.VMEM((KN, 2 * HD), BF),
            pltpu.VMEM((KN, HD), F32),
            pltpu.VMEM((KN, HD), F32),
        ],
        compiler_params=pltpu.CompilerParams(vmem_limit_bytes=24 << 20),
        name="attend",
    )(arrived, kpos, qpos, qlow)
    first_twin = other_core(columns[0])
    back, columns[1], columns[3], first_twin = lax.optimization_barrier(
        (back, columns[1], columns[3], first_twin)
    )
    home = lax.all_to_all(back, peers, 0, 0, tiled=True)
    twin = [first_twin, other_core(columns[1]), other_core(columns[3])]
    home, *twin = lax.optimization_barrier((home, *twin))

    query_grad, near_grad, far_grad = pl.pallas_call(
        collect_kernel,
        out_shape=(
            jax.ShapeDtypeStruct((2, ROWS, HEADS * HD), BF),
            jax.ShapeDtypeStruct((2, 2 * ROWS, HD), F32),
            jax.ShapeDtypeStruct((2, 2 * ROWS, HD), BF),
        ),
        grid=(1,),
        in_specs=[whole((PEERS, BACK, HD))],
        out_specs=(
            whole((2, ROWS, HEADS * HD)),
            whole((2, 2 * ROWS, HD)),
            whole((2, 2 * ROWS, HD)),
        ),
        scratch_shapes=[pltpu.VMEM((GROUPS * 32, HD), F32)],
        compiler_params=pltpu.CompilerParams(vmem_limit_bytes=8 << 20),
        name="collect",
    )(home)
    far_grad = lax.ppermute(far_grad, "zu", [(0, 1), (1, 0)])
    far_grad, columns[2] = lax.optimization_barrier((far_grad, columns[2]))
    kv_grad = pl.pallas_call(
        spread_kernel,
        out_shape=jax.ShapeDtypeStruct((8, 2 * ROWS, HD), BF),
        grid=(1,),
        in_specs=[whole((2, 2 * ROWS, HD)), whole((2, 2 * ROWS, HD))],
        out_specs=whole((8, 2 * ROWS, HD)),
        compiler_params=pltpu.CompilerParams(vmem_limit_bytes=4 << 20),
        name="spread",
    )(near_grad, far_grad)
    twin = [twin[0], twin[1], other_core(columns[2]), twin[2]]
    grads = lax.all_to_all(kv_grad, ("x", "core"), 0, 0, tiled=True)
    part = jnp.zeros((quarter, HD), F32)
    for step in range(4):
        for piece, at in ((columns[step], core), (twin[step], 1 - core)):
            grad = lax.dynamic_index_in_dim(
                grads, (x_at - step) % 4 * 2 + at, 0, keepdims=False
            )
            part = part + lax.dot_general(
                piece, grad, (((0,), (0,)), ((), ())), preferred_element_type=F32
            )
    part = part.reshape(16, 64, HD).astype(BF)
    part = lax.all_to_all(part, ("zu", "zd", "y"), 0, 0, tiled=True)
    part = jnp.sum(part.astype(F32), axis=0).astype(BF)
    part = lax.all_to_all(
        jnp.broadcast_to(part[None], (8, 64, HD)), ("zh", "core"), 0, 0, tiled=True
    )
    weight_grad = pl.pallas_call(
        finish_kernel,
        out_shape=jax.ShapeDtypeStruct((64, 2 * HD), F32),
        in_specs=[pl.BlockSpec(memory_space=pltpu.VMEM)],
        out_specs=pl.BlockSpec(memory_space=pltpu.VMEM),
        compiler_params=pltpu.CompilerParams(vmem_limit_bytes=4 << 20),
        name="finish",
    )(part)
    return (query_grad, weight_grad)


def solution(mesh):
    devices = mesh.devices.reshape(4, 2, 2, 4, -1, 2)
    inner = Mesh(devices, ("x", "zu", "zd", "y", "zh", "core"))
    ctx, dp = ("x", "zu", "zd", "y"), ("zh", "core")
    rows = P(dp, ctx, None)
    whole_rows = P(dp, None)
    return jax.shard_map(
        local,
        mesh=inner,
        in_specs=(rows,) * 6 + (whole_rows,) * 2,
        out_specs=(rows, P(ctx, None)),
        check_vma=False,
    )
```
